32 devices in a mesh: ctx: 16 (over z, y, core), fsdp: 2 (over x).
Axes of the slice: x: 2, y: 2, z: 4, core: 2. Of those that a mesh axis runs over, the one named last changes fastest.
Arguments:
- tokens: bfloat16 [2, 2, 1024, 1024], P(None, 'fsdp', 'ctx'), may hold values from -6 to 6
- cotangent: bfloat16 [2, 2, 1024, 1024], P(None, 'fsdp', 'ctx'), may hold values from -6 to 6
- qkv_weight: bfloat16 [1024, 3072], P(('ctx', 'fsdp')), may hold values from -0.25 to 0.25
- out_weight: bfloat16 [1024, 1024], P(('ctx', 'fsdp')), may hold values from -1.5 to 1.5
- up_weight: bfloat16 [1024, 4096], P(('ctx', 'fsdp')), may hold values from -0.1875 to 0.1875
- down_weight: bfloat16 [4096, 1024], P(('ctx', 'fsdp')), may hold values from -0.09375 to 0.09375
- qkv_bias: bfloat16 [3072], P(('ctx', 'fsdp')), may hold values from -1.5 to 1.5
- out_bias: bfloat16 [1024], P(('ctx', 'fsdp')), may hold values from -1.5 to 1.5
- up_bias: bfloat16 [4096], P(('ctx', 'fsdp')), may hold values from -1.5 to 1.5
- down_bias: bfloat16 [1024], P(('ctx', 'fsdp')), may hold values from -1.5 to 1.5
- first_gain: bfloat16 [1024], P(('ctx', 'fsdp')), may hold values from 0.5 to 1.5
- first_shift: bfloat16 [1024], P(('ctx', 'fsdp')), may hold values from -1.5 to 1.5
- second_gain: bfloat16 [1024], P(('ctx', 'fsdp')), may hold values from 0.5 to 1.5
- second_shift: bfloat16 [1024], P(('ctx', 'fsdp')), may hold values from -1.5 to 1.5
Outputs:
- output: bfloat16 [2, 2, 1024, 1024], P(None, 'fsdp', 'ctx')
- token_grad: float32 [2, 2, 1024, 1024], P(None, 'fsdp', 'ctx')
- qkv_weight_grad: float32 [1024, 3072], P(('ctx', 'fsdp'))
- out_weight_grad: float32 [1024, 1024], P(('ctx', 'fsdp'))
- up_weight_grad: float32 [1024, 4096], P(('ctx', 'fsdp'))
- down_weight_grad: float32 [4096, 1024], P(('ctx', 'fsdp'))
- qkv_bias_grad: float32 [3072], P(('ctx', 'fsdp'))
- out_bias_grad: float32 [1024], P(('ctx', 'fsdp'))
- up_bias_grad: float32 [4096], P(('ctx', 'fsdp'))
- down_bias_grad: float32 [1024], P(('ctx', 'fsdp'))
- first_gain_grad: float32 [1024], P(('ctx', 'fsdp'))
- first_shift_grad: float32 [1024], P(('ctx', 'fsdp'))
- second_gain_grad: float32 [1024], P(('ctx', 'fsdp'))
- second_shift_grad: float32 [1024], P(('ctx', 'fsdp'))
The draws below stay inside these ranges and needn't reach their ends.
All inputs are finite; a program needn't handle non-finite values.
Results may differ from the reference program's by a relative error of at most 0.017.
The reference program's roundings to bfloat16 on the way count: a program that leaves them out, or rounds other values in their place, can miss the bound.
Values may be sent and summed in bfloat16 or wider, within the bound.
A program may use at most 576 MiB of HBM per device.

```python
import math
import jax
import jax.numpy as jnp
from jax import lax

D = 1024
HEADS = 16
HEAD = 64
FF = 4096
MICRO = 2
TOK_DEV = 64
SEQS = 2
LEN = 1024
N_CTX = 16


def raised(entries, key, source, target, parts, factor):
    owner, partner = [(jnp.arange(entries.shape[axis_at]) // (entries.shape[axis_at] // parts)).reshape([-1 if axis == axis_at else 1 for axis in range(entries.ndim)]) for axis_at in (source, target)]
    chosen = jax.random.permutation(key, parts)[partner]
    strong = (owner == chosen) | (owner == (partner + parts // 2) % parts)
    return jnp.where(strong, factor * entries, entries)


def steps_of(rng, extent, pieces, low, top_value):
    def one(axis_at, shards_of):
        steps = jax.random.uniform(jax.random.fold_in(jax.random.fold_in(rng, 6), axis_at), (shards_of,), jnp.float32, low / len(pieces), top_value / len(pieces))
        return jnp.repeat(jnp.exp(steps), extent[axis_at] // shards_of).reshape((-1,) + (1,) * (len(extent) - axis_at - 1))

    level = one(*pieces[0])
    for cut in pieces[1:]:
        level = level * one(*cut)
    return level


def bell_draw(key, extent, scale, limit, shards=(), kind=jnp.bfloat16):
    drawn = jax.random.normal(key, extent, jnp.float32) * scale
    if len(shards) > 0:
        drawn = steps_of(key, extent, shards, -0.22, 0.18) * drawn
    return jnp.clip(drawn, min=-limit, max=limit).astype(kind)


def noise_with(key, extent, deviation, bound, pieces, heavy, kind=jnp.bfloat16):
    values = deviation * jax.random.normal(key, extent, jnp.float32)
    if pieces:
        values = values * steps_of(key, extent, pieces, -0.22, 0.18)
    return jnp.clip(raised(values, jax.random.fold_in(key, 3), *heavy), -bound, bound).astype(kind)


def setup_inputs(seed: int = 0) -> dict:
    splits = jax.random.split(jax.random.key(seed), 15)
    tokens = bell_draw(splits[0], (MICRO, SEQS, LEN, D), 1.0, 6.0, ((1, 2), (2, 16)))
    cotangent = noise_with(splits[1], (MICRO, SEQS, LEN, D), 1.0, 6.0, ((1, 2), (2, 16)), (2, 3, 16, 2.0))
    qkv_weight = bell_draw(splits[2], (D, 3 * D), (D // 2) ** -0.5, 0.25, ((0, 32),))
    out_weight = bell_draw(splits[3], (D, D), (D // 64) ** -0.5, 1.5, ((0, 32),))
    up_weight = bell_draw(splits[4], (D, FF), D ** -0.5, 0.1875, ((0, 32),))
    down_weight = bell_draw(splits[5], (FF, D), FF ** -0.5, 0.09375, ((0, 32),))
    qkv_bias = bell_draw(splits[6], (3 * D,), 0.3, 1.5, ((0, 32),))
    out_bias = bell_draw(splits[7], (D,), 0.3, 1.5, ((0, 32),))
    up_bias = bell_draw(splits[8], (FF,), 0.3, 1.5, ((0, 32),))
    down_bias = bell_draw(splits[9], (D,), 0.3, 1.5, ((0, 32),))
    first_gain = jnp.clip(1.0 + 0.1 * jax.random.normal(splits[10], (D,), jnp.float32), 0.5, 1.5).astype(jnp.bfloat16)
    first_shift = bell_draw(splits[11], (D,), 0.3, 1.5, ((0, 32),))
    second_gain = jnp.clip(1.0 + 0.1 * jax.random.normal(splits[12], (D,), jnp.float32), 0.5, 1.5).astype(jnp.bfloat16)
    second_shift = bell_draw(splits[13], (D,), 0.3, 1.5, ((0, 32),))
    return dict(tokens=tokens, cotangent=cotangent, qkv_weight=qkv_weight, out_weight=out_weight, up_weight=up_weight, down_weight=down_weight, qkv_bias=qkv_bias, out_bias=out_bias, up_bias=up_bias, down_bias=down_bias, first_gain=first_gain, first_shift=first_shift, second_gain=second_gain, second_shift=second_shift)


highest = lax.Precision.HIGHEST

@jax.custom_vjp
def low(v):
    return lax.optimization_barrier(v.astype(jnp.bfloat16)).astype(jnp.float32)

@jax.custom_vjp
def low_back(v):
    return v

def low_keep(v):
    return (low(v), None)

def low_pass(kept, grad):
    return (grad,)

def back_keep(v):
    return (v, None)

def back_low(kept, grad):
    return (low(grad),)
low.defvjp(low_keep, low_pass)
low_back.defvjp(back_keep, back_low)

def layernorm(resid, gain, shift):
    center = resid - lax.optimization_barrier(jnp.mean(resid, axis=-1, keepdims=True))
    spread = lax.optimization_barrier(jnp.mean(center * center, axis=-1, keepdims=True))
    return center * lax.rsqrt(spread + 1e-05) * gain + shift

def tables(position):
    freqs = 10000.0 ** (-jnp.arange(0, HEAD, 2, dtype=jnp.float32) / HEAD)
    angles = position[:, None] * freqs[None, :]
    return (jnp.cos(angles)[:, None, :], jnp.sin(angles)[:, None, :])

def rotate(heads_in, cosine, sine):
    middle = heads_in.shape[-1] // 2
    first = heads_in[..., :middle]
    second = heads_in[..., middle:]
    return jnp.concatenate([first * cosine - second * sine, second * cosine + first * sine], axis=-1)

def attend(keys_low, values_low, query_block):
    scores = low_back(jnp.einsum('qhd,khd->hqk', query_block, keys_low, precision=highest) * 0.125)
    chance = low(jax.nn.softmax(scores, axis=-1))
    return jnp.einsum('hqk,khd->qhd', chance, values_low, precision=highest)

def layer(params, sequence):
    qkv_weight, out_weight, up_weight, down_weight, qkv_bias, out_bias, up_bias, down_bias, first_gain, first_shift, second_gain, second_shift = params
    cosine, sine = tables(jnp.arange(LEN, dtype=jnp.float32))
    joined = low_back(jnp.dot(sequence, qkv_weight, precision=highest) + qkv_bias)
    query_low = low(rotate(joined[:, :D].reshape(LEN, HEADS, HEAD), cosine, sine))
    keys_low = low(rotate(joined[:, D:2 * D].reshape(LEN, HEADS, HEAD), cosine, sine))
    values_low = low(joined[:, 2 * D:].reshape(LEN, HEADS, HEAD))
    blockwise = jax.checkpoint(attend)
    span = TOK_DEV * math.gcd(N_CTX, 8)
    blocks = query_low.reshape(LEN // span, span, HEADS, HEAD)
    attended = lax.map(lambda query_block: blockwise(keys_low, values_low, query_block), blocks)
    att_low = low(low_back(attended.reshape(LEN, D)))
    projected = low_back(jnp.dot(att_low, out_weight, precision=highest) + out_bias)
    hidden = layernorm(sequence + projected, first_gain, first_shift)
    preact = low_back(jnp.dot(low(hidden), up_weight, precision=highest) + up_bias)
    activ_low = low(jax.nn.gelu(preact, approximate=False))
    branch = low_back(jnp.dot(activ_low, down_weight, precision=highest) + down_bias)
    return layernorm(hidden + branch, second_gain, second_shift)

def forward(tokens, *params):
    flat = tokens.reshape(MICRO * SEQS, LEN, D)

    def advance(carried, sequence):
        return (carried, layer(params, sequence))
    carried_out, result = lax.scan(advance, jnp.zeros((), jnp.float32), flat)
    return result.reshape(MICRO, SEQS, LEN, D)

def reference(tokens, cotangent, qkv_weight, out_weight, up_weight, down_weight, qkv_bias, out_bias, up_bias, down_bias, first_gain, first_shift, second_gain, second_shift):
    primals = [tokens.astype(jnp.float32), qkv_weight.astype(jnp.float32), out_weight.astype(jnp.float32), up_weight.astype(jnp.float32), down_weight.astype(jnp.float32), qkv_bias.astype(jnp.float32), out_bias.astype(jnp.float32), up_bias.astype(jnp.float32), down_bias.astype(jnp.float32), first_gain.astype(jnp.float32), first_shift.astype(jnp.float32), second_gain.astype(jnp.float32), second_shift.astype(jnp.float32)]
    result, pullback = jax.vjp(forward, *primals)
    grads = pullback(cotangent.astype(jnp.float32))
    return (result.astype(jnp.bfloat16), grads[0], grads[1], grads[2], grads[3], grads[4], grads[5], grads[6], grads[7], grads[8], grads[9], grads[10], grads[11], grads[12])
```

```python
from functools import partial
import math

import jax
import jax.numpy as jnp
from jax import lax
from jax.experimental import pallas as pl
from jax.experimental.pallas import tpu as pltpu
from jax.sharding import PartitionSpec as P
import numpy as np

HEADS = 16
HEAD = 64
MICRO = 2
MESH = pl.DeviceIdType.MESH
F32 = jnp.float32
BF16 = jnp.bfloat16


NCTX = 16
NCHIP = 8
BLK = 64
D = 1024
UNITS = 256
CHUNK = 256


def chip_at(place):
    row = lax.div(place, 4)
    return ((1 - row) * place + row * (7 - place)) * 2 + row


def nn(a, b):
    return jnp.dot(a, b, preferred_element_type=F32)


def nt(a, b):
    return lax.dot_general(a, b, (((1,), (1,)), ((), ())), preferred_element_type=F32)


def tn(a, b):
    return lax.dot_general(a, b, (((0,), (0,)), ((), ())), preferred_element_type=F32)


def row_mean(v):
    return jnp.sum(v, axis=1, keepdims=True) * (1.0 / D)


def col_sum(v):
    return jnp.sum(v, axis=0, keepdims=True)


def layer_kernel(
    x_ref, ct_ref, wq_ref, wo_ref, wu_ref, wd_ref, vec_ref, rope_ref,
    out_ref, tg_ref, gq_ref, go_ref, gu_ref, gd_ref, gs_ref, gb_ref,
    XF, HF, BG, WP, WB, WO, WD, VB, VF, UB, QBR, BQ, WHT, QT, KT, VT, KN, VN, PT, ATD, ATS, AT, AGT,
    H1, Z1, R1, SEC, G2, DG, ACT, PG, PB, SS, SR, RSD, RR, TT, TMP,
    GU, XSU, XRU, AU, RU, GD, XSD, XRD, GO, XSO, XRO, SSO, SRO, PO, RO, SG, SGR, SGT, SGC, AGQ,
    DK, DV, JG, XSQ, XRQ, AQ, RQ, QB1, QB2, QB3,
    agx_s, agx_r, sbx_s, sbx_r, ag_s, ag_r, sb_s, sb_r, ss_s, ss_r, rs_s, rs_r, wo_s, wo_r, wos_s, wos_r,
    all_s, all_r, pair_s, pair_r, po_s, po_r,
):
    c = lax.axis_index("ctx")
    f = lax.axis_index("fsdp")
    core = lax.rem(c, 2)
    chip = lax.div(c, 2)
    yy = lax.rem(chip, 2)
    zz = lax.div(chip, 2)
    r = (1 - yy) * zz + yy * (7 - zz)
    nxt = chip_at(lax.rem(r + 1, 8)) * 2 + core
    prv = chip_at(lax.rem(r + 7, 8)) * 2 + core
    sib = c + 1 - 2 * core
    mine = pl.multiple_of(core * BLK, BLK)
    other = pl.multiple_of((1 - core) * BLK, BLK)
    lane = lax.broadcasted_iota(jnp.int32, (1, 128), 1)
    low_half = lane < 64

    def remote(src, dst, ss, rs, axis, to):
        return pltpu.make_async_remote_copy(
            src_ref=src, dst_ref=dst, send_sem=ss, recv_sem=rs, device_id={axis: to}, device_id_type=MESH
        )

    def target(d):
        return nxt if d == 0 else prv

    def chip_of(d, k):
        return chip_at(lax.rem(r - k + 8, 8) if d == 0 else lax.rem(r + k, 8))

    def send_all(e, src_at, dst):
        @pl.loop(1, NCTX)
        def _(o):
            to = lax.rem(c + o, NCTX)
            remote(src_at(to), dst, all_s.at[e, o], all_r.at[e, o], "ctx", to).start()

    def recv_all(e, dst_at):
        @pl.loop(1, NCTX)
        def _(o):
            at = dst_at(lax.rem(c + NCTX - o, NCTX))
            remote(at, at, all_s.at[e, o], all_r.at[e, o], "ctx", sib).wait_recv()

    def sent_all(e, src_at):
        @pl.loop(1, NCTX)
        def _(o):
            at = src_at(lax.rem(c + o, NCTX))
            remote(at, at, all_s.at[e, o], all_r.at[e, o], "ctx", sib).wait_send()

    def pair(i, src, dst):
        return remote(src, dst, pair_s.at[i], pair_r.at[i], "fsdp", 1 - f)

    barrier = pltpu.get_barrier_semaphore()

    @pl.loop(1, NCTX)
    def _(o):
        pl.semaphore_signal(barrier, inc=1, device_id={"ctx": lax.rem(c + o, NCTX)}, device_id_type=MESH)

    pl.semaphore_signal(barrier, inc=1, device_id={"fsdp": 1 - f}, device_id_type=MESH)
    pl.semaphore_wait(barrier, NCTX)

    def block(buf, m, ch, row0):
        return buf.at[m, ch, pl.ds(row0, BLK)]

    def sub(m, ch, q):
        return XF.at[m, ch, pl.ds(pl.multiple_of(core * BLK + 16 * q, 16), 16)]

    for m in range(2):
        XF[m, chip, pl.ds(mine, BLK)] = x_ref[m]
    WO[c, f] = wo_ref[...]
    WD[f] = wd_ref[...]
    VB[c, f] = vec_ref[...]

    def gather_x(k):
        for d in range(2):
            ch = chip_of(d, k)
            for q in range(4):
                at = sub(d, ch, q)

                @pl.when(k > 0)
                def _():
                    remote(at, at, agx_s.at[d, 0], agx_r.at[d, (k - 1) * 4 + q], "ctx", target(d)).wait_recv()

                @pl.when(k < 7)
                def _():
                    remote(at, at, agx_s.at[d, k * 4 + q], agx_r.at[d, k * 4 + q], "ctx", target(d)).start()

            whole = block(XF, d, ch, mine)
            remote(whole, whole, sbx_s.at[d, k], sbx_r.at[d, k], "ctx", sib).start()

    pl.loop(0, 1)(gather_x)
    pair(0, vec_ref, VB.at[c, f]).start()
    pair(1, wo_ref, WO.at[c, f]).start()
    pair(2, wd_ref, WD.at[f]).start()

    for j in range(8):
        qt = wq_ref[:, 128 * j : 128 * j + 128].astype(F32)
        kt = wq_ref[:, D + 128 * j : D + 128 * j + 128].astype(F32)
        vt = wq_ref[:, 2 * D + 128 * j : 2 * D + 128 * j + 128].astype(F32)
        for e in range(2):
            w = 2 * j + e
            WP[w, :, 0:256] = wu_ref[:, 256 * w : 256 * w + 256]
            qk = jnp.where(low_half, qt, pltpu.roll(kt, 64, 1)) if e == 0 else jnp.where(low_half, pltpu.roll(qt, 64, 1), kt)
            WP[w, :, 256:384] = qk.astype(BF16)
            WP[w, :, 384:512] = (vt if e == 0 else pltpu.roll(vt, 64, 1)).astype(BF16)
    WB[c, f] = WP[c]
    send_all(0, lambda to: WP.at[to], WB.at[c, f])
    pl.loop(1, 5)(gather_x)
    pair(0, VB.at[c, 1 - f], VB.at[c, 1 - f]).wait_recv()
    send_all(1, lambda to: VB.at[c], VB.at[c])
    recv_all(0, lambda s: WB.at[s, f])
    pair(3, WB.at[:, f], WB.at[:, f]).start()
    pl.loop(5, 8)(gather_x)

    @pl.loop(0, 8)
    def _(k):
        for d in range(2):
            at = block(XF, d, chip_of(d, k), other)
            remote(at, at, sbx_s.at[d, k], sbx_r.at[d, k], "ctx", sib).wait_recv()

    pair(1, WO.at[c, 1 - f], WO.at[c, 1 - f]).wait_recv()
    pair(2, WD.at[1 - f], WD.at[1 - f]).wait_recv()
    recv_all(1, lambda s: VB.at[s])

    for j in range(8):
        tiles = [VB[2 * j + q // 2, q % 2] for q in range(4)]
        total = tiles[0]
        for q in range(1, 4):
            total = total + pltpu.roll(tiles[q], 32 * q, 1)
        VF[:, 128 * j : 128 * j + 128] = total
        v1 = pltpu.roll(tiles[1], 96, 1)
        v2 = pltpu.roll(tiles[2], 64, 1)
        v3 = pltpu.roll(tiles[3], 32, 1)
        rows = (
            tiles[0] + jnp.where(lane >= 96, v1, 0.0),
            jnp.where(lane < 64, v1, 0.0) + jnp.where(lane >= 64, v2, 0.0),
            jnp.where(lane < 32, v2, 0.0) + v3,
        )
        for i in range(3):
            QBR[3 * j + i : 3 * j + i + 1, :] = rows[i][1:2, :]
    UB[0:1, 0:128] = VB[c, 0, 0:1, :]
    UB[0:1, 128:256] = VB[c, 1, 0:1, :]
    for i in range(3):
        row = QBR[pl.ds(8 * i + chip, 1), :]
        BQ[i] = jnp.broadcast_to(row, (128, 128)).T
    pair(3, WB.at[:, 1 - f], WB.at[:, 1 - f]).wait_recv()
    WHT[...] = WB[:, :, :, 256:512].reshape(D, 256).T

    def lanes(n):
        return pl.ds(pl.multiple_of(n * CHUNK, CHUNK), CHUNK)

    def turn(u, cosine, sine):
        a, b = u[0:32], u[32:64]
        return jnp.concatenate([a * cosine - b * sine, b * cosine + a * sine], axis=0)

    def unturn(u, cosine, sine):
        a, b = u[0:32], u[32:64]
        return jnp.concatenate([a * cosine + b * sine, b * cosine - a * sine], axis=0)

    @pl.loop(0, 8)
    def _(it):
        m = lax.div(it, 4)
        n = lax.rem(it, 4)
        xs = XF[m, pl.ds(2 * n, 2)].reshape(CHUNK, D)
        joined = nt(WHT[0:192, :], xs)
        cosine = rope_ref[0, :, lanes(n)]
        sine = rope_ref[1, :, lanes(n)]
        q = joined[0:64] + BQ[0, pl.ds(mine, BLK), 0:1]
        k = joined[64:128] + BQ[1, pl.ds(mine, BLK), 0:1]
        v = joined[128:192] + BQ[2, pl.ds(mine, BLK), 0:1]
        q = turn(q, cosine, sine)
        k = turn(k, cosine, sine)
        rows = pl.ds(pl.multiple_of(n * CHUNK, CHUNK), CHUNK)
        QT[m, :, lanes(n)] = q.astype(BF16)
        KT[m, :, lanes(n)] = k.astype(BF16)
        VT[m, :, lanes(n)] = v.astype(BF16)
        KN[m, rows, :] = k.T.astype(BF16)
        VN[m, rows, :] = v.T.astype(BF16)

    def gather_wo(k):
        for d in range(2):
            at = WO.at[chip_of(d, k) * 2 + core, d]

            @pl.when(k > 0)
            def _():
                remote(at, at, wo_s.at[d, 0], wo_r.at[d, k - 1], "ctx", target(d)).wait_recv()

            @pl.when(k < 7)
            def _():
                remote(at, at, wo_s.at[d, k], wo_r.at[d, k], "ctx", target(d)).start()

            remote(at, at, wos_s.at[d, k], wos_r.at[d, k], "ctx", sib).start()

    @pl.loop(0, 8)
    def _(it):
        gather_wo(it)
        m = lax.div(it, 4)
        n = lax.rem(it, 4)
        s = nn(KN[m], QT[m, :, lanes(n)]) * 0.125
        e = jnp.exp(s - jnp.max(s, axis=0, keepdims=True))
        p = (e * (1.0 / jnp.sum(e, axis=0, keepdims=True))).astype(BF16)
        PT[m, :, lanes(n)] = p
        ATD[m, :, lanes(n)] = nn(VT[m], p)

    for j in range(8):
        a0 = ATD[0, :, 128 * j : 128 * j + 128]
        a1 = ATD[1, :, 128 * j : 128 * j + 128]
        ATS[2 * j] = jnp.where(low_half, a0, pltpu.roll(a1, 64, 1)).astype(BF16)
        ATS[2 * j + 1] = jnp.where(low_half, pltpu.roll(a0, 64, 1), a1).astype(BF16)
    AT[c] = ATS[c]
    send_all(2, lambda to: ATS.at[to], AT.at[c])

    @pl.loop(0, 8)
    def _(k):
        for d in range(2):
            at = WO.at[chip_of(d, k) * 2 + 1 - core, d]
            remote(at, at, wos_s.at[d, k], wos_r.at[d, k], "ctx", sib).wait_recv()

    recv_all(2, lambda s: AT.at[s])

    att_rows = AT[...].reshape(D, 128).T
    resid = x_ref[...].reshape(128, D).astype(F32) + nn(att_rows, WO[...].reshape(D, D)) + VF[2:3, :]
    center = resid - row_mean(resid)
    root = lax.rsqrt(row_mean(center * center) + 1e-05)
    z = center * root
    hidden = z * VF[4:5, :] + VF[5:6, :]
    Z1[...] = z
    R1[...] = jnp.broadcast_to(root, (128, 128))
    H1[...] = hidden
    hidden_low = hidden.astype(BF16)
    for m in range(2):
        HF[m, chip, pl.ds(mine, BLK)] = hidden_low[m * BLK : (m + 1) * BLK]

    def ring(p, buf, make, extra, finish):
        def first(k):
            slot = 2 - lax.div(k + 7, 8) * (2 - lax.rem(k, 2))
            for d in range(2):
                ch = chip_of(d, k)
                if buf is not None:
                    at = block(buf, d, ch, mine)

                    @pl.when(k > 0)
                    def _():
                        remote(at, at, ag_s.at[p, d, 0], ag_r.at[p, d, k - 1], "ctx", target(d)).wait_recv()

                    @pl.when(k < 7)
                    def _():
                        remote(at, at, ag_s.at[p, d, k], ag_r.at[p, d, k], "ctx", target(d)).start()

                    remote(at, at, sb_s.at[p, d, k], sb_r.at[p, d, k], "ctx", sib).start()
            for d in range(2):
                ch = chip_of(d, k)
                if buf is not None:
                    at = block(buf, d, ch, other)
                    remote(at, at, sb_s.at[p, d, k], sb_r.at[p, d, k], "ctx", sib).wait_recv()
                PB[d, slot] = make(d, ch)
                SS[d, k] = PB[d, slot, pl.ds(other, BLK)].astype(BF16)
                remote(SS.at[d, k], SR.at[d, k], ss_s.at[p, d, k], ss_r.at[p, d, k], "ctx", sib).start()

        def second(k):
            slot = lax.rem(k, 2)
            for d in range(2):
                at = SR.at[d, k]
                remote(at, at, ss_s.at[p, d, k], ss_r.at[p, d, k], "ctx", sib).wait_recv()

                @pl.when(k > 1)
                def _():
                    got = RR.at[d, k - 1]
                    remote(got, got, rs_s.at[p, d, k], rs_r.at[p, d, k - 1], "ctx", sib).wait_recv()
                    total = PB[d, slot, pl.ds(mine, BLK)] + SR[d, k].astype(F32) + RR[d, k - 1].astype(F32)
                    RSD[d, k] = total.astype(BF16)

                @pl.when(k == 1)
                def _():
                    total = PB[d, slot, pl.ds(mine, BLK)] + SR[d, k].astype(F32)
                    RSD[d, k] = total.astype(BF16)

                remote(RSD.at[d, k], RR.at[d, k], rs_s.at[p, d, k], rs_r.at[p, d, k], "ctx", target(d)).start()

        @pl.loop(0, 9)
        def _(it):
            @pl.when(it < 8)
            def _():
                first(it)

            @pl.when(it > 1)
            def _():
                second(it - 1)

            extra(it)

        for d in range(2):
            at = SR.at[d, 0]
            remote(at, at, ss_s.at[p, d, 0], ss_r.at[p, d, 0], "ctx", sib).wait_recv()
            got = RR.at[d, 7]
            remote(got, got, rs_s.at[p, d, 7], rs_r.at[p, d, 7], "ctx", sib).wait_recv()
            finish(d, PB[d, 2, pl.ds(mine, BLK)] + SR[d, 0].astype(F32) + RR[d, 7].astype(F32))

        @pl.loop(0, 8)
        def _(k):
            for d in range(2):
                if buf is not None:
                    at = block(buf, d, chip_of(d, k), mine)

                    @pl.when(k < 7)
                    def _():
                        remote(at, at, ag_s.at[p, d, k], ag_r.at[p, d, k], "ctx", sib).wait_send()

                    remote(at, at, sb_s.at[p, d, k], sb_r.at[p, d, k], "ctx", sib).wait_send()
                remote(SS.at[d, k], SS.at[d, k], ss_s.at[p, d, k], ss_r.at[p, d, k], "ctx", sib).wait_send()

                @pl.when(k > 0)
                def _():
                    remote(RSD.at[d, k], RSD.at[d, k], rs_s.at[p, d, k], rs_r.at[p, d, k], "ctx", sib).wait_send()

    def nothing(it):
        pass

    def up_w():
        return WB[:, :, :, 0:256].reshape(D, UNITS)

    def down_w():
        return WD[...].reshape(UNITS, D)

    def make_up(m, ch):
        u = nn(HF[m, ch], up_w()) + UB[0:1, :]
        phi = 0.5 * (1.0 + lax.erf(u * 0.7071067811865476))
        a = (u * phi).astype(BF16)
        DG[m, ch] = phi + u * (jnp.exp(-0.5 * u * u) * 0.3989422804014327)
        ACT[m, ch] = a
        return nn(a, down_w())

    def finish_up(d, total):
        rows = slice(d * BLK, (d + 1) * BLK)
        SEC[rows, :] = H1[rows, :] + total + VF[3:4, :]

    ring(0, HF, make_up, nothing, finish_up)

    resid = SEC[...]
    center = resid - row_mean(resid)
    root = lax.rsqrt(row_mean(center * center) + 1e-05)
    z = center * root
    out_ref[...] = (z * VF[6:7, :] + VF[7:8, :]).astype(BF16).reshape(2, BLK, D)
    cot = ct_ref[...].reshape(128, D).astype(F32)
    SG[...] = jnp.zeros((8, D), F32)
    SG[4:5, :] = col_sum(cot * z)
    SG[5:6, :] = col_sum(cot)
    u = cot * VF[6:7, :]
    grad = (u - row_mean(u) - z * row_mean(u * z)) * root
    G2[...] = grad
    grad_low = grad.astype(BF16)
    SG[1:2, :] = col_sum(grad_low.astype(F32))
    for m in range(2):
        BG[m, chip, pl.ds(mine, BLK)] = grad_low[m * BLK : (m + 1) * BLK]

    def make_down(m, ch):
        pg = (nt(BG[m, ch], down_w()) * DG[m, ch]).astype(BF16)
        PG[m, ch] = pg
        return nt(pg, up_w())

    def finish_down(d, total):
        rows = slice(d * BLK, (d + 1) * BLK)
        SEC[rows, :] = G2[rows, :] + total

    ring(1, BG, make_down, nothing, finish_down)

    hid = SEC[...]
    z = Z1[...]
    SG[2:3, :] = col_sum(hid * z)
    SG[3:4, :] = col_sum(hid)
    u = hid * VF[4:5, :]
    grad = (u - row_mean(u) - z * row_mean(u * z)) * R1[:, 0:1]
    H1[...] = grad
    proj = grad.astype(BF16)
    SG[0:1, :] = col_sum(proj.astype(F32))
    sent_all(2, lambda to: ATS.at[to])
    ATS[...] = nt(WO[...].reshape(D, D), proj).astype(BF16).reshape(NCTX, HEAD, 128)
    AGT[c] = ATS[c]
    send_all(3, lambda to: ATS.at[to], AGT.at[c])

    TT[...] = PG[...].reshape(2048, UNITS).T
    ones = jnp.ones((8, 2048), BF16)
    SG[6:7, 0:256] = nn(ones, PG[...].reshape(2048, UNITS))[0:1, :]
    pair(4, SG, SGR).start()

    @pl.loop(0, NCTX)
    def _(w):
        TMP[...] = nn(AT[w], proj)
        GO[w] = TMP[pl.ds(pl.multiple_of(f * 32, 32), 32)]
        XSO[w] = TMP[pl.ds(pl.multiple_of((1 - f) * 32, 32), 32)].astype(BF16)

    pair(5, XSO, XRO).start()

    for n in range(4):
        g = nn(TT[...], HF[:, :, :, CHUNK * n : CHUNK * (n + 1)].reshape(2048, CHUNK))
        GU[4 * n : 4 * n + 4] = g.T.reshape(4, 2, 32, UNITS)
    XSU[...] = GU[:, 1 - f].astype(BF16)
    pair(6, XSU, XRU).start()
    TT[...] = ACT[...].reshape(2048, UNITS).T
    for n in range(4):
        g = nn(TT[...], BG[:, :, :, CHUNK * n : CHUNK * (n + 1)].reshape(2048, CHUNK))
        GD[:, :, CHUNK * n : CHUNK * (n + 1)] = g.reshape(2, 128, CHUNK)
    XSD[...] = GD[1 - f].astype(BF16)
    pair(7, XSD, XRD).start()
    recv_all(3, lambda s: AGT.at[s])
    sent_all(3, lambda to: ATS.at[to])

    for j in range(8):
        t0 = AGT[2 * j].astype(F32)
        t1 = AGT[2 * j + 1].astype(F32)
        AGQ[0, :, 128 * j : 128 * j + 128] = jnp.where(low_half, t0, pltpu.roll(t1, 64, 1)).astype(BF16)
        AGQ[1, :, 128 * j : 128 * j + 128] = jnp.where(low_half, pltpu.roll(t0, 64, 1), t1).astype(BF16)

    DK[...] = jnp.zeros((2, HEAD, D), F32)
    DV[...] = jnp.zeros((2, HEAD, D), F32)

    def go_sum():
        pair(5, XRO, XRO).wait_recv()
        for j in range(NCHIP):
            w = 2 * j + core
            v = 2 * j + 1 - core
            GO[w] = GO[w] + XRO[w].astype(F32)
            SSO[j] = (GO[v] + XRO[v].astype(F32)).astype(BF16)
        remote(SSO, SRO, po_s.at[0], po_r.at[0], "ctx", sib).start()

    def go_push():
        remote(SRO, SRO, po_s.at[0], po_r.at[0], "ctx", sib).wait_recv()
        for j in range(NCHIP):
            w = 2 * j + core
            GO[w] = GO[w] + SRO[j].astype(F32)
            PO[j] = GO[w].astype(BF16)
        for o in range(1, NCHIP):
            j = lax.rem(chip + o, NCHIP)
            remote(PO.at[j], RO.at[chip], po_s.at[o], po_r.at[o], "ctx", 2 * j + core).start()

    def small_push():
        pair(4, SGR, SGR).wait_recv()
        SGT[...] = SG[...] + SGR[...]
        SGC[c] = SGT[:, pl.ds(pl.multiple_of(chip * 128, 128), 128)]
        send_all(4, lambda to: SGT.at[:, pl.ds(pl.multiple_of(lax.div(to, 2) * 128, 128), 128)], SGC.at[c])

    def up_push():
        pair(6, XRU, XRU).wait_recv()
        AU[...] = (GU[:, f] + XRU[...].astype(F32)).astype(BF16)
        RU[c] = AU[c]
        send_all(5, lambda to: AU.at[to], RU.at[c])

    @pl.loop(0, 8)
    def _(it):
        pl.when(it == 2)(small_push)
        pl.when(it == 3)(go_sum)
        pl.when(it == 5)(go_push)
        pl.when(it == 6)(up_push)
        m = lax.div(it, 4)
        n = lax.rem(it, 4)
        q = QT[m, :, lanes(n)]
        g = AGQ[m, :, lanes(n)]
        delta = jnp.sum(g.astype(F32) * ATD[m, :, lanes(n)], axis=0, keepdims=True)
        p = PT[m, :, lanes(n)]
        ds = (p.astype(F32) * (nn(VN[m], g) - delta)).astype(BF16)
        DK[m] = DK[m] + nt(q, ds)
        DV[m] = DV[m] + nt(g, p)
        dq = nn(KT[m], ds) * 0.125
        JG[m, 0:64, lanes(n)] = unturn(dq, rope_ref[0, :, lanes(n)], rope_ref[1, :, lanes(n)]).astype(BF16)

    for m in range(2):
        JG[m, 64:128, :] = unturn(DK[m] * 0.125, rope_ref[0], rope_ref[1]).astype(BF16)
        JG[m, 128:192, :] = DV[m].astype(BF16)

    def make_token(m, ch):
        jg = JG[m, :, pl.ds(pl.multiple_of(ch * 128, 128), 128)]
        return tn(jg, WHT[0:192, :])

    def finish_token(d, total):
        tg_ref[d] = H1[d * BLK : (d + 1) * BLK, :] + total

    def qkv_grad():
        for n in range(4):
            cols = slice(CHUNK * n, CHUNK * (n + 1))
            g = nn(JG[0], XF[0, :, :, cols].reshape(D, CHUNK)) + nn(JG[1], XF[1, :, :, cols].reshape(D, CHUNK))
            g = jnp.concatenate([g, jnp.zeros((64, CHUNK), F32)], axis=0)
            GU[4 * n : 4 * n + 4] = g.T.reshape(4, 2, 32, UNITS)
        XSQ[...] = GU[:, 1 - f].astype(BF16)
        pair(8, XSQ, XRQ).start()
        ones8 = jnp.ones((8, D), BF16)
        b = nt(ones8, JG[0]) + nt(ones8, JG[1])
        QB1[...] = jnp.concatenate([b, jnp.zeros((8, 64), F32)], axis=1)
        pair(9, QB1, QB2).start()

    def qkv_push():
        pair(8, XRQ, XRQ).wait_recv()
        AQ[...] = (GU[:, f] + XRQ[...].astype(F32)).astype(BF16)
        RQ[c] = AQ[c]
        send_all(6, lambda to: AQ.at[to], RQ.at[c])
        pair(9, QB2, QB2).wait_recv()
        pair(9, QB1, QB1).wait_send()
        QB1[...] = QB1[...] + QB2[...]
        QB3[c] = QB1[...]
        send_all(7, lambda to: QB1, QB3.at[c])

    def out_rest():
        for o in range(1, NCHIP):
            j = lax.rem(chip + NCHIP - o, NCHIP)
            remote(RO.at[j], RO.at[j], po_s.at[o], po_r.at[o], "ctx", sib).wait_recv()
        total = GO[c]
        for o in range(1, NCHIP):
            total = total + RO[lax.rem(chip + o, NCHIP)].astype(F32)
        go_ref[...] = total

    def small_rest():
        recv_all(4, lambda s: SGC.at[s])
        total = SGC[0]
        for w in range(1, NCTX):
            total = total + SGC[w]
        gs_ref[...] = total
        gs_ref[6:7, :] = SGT[6:7, pl.ds(pl.multiple_of(f * 128, 128), 128)]
        pair(7, XRD, XRD).wait_recv()
        gd_ref[...] = GD[f] + XRD[...].astype(F32)

    def up_rest():
        recv_all(5, lambda s: RU.at[s])
        for w in range(NCTX):
            gu_ref[:, UNITS * w : UNITS * (w + 1)] = RU[w].astype(F32)

    def on_the_way(it):
        pl.when(it == 1)(qkv_grad)
        pl.when(it == 3)(small_rest)
        pl.when(it == 4)(qkv_push)
        pl.when(it == 5)(out_rest)
        pl.when(it == 6)(up_rest)

    ring(2, None, make_token, on_the_way, finish_token)

    recv_all(6, lambda s: RQ.at[s])
    for j in range(8):
        a = RQ[2 * j].astype(F32)
        b = RQ[2 * j + 1].astype(F32)
        cols = slice(128 * j, 128 * (j + 1))
        gq_ref[:, cols] = jnp.where(low_half, a[:, 0:128], pltpu.roll(b[:, 0:128], 64, 1))
        gq_ref[:, D + 128 * j : D + 128 * (j + 1)] = jnp.where(low_half, pltpu.roll(a[:, 0:128], 64, 1), b[:, 0:128])
        gq_ref[:, 2 * D + 128 * j : 2 * D + 128 * (j + 1)] = jnp.where(low_half, a[:, 128:256], pltpu.roll(b[:, 128:256], 64, 1))
    recv_all(7, lambda s: QB3.at[s])
    for j in range(8):
        a = QB3[2 * j]
        b = QB3[2 * j + 1]
        rows = (
            jnp.where(low_half, a[:, 0:128], pltpu.roll(b[:, 0:128], 64, 1)),
            jnp.where(low_half, pltpu.roll(a[:, 0:128], 64, 1), b[:, 0:128]),
            jnp.where(low_half, a[:, 128:256], pltpu.roll(b[:, 128:256], 64, 1)),
        )
        for i in range(3):
            gb_ref[8 * i + j : 8 * i + j + 1, :] = rows[i][0:1, :]

    @pl.loop(0, 8)
    def _(k):
        for d in range(2):
            ch = chip_of(d, k)

            @pl.when(k < 7)
            def _():
                for q in range(4):
                    at = sub(d, ch, q)
                    remote(at, at, agx_s.at[d, k * 4 + q], agx_r.at[d, k * 4 + q], "ctx", sib).wait_send()
                at = WO.at[ch * 2 + core, d]
                remote(at, at, wo_s.at[d, k], wo_r.at[d, k], "ctx", sib).wait_send()

            at = WO.at[ch * 2 + core, d]
            remote(at, at, wos_s.at[d, k], wos_r.at[d, k], "ctx", sib).wait_send()
            whole = block(XF, d, ch, mine)
            remote(whole, whole, sbx_s.at[d, k], sbx_r.at[d, k], "ctx", sib).wait_send()

    sent_all(0, lambda to: WP.at[to])
    sent_all(1, lambda to: VB.at[c])
    sent_all(4, lambda to: SGT.at[:, pl.ds(pl.multiple_of(lax.div(to, 2) * 128, 128), 128)])
    sent_all(5, lambda to: AU.at[to])
    sent_all(6, lambda to: AQ.at[to])
    sent_all(7, lambda to: QB1)
    remote(SSO, SSO, po_s.at[0], po_r.at[0], "ctx", sib).wait_send()
    for o in range(1, NCHIP):
        j = lax.rem(chip + o, NCHIP)
        remote(PO.at[j], PO.at[j], po_s.at[o], po_r.at[o], "ctx", sib).wait_send()
    for i, at in enumerate((vec_ref, wo_ref, wd_ref, WB.at[:, f], SG, XSO, XSU, XSD, XSQ)):
        pair(i, at, at).wait_send()


def rope_tables():
    freqs = (np.float32(10000.0) ** (-np.arange(0, HEAD, 2, dtype=np.float32) / np.float32(HEAD))).astype(np.float32)
    angles = freqs[:, None] * np.arange(1024, dtype=np.float32)[None, :]
    return np.stack([np.cos(angles), np.sin(angles)]).astype(np.float32)


def fused_body(
    tokens, cotangent, qkv_weight, out_weight, up_weight, down_weight, qkv_bias, out_bias, up_bias, down_bias,
    first_gain, first_shift, second_gain, second_shift,
):
    def wide(v):
        return jnp.pad(v.astype(F32), (0, 128 - v.shape[0]))

    vec = jnp.stack(
        [wide(v) for v in (up_bias, qkv_bias, out_bias, down_bias, first_gain, first_shift, second_gain, second_shift)]
    )
    scratch = [
        ((2, 8, 128, D), BF16), ((2, 8, 128, D), BF16), ((2, 8, 128, D), BF16),
        ((16, 32, 512), BF16), ((16, 2, 32, 512), BF16), ((16, 2, 32, D), BF16), ((2, 128, D), BF16),
        ((16, 2, 8, 128), F32), ((8, D), F32), ((8, UNITS), F32), ((24, 128), F32), ((3, 128, 128), F32),
        ((256, D), BF16),
        ((2, 64, D), BF16), ((2, 64, D), BF16), ((2, 64, D), BF16), ((2, D, 64), BF16), ((2, D, 64), BF16),
        ((2, D, D), BF16), ((2, 64, D), F32),
        ((16, 64, 128), BF16), ((16, 64, 128), BF16), ((16, 64, 128), BF16),
        ((128, D), F32), ((128, D), F32), ((128, 128), F32), ((128, D), F32), ((128, D), F32),
        ((2, 8, 128, UNITS), F32), ((2, 8, 128, UNITS), BF16), ((2, 8, 128, UNITS), BF16),
        ((2, 3, 128, D), F32),
        ((2, 8, BLK, D), BF16), ((2, 8, BLK, D), BF16), ((2, 8, BLK, D), BF16), ((2, 8, BLK, D), BF16),
        ((UNITS, 2048), BF16), ((64, D), F32),
        ((16, 2, 32, UNITS), F32), ((16, 32, UNITS), BF16), ((16, 32, UNITS), BF16), ((16, 32, UNITS), BF16), ((16, 32, UNITS), BF16),
        ((2, 128, D), F32), ((128, D), BF16), ((128, D), BF16),
        ((16, 32, D), F32), ((16, 32, D), BF16), ((16, 32, D), BF16),
        ((8, 32, D), BF16), ((8, 32, D), BF16), ((8, 32, D), BF16), ((8, 32, D), BF16),
        ((8, D), F32), ((8, D), F32), ((8, D), F32), ((16, 8, 128), F32), ((2, 64, D), BF16),
        ((2, 64, D), F32), ((2, 64, D), F32), ((2, 192, D), BF16),
        ((16, 32, UNITS), BF16), ((16, 32, UNITS), BF16), ((16, 32, UNITS), BF16), ((16, 32, UNITS), BF16),
        ((8, 256), F32), ((8, 256), F32), ((16, 8, 256), F32),
    ]
    sems = [(2, 32)] * 2 + [(2, 8)] * 2 + [(2, 2, 8)] * 4 + [(3, 2, 8)] * 4 + [(2, 8)] * 4 + [(8, 16)] * 2 + [(10,)] * 2 + [(8,)] * 2
    vmem = pl.BlockSpec(memory_space=pltpu.VMEM)
    shapes = [((2, BLK, D), BF16), ((2, BLK, D), F32), ((32, 3 * D), F32), ((32, D), F32), ((32, 4 * D), F32), ((128, D), F32), ((8, 128), F32), ((24, 128), F32)]
    output, token_grad, qkv_grad, out_grad, up_grad, down_grad, small, qkv_small = pl.pallas_call(
        layer_kernel,
        out_shape=[jax.ShapeDtypeStruct(s, t) for s, t in shapes],
        in_specs=[vmem] * 8,
        out_specs=[vmem] * 8,
        scratch_shapes=[pltpu.VMEM(s, t) for s, t in scratch] + [pltpu.SemaphoreType.DMA(s) for s in sems],
        compiler_params=pltpu.CompilerParams(collective_id=0, has_side_effects=True, vmem_limit_bytes=VMEM_LIMIT),
        name="layer",
    )(tokens[:, 0], cotangent[:, 0], qkv_weight, out_weight, up_weight, down_weight, vec, jnp.asarray(rope_tables()))
    index = lax.axis_index("ctx") * 2 + lax.axis_index("fsdp")
    part = lax.dynamic_slice_in_dim(small, 32 * lax.rem(index, 4), 32, 1)
    qkv_part = lax.dynamic_slice_in_dim(qkv_small.reshape(3 * D), 96 * index, 96, 0)
    return (
        output[:, None], token_grad[:, None], qkv_grad, out_grad, up_grad, down_grad,
        qkv_part, part[0], small[6], part[1], part[2], part[3], part[4], part[5],
    )


VMEM_LIMIT = 63 * 1024 * 1024


def layernorm(resid, gain, shift):
    center = resid - jnp.mean(resid, axis=-1, keepdims=True)
    spread = jnp.mean(center * center, axis=-1, keepdims=True)
    return center * lax.rsqrt(spread + 1e-05) * gain + shift


def tables(position):
    freqs = 10000.0 ** (-jnp.arange(0, HEAD, 2, dtype=jnp.float32) / HEAD)
    angles = position[:, None] * freqs[None, :]
    return (jnp.cos(angles)[:, None, :], jnp.sin(angles)[:, None, :])


def rotate(heads_in, cosine, sine):
    middle = heads_in.shape[-1] // 2
    first = heads_in[..., :middle]
    second = heads_in[..., middle:]
    return jnp.concatenate(
        [first * cosine - second * sine, second * cosine + first * sine], axis=-1
    )


def unrotate(heads_in, cosine, sine):
    middle = heads_in.shape[-1] // 2
    first = heads_in[..., :middle]
    second = heads_in[..., middle:]
    return jnp.concatenate(
        [first * cosine + second * sine, second * cosine - first * sine], axis=-1
    )


def split_heads(flat_rows):
    return flat_rows.reshape(flat_rows.shape[0], HEADS, HEAD)


def over_blocks(update, carried, count, limit):
    size = math.gcd(count, limit)

    def advance(block_idx, state):
        return update(state, block_idx * size, size)

    return lax.fori_loop(0, count // size, advance, carried)


def column_sum(matrix):
    return jnp.sum(matrix.astype(jnp.float32), axis=0)


def forward_local(sequence, weights_now, cosine, sine, group):
    (
        qkv_full,
        out_full,
        up_full,
        down_full,
        qkv_vector,
        out_vector,
        up_vector,
        down_vector,
        gain_first,
        shift_first,
        gain_second,
        shift_second,
    ) = weights_now
    rows = sequence.shape[0]
    width = sequence.shape[1]
    joined = jnp.dot(sequence, qkv_full, preferred_element_type=jnp.float32) + qkv_vector.astype(
        jnp.float32
    )
    query_flat = (
        rotate(split_heads(joined[:, :width]), cosine, sine)
        .astype(jnp.bfloat16)
        .reshape(rows, width)
    )
    keys_flat = (
        rotate(split_heads(joined[:, width : 2 * width]), cosine, sine)
        .astype(jnp.bfloat16)
        .reshape(rows, width)
    )
    values_flat = joined[:, 2 * width :].astype(jnp.bfloat16)
    query_heads = split_heads(query_flat)
    start_state = (
        jnp.full((HEADS, rows), -1e30, jnp.float32),
        jnp.zeros((HEADS, rows), jnp.float32),
        jnp.zeros((rows, HEADS, HEAD), jnp.float32),
    )
    keys_piece = lax.all_gather(keys_flat, "ctx", axis=0, tiled=True)
    values_piece = lax.all_gather(values_flat, "ctx", axis=0, tiled=True)

    def absorb_block(state, offset, size):
        running, total, accum = state
        key_block = split_heads(lax.dynamic_slice_in_dim(keys_piece, offset, size, 0))
        value_block = split_heads(lax.dynamic_slice_in_dim(values_piece, offset, size, 0))
        scores = (
            jnp.einsum("qhd,khd->hqk", query_heads, key_block, preferred_element_type=jnp.float32)
            * 0.125
        )
        highest_new = jnp.maximum(running, jnp.max(scores, axis=-1))
        factor = jnp.exp(running - highest_new)
        expo = jnp.exp(scores - highest_new[:, :, None])
        total = total * factor + jnp.sum(expo, axis=-1)
        accum = accum * factor.T[:, :, None] + jnp.einsum(
            "hqk,khd->qhd",
            expo.astype(jnp.bfloat16),
            value_block,
            preferred_element_type=jnp.float32,
        )
        return (highest_new, total, accum)

    running, total, accum = over_blocks(absorb_block, start_state, keys_piece.shape[0], group)
    attended = accum / total.T[:, :, None]
    logsum = running + jnp.log(total)
    att_low = attended.reshape(rows, width).astype(jnp.bfloat16)
    projected = jnp.dot(att_low, out_full, preferred_element_type=jnp.float32) + out_vector.astype(
        jnp.float32
    )
    resid_first = sequence.astype(jnp.float32) + projected
    hidden = layernorm(resid_first, gain_first.astype(jnp.float32), shift_first.astype(jnp.float32))
    hidden_low = hidden.astype(jnp.bfloat16)
    preact = jnp.dot(hidden_low, up_full, preferred_element_type=jnp.float32) + up_vector.astype(
        jnp.float32
    )
    activ_low = jax.nn.gelu(preact, approximate=False).astype(jnp.bfloat16)
    branch = jnp.dot(activ_low, down_full, preferred_element_type=jnp.float32) + down_vector.astype(
        jnp.float32
    )
    resid_second = hidden + branch
    output = layernorm(
        resid_second, gain_second.astype(jnp.float32), shift_second.astype(jnp.float32)
    )
    saved = (
        query_flat,
        keys_flat,
        values_flat,
        attended,
        logsum,
        att_low,
        resid_first,
        hidden_low,
        preact,
        activ_low,
        resid_second,
    )
    return (output.astype(jnp.bfloat16), saved)


def body(
    tokens,
    cotangent,
    qkv_weight,
    out_weight,
    up_weight,
    down_weight,
    qkv_bias,
    out_bias,
    up_bias,
    down_bias,
    first_gain,
    first_shift,
    second_gain,
    second_shift,
):
    gathered = (
        lax.all_gather(qkv_weight, ("ctx", "fsdp"), axis=0, tiled=True),
        lax.all_gather(out_weight, ("ctx", "fsdp"), axis=0, tiled=True),
        lax.all_gather(up_weight, ("ctx", "fsdp"), axis=0, tiled=True),
        lax.all_gather(down_weight, ("ctx", "fsdp"), axis=0, tiled=True),
        lax.all_gather(qkv_bias, ("ctx", "fsdp"), axis=0, tiled=True),
        lax.all_gather(out_bias, ("ctx", "fsdp"), axis=0, tiled=True),
        lax.all_gather(up_bias, ("ctx", "fsdp"), axis=0, tiled=True),
        lax.all_gather(down_bias, ("ctx", "fsdp"), axis=0, tiled=True),
        lax.all_gather(first_gain, ("ctx", "fsdp"), axis=0, tiled=True),
        lax.all_gather(first_shift, ("ctx", "fsdp"), axis=0, tiled=True),
        lax.all_gather(second_gain, ("ctx", "fsdp"), axis=0, tiled=True),
        lax.all_gather(second_shift, ("ctx", "fsdp"), axis=0, tiled=True),
    )
    rows = tokens.shape[2]
    width = tokens.shape[3]
    cycle_size = lax.axis_size("ctx")
    group = rows * math.gcd(cycle_size, 8)
    length = rows * cycle_size
    position = (lax.axis_index("ctx") * rows + jnp.arange(rows)).astype(jnp.float32)
    cosine, sine = tables(position)
    outputs = []
    savings = []
    for micro_idx in range(MICRO):
        output, saved = forward_local(tokens[micro_idx, 0], gathered, cosine, sine, group)
        outputs.append(output)
        savings.append(saved)
    weights_back = (
        lax.all_gather(qkv_weight, ("ctx", "fsdp"), axis=0, tiled=True),
        lax.all_gather(out_weight, ("ctx", "fsdp"), axis=0, tiled=True),
        lax.all_gather(up_weight, ("ctx", "fsdp"), axis=0, tiled=True),
        lax.all_gather(down_weight, ("ctx", "fsdp"), axis=0, tiled=True),
        lax.all_gather(qkv_bias, ("ctx", "fsdp"), axis=0, tiled=True),
        lax.all_gather(out_bias, ("ctx", "fsdp"), axis=0, tiled=True),
        lax.all_gather(up_bias, ("ctx", "fsdp"), axis=0, tiled=True),
        lax.all_gather(down_bias, ("ctx", "fsdp"), axis=0, tiled=True),
        lax.all_gather(first_gain, ("ctx", "fsdp"), axis=0, tiled=True),
        lax.all_gather(first_shift, ("ctx", "fsdp"), axis=0, tiled=True),
        lax.all_gather(second_gain, ("ctx", "fsdp"), axis=0, tiled=True),
        lax.all_gather(second_shift, ("ctx", "fsdp"), axis=0, tiled=True),
    )
    (
        qkv_full,
        out_full,
        up_full,
        down_full,
        qkv_vector,
        out_vector,
        up_vector,
        down_vector,
        gain_first,
        shift_first,
        gain_second,
        shift_second,
    ) = weights_back
    token_grads = []
    totals = []
    for micro_idx in range(MICRO):
        (
            query_flat,
            keys_flat,
            values_flat,
            attended,
            logsum,
            att_low,
            resid_first,
            hidden_low,
            preact,
            activ_low,
            resid_second,
        ) = savings[micro_idx]
        sequence = tokens[micro_idx, 0]
        grad_out = cotangent[micro_idx, 0].astype(jnp.float32)
        unused_two, second_back = jax.vjp(
            layernorm,
            resid_second,
            gain_second.astype(jnp.float32),
            shift_second.astype(jnp.float32),
        )
        grad_second, second_gain_grad, second_shift_grad = second_back(grad_out)
        branch_grad = grad_second.astype(jnp.bfloat16)
        down_bias_grad = column_sum(branch_grad)
        down_weight_grad = jnp.einsum(
            "tf,td->fd", activ_low, branch_grad, preferred_element_type=jnp.float32
        )
        activ_grad = jnp.einsum(
            "td,fd->tf", branch_grad, down_full, preferred_element_type=jnp.float32
        )
        unused_gelu, gelu_back = jax.vjp(partial(jax.nn.gelu, approximate=False), preact)
        preact_grad = gelu_back(activ_grad)[0].astype(jnp.bfloat16)
        up_bias_grad = column_sum(preact_grad)
        up_weight_grad = jnp.einsum(
            "td,tf->df", hidden_low, preact_grad, preferred_element_type=jnp.float32
        )
        hidden_grad = grad_second + jnp.einsum(
            "tf,df->td", preact_grad, up_full, preferred_element_type=jnp.float32
        )
        unused_one, first_back = jax.vjp(
            layernorm, resid_first, gain_first.astype(jnp.float32), shift_first.astype(jnp.float32)
        )
        grad_first, first_gain_grad, first_shift_grad = first_back(hidden_grad)
        proj_grad = grad_first.astype(jnp.bfloat16)
        out_bias_grad = column_sum(proj_grad)
        out_weight_grad = jnp.einsum(
            "tc,te->ce", att_low, proj_grad, preferred_element_type=jnp.float32
        )
        att_grad = jnp.einsum(
            "te,ce->tc", proj_grad, out_full, preferred_element_type=jnp.float32
        ).astype(jnp.bfloat16)
        att_heads = split_heads(att_grad)
        query_heads = split_heads(query_flat)
        delta = jnp.sum(att_heads.astype(jnp.float32) * attended, axis=-1).T
        key_all, value_all = (
            lax.all_gather(keys_flat, "ctx", axis=0, tiled=True),
            lax.all_gather(values_flat, "ctx", axis=0, tiled=True),
        )

        def query_update(state, offset, size):
            key_block = split_heads(lax.dynamic_slice_in_dim(key_all, offset, size, 0))
            value_block = split_heads(lax.dynamic_slice_in_dim(value_all, offset, size, 0))
            scores = (
                jnp.einsum(
                    "qhd,khd->hqk", query_heads, key_block, preferred_element_type=jnp.float32
                )
                * 0.125
            )
            chance = jnp.exp(scores - logsum[:, :, None])
            dprob = jnp.einsum(
                "qhd,khd->hqk", att_heads, value_block, preferred_element_type=jnp.float32
            )
            score_grad = (chance * (dprob - delta[:, :, None])).astype(jnp.bfloat16)
            return state + jnp.einsum(
                "hqk,khd->qhd", score_grad, key_block, preferred_element_type=jnp.float32
            )

        query_grad = (
            over_blocks(query_update, jnp.zeros((rows, HEADS, HEAD), jnp.float32), length, group)
            * 0.125
        )

        def fill(state, offset, size):
            key_block = split_heads(lax.dynamic_slice_in_dim(key_all, offset, size, 0))
            value_block = split_heads(lax.dynamic_slice_in_dim(value_all, offset, size, 0))
            scores = (
                jnp.einsum(
                    "qhd,khd->hqk", query_heads, key_block, preferred_element_type=jnp.float32
                )
                * 0.125
            )
            chance = jnp.exp(scores - logsum[:, :, None])
            value_part = jnp.einsum(
                "hqk,qhd->khd",
                chance.astype(jnp.bfloat16),
                att_heads,
                preferred_element_type=jnp.float32,
            )
            dprob = jnp.einsum(
                "qhd,khd->hqk", att_heads, value_block, preferred_element_type=jnp.float32
            )
            score_grad = (chance * (dprob - delta[:, :, None])).astype(jnp.bfloat16)
            key_part = (
                jnp.einsum(
                    "hqk,qhd->khd", score_grad, query_heads, preferred_element_type=jnp.float32
                )
                * 0.125
            )
            piece = jnp.concatenate(
                [key_part.reshape(size, width), value_part.reshape(size, width)], axis=1
            )
            return lax.dynamic_update_slice_in_dim(state, piece, offset, 0)

        combined = lax.psum_scatter(
            over_blocks(
                fill,
                jnp.zeros((lax.axis_size("ctx") * rows, 2 * width), jnp.float32),
                lax.axis_size("ctx") * rows,
                group,
            ),
            "ctx",
            scatter_dimension=0,
            tiled=True,
        )
        key_grad = split_heads(combined[:, :width])
        value_grad = combined[:, width:]
        joined_grad = jnp.concatenate(
            [
                unrotate(query_grad, cosine, sine).reshape(rows, width),
                unrotate(key_grad, cosine, sine).reshape(rows, width),
                value_grad,
            ],
            axis=1,
        ).astype(jnp.bfloat16)
        qkv_bias_grad = column_sum(joined_grad)
        qkv_weight_grad = jnp.einsum(
            "tc,te->ce", sequence, joined_grad, preferred_element_type=jnp.float32
        )
        token_grads.append(
            grad_first
            + jnp.einsum("te,ce->tc", joined_grad, qkv_full, preferred_element_type=jnp.float32)
        )
        fresh = [
            qkv_weight_grad,
            out_weight_grad,
            up_weight_grad,
            down_weight_grad,
            qkv_bias_grad,
            out_bias_grad,
            up_bias_grad,
            down_bias_grad,
            first_gain_grad,
            first_shift_grad,
            second_gain_grad,
            second_shift_grad,
        ]
        if micro_idx == 0:
            totals = fresh
        else:
            totals = [older + newer for older, newer in zip(totals, fresh)]
    summed = (
        lax.psum_scatter(totals[0], ("ctx", "fsdp"), scatter_dimension=0, tiled=True),
        lax.psum_scatter(totals[1], ("ctx", "fsdp"), scatter_dimension=0, tiled=True),
        lax.psum_scatter(totals[2], ("ctx", "fsdp"), scatter_dimension=0, tiled=True),
        lax.psum_scatter(totals[3], ("ctx", "fsdp"), scatter_dimension=0, tiled=True),
        lax.psum_scatter(totals[4], ("ctx", "fsdp"), scatter_dimension=0, tiled=True),
        lax.psum_scatter(totals[5], ("ctx", "fsdp"), scatter_dimension=0, tiled=True),
        lax.psum_scatter(totals[6], ("ctx", "fsdp"), scatter_dimension=0, tiled=True),
        lax.psum_scatter(totals[7], ("ctx", "fsdp"), scatter_dimension=0, tiled=True),
        lax.psum_scatter(totals[8], ("ctx", "fsdp"), scatter_dimension=0, tiled=True),
        lax.psum_scatter(totals[9], ("ctx", "fsdp"), scatter_dimension=0, tiled=True),
        lax.psum_scatter(totals[10], ("ctx", "fsdp"), scatter_dimension=0, tiled=True),
        lax.psum_scatter(totals[11], ("ctx", "fsdp"), scatter_dimension=0, tiled=True),
    )
    output_all = jnp.stack(outputs)[:, None]
    token_all = jnp.stack(token_grads)[:, None]
    return (
        output_all,
        token_all,
        summed[0],
        summed[1],
        summed[2],
        summed[3],
        summed[4],
        summed[5],
        summed[6],
        summed[7],
        summed[8],
        summed[9],
        summed[10],
        summed[11],
    )


def solution(mesh):
    in_specs = (
        P(None, "fsdp", "ctx", None),
        P(None, "fsdp", "ctx", None),
        P(("ctx", "fsdp"), None),
        P(("ctx", "fsdp"), None),
        P(("ctx", "fsdp"), None),
        P(("ctx", "fsdp"), None),
        P(("ctx", "fsdp")),
        P(("ctx", "fsdp")),
        P(("ctx", "fsdp")),
        P(("ctx", "fsdp")),
        P(("ctx", "fsdp")),
        P(("ctx", "fsdp")),
        P(("ctx", "fsdp")),
        P(("ctx", "fsdp")),
    )
    out_specs = (
        P(None, "fsdp", "ctx", None),
        P(None, "fsdp", "ctx", None),
        P(("ctx", "fsdp"), None),
        P(("ctx", "fsdp"), None),
        P(("ctx", "fsdp"), None),
        P(("ctx", "fsdp"), None),
        P(("ctx", "fsdp")),
        P(("ctx", "fsdp")),
        P(("ctx", "fsdp")),
        P(("ctx", "fsdp")),
        P(("ctx", "fsdp")),
        P(("ctx", "fsdp")),
        P(("ctx", "fsdp")),
        P(("ctx", "fsdp")),
    )
    fused = mesh.shape["ctx"] == NCTX and mesh.shape["fsdp"] == 2
    return jax.shard_map(fused_body if fused else body, mesh=mesh, in_specs=in_specs, out_specs=out_specs, check_vma=False)
```

```python
from functools import partial
import math

import jax
import jax.numpy as jnp
from jax import lax
from jax.experimental import pallas as pl
from jax.experimental.pallas import tpu as pltpu
from jax.sharding import PartitionSpec as P
import numpy as np

HEADS = 16
HEAD = 64
MICRO = 2
MESH = pl.DeviceIdType.MESH
F32 = jnp.float32
BF16 = jnp.bfloat16


NCTX = 16
NCHIP = 8
BLK = 64
D = 1024
UNITS = 256
CHUNK = 256
AQS = 2
RQS = 2
ROWS = BLK // RQS


def chip_at(place):
    row = lax.div(place, 4)
    return ((1 - row) * place + row * (7 - place)) * 2 + row


def nn(a, b):
    return jnp.dot(a, b, preferred_element_type=F32)


def nt(a, b):
    return lax.dot_general(a, b, (((1,), (1,)), ((), ())), preferred_element_type=F32)


def tn(a, b):
    return lax.dot_general(a, b, (((0,), (0,)), ((), ())), preferred_element_type=F32)


def row_mean(v):
    return jnp.sum(v, axis=1, keepdims=True) * (1.0 / D)


def col_sum(v):
    return jnp.sum(v, axis=0, keepdims=True)


def layer_kernel(
    x_ref, ct_ref, wq_ref, wo_ref, wu_ref, wd_ref, rope_ref, v0, v1, v2, v3, v4, v5, v6, v7,
    out_ref, tg_ref, gq_ref, go_ref, gu_ref, gd_ref, gs_ref, gb_ref,
    VEC, XF, HF, BG, WP, WB, WU, WO, WD, VB, VF, UB, QBR, BQ, WHT, QT, KT, VT, KN, VN, PT, ATD, ATS, AT, AGT,
    H1, Z1, R1, SEC, G2, DG, ACT, PG, PB, SS, SR, RSD, RR, TT,
    GU, XSU, XRU, AU, RU, GD, XSD, XRD, GO, XSO, XRO, SSO, SRO, SG, SGR, SGT, SGC, AGQ,
    DK, DV, JG, XSQ, XRQ, AQ, RQ, QB1, QB2, QB3,
    one, ag_r, sb_r, ss_r, rs_r, wo_r, all_s, all_r, pair_s, pair_r,
):
    c = lax.axis_index("ctx")
    f = lax.axis_index("fsdp")
    core = lax.rem(c, 2)
    chip = lax.div(c, 2)
    yy = lax.rem(chip, 2)
    zz = lax.div(chip, 2)
    r = (1 - yy) * zz + yy * (7 - zz)
    nxt = chip_at(lax.rem(r + 1, 8)) * 2 + core
    prv = chip_at(lax.rem(r + 7, 8)) * 2 + core
    sib = c + 1 - 2 * core
    mine = pl.multiple_of(core * BLK, BLK)
    other = pl.multiple_of((1 - core) * BLK, BLK)
    lane = lax.broadcasted_iota(jnp.int32, (1, 128), 1)
    low_half = lane < 64

    def remote(src, dst, ss, rs, axis, to):
        return pltpu.make_async_remote_copy(
            src_ref=src, dst_ref=dst, send_sem=ss, recv_sem=rs, device_id={axis: to}, device_id_type=MESH
        )

    def target(d):
        return nxt if d == 0 else prv

    def chip_of(d, k):
        return chip_at(lax.rem(r - k + 8, 8) if d == 0 else lax.rem(r + k, 8))

    def send_all(e, src_at, dst):
        @pl.loop(1, NCTX)
        def _(o):
            to = lax.rem(c + o, NCTX)
            remote(src_at(to), dst, all_s.at[e], all_r.at[e], "ctx", to).start()

    def recv_all(e, slab):
        remote(slab, slab, all_s.at[e], all_r.at[e], "ctx", sib).wait_recv()

    def sent_all(e, slab):
        remote(slab, slab, all_s.at[e], all_r.at[e], "ctx", sib).wait_send()

    def pair(i, src, dst):
        return remote(src, dst, pair_s.at[i], pair_r.at[i], "fsdp", 1 - f)

    agx_s, sbx_s, sbx_r, ag_s, sb_s, ss_s, rs_s, wo_s, wos_s, wos_r, po_s, po_r = (one.at[i] for i in range(12))
    barrier = pltpu.get_barrier_semaphore()

    @pl.loop(1, NCTX)
    def _(o):
        pl.semaphore_signal(barrier, inc=1, device_id={"ctx": lax.rem(c + o, NCTX)}, device_id_type=MESH)

    pl.semaphore_signal(barrier, inc=1, device_id={"fsdp": 1 - f}, device_id_type=MESH)
    pl.semaphore_wait(barrier, NCTX)

    def block(buf, m, ch, row0):
        return buf.at[m, ch, pl.ds(row0, BLK)]

    def sub(m, ch, q):
        return XF.at[m, ch, pl.ds(pl.multiple_of(core * BLK + (BLK // AQS) * q, BLK // AQS), BLK // AQS)]

    for m in range(2):
        XF[m, chip, pl.ds(mine, BLK)] = x_ref[m]
    WO[c, f] = wo_ref[...]
    WD[f] = wd_ref[...]
    VEC[...] = jnp.zeros((8, 128), F32)
    for i, v in enumerate((v0, v1, v2, v3, v4, v5, v6, v7)):
        VEC[i : i + 1, 0 : v.shape[1]] = v[...].astype(F32)
    VB[c, f] = VEC[...]

    def gather_x(k):
        for d in range(2):
            ch = chip_of(d, k)
            for q in range(AQS):
                at = sub(d, ch, q)

                @pl.when(k > 0)
                def _():
                    remote(at, at, agx_s, ag_r.at[d, (k - 1) * AQS + q], "ctx", target(d)).wait_recv()

                @pl.when(k < 7)
                def _():
                    remote(at, at, agx_s, ag_r.at[d, k * AQS + q], "ctx", target(d)).start()

            whole = block(XF, d, ch, mine)
            remote(whole, whole, sbx_s, sbx_r, "ctx", sib).start()

    def gather_wo(k):
        for d in range(2):
            at = WO.at[chip_of(d, k) * 2 + core, d]

            @pl.when(k > 0)
            def _():
                remote(at, at, wo_s, wo_r.at[d, k - 1], "ctx", target(d)).wait_recv()

            @pl.when(k < 7)
            def _():
                remote(at, at, wo_s, wo_r.at[d, k], "ctx", target(d)).start()

            remote(at, at, wos_s, wos_r, "ctx", sib).start()

    pl.loop(0, 1)(gather_x)
    pair(0, VEC, VB.at[c, f]).start()
    pair(1, wo_ref, WO.at[c, f]).start()

    for j in range(8):
        qt = wq_ref[:, 128 * j : 128 * j + 128].astype(F32)
        kt = wq_ref[:, D + 128 * j : D + 128 * j + 128].astype(F32)
        vt = wq_ref[:, 2 * D + 128 * j : 2 * D + 128 * j + 128].astype(F32)
        for e in range(2):
            w = 2 * j + e
            qk = jnp.where(low_half, qt, pltpu.roll(kt, 64, 1)) if e == 0 else jnp.where(low_half, pltpu.roll(qt, 64, 1), kt)
            WP[w, :, 0:128] = qk.astype(BF16)
            WP[w, :, 128:256] = (vt if e == 0 else pltpu.roll(vt, 64, 1)).astype(BF16)
    WB[c, f] = WP[c]
    send_all(0, lambda to: WP.at[to], WB.at[c, f])
    pl.loop(1, 4)(gather_x)
    pair(0, VB.at[c, 1 - f], VB.at[c, 1 - f]).wait_recv()
    send_all(1, lambda to: VB.at[c], VB.at[c])
    recv_all(0, WB.at[0:15, 0])
    pair(3, WB.at[:, f], WB.at[:, f]).start()
    pair(1, WO.at[c, 1 - f], WO.at[c, 1 - f]).wait_recv()

    @pl.loop(4, 8)
    def _(k):
        gather_x(k)
        gather_wo(k - 4)

    WU[c, f] = wu_ref[:, pl.ds(pl.multiple_of(c * UNITS, UNITS), UNITS)]
    send_all(8, lambda to: wu_ref.at[:, pl.ds(pl.multiple_of(to * UNITS, UNITS), UNITS)], WU.at[c, f])
    pair(2, wd_ref, WD.at[f]).start()

    remote(XF.at[0], XF.at[0], sbx_s, sbx_r, "ctx", sib).wait_recv()
    recv_all(1, VB.at[0:15])

    for j in range(8):
        tiles = [VB[2 * j + q // 2, q % 2] for q in range(4)]
        total = tiles[0]
        for q in range(1, 4):
            total = total + pltpu.roll(tiles[q], 32 * q, 1)
        VF[:, 128 * j : 128 * j + 128] = total
        v1 = pltpu.roll(tiles[1], 96, 1)
        v2 = pltpu.roll(tiles[2], 64, 1)
        v3 = pltpu.roll(tiles[3], 32, 1)
        rows = (
            tiles[0] + jnp.where(lane >= 96, v1, 0.0),
            jnp.where(lane < 64, v1, 0.0) + jnp.where(lane >= 64, v2, 0.0),
            jnp.where(lane < 32, v2, 0.0) + v3,
        )
        for i in range(3):
            QBR[3 * j + i : 3 * j + i + 1, :] = rows[i][1:2, :]
    UB[0:1, 0:128] = VB[c, 0, 0:1, :]
    UB[0:1, 128:256] = VB[c, 1, 0:1, :]
    for i in range(3):
        row = QBR[pl.ds(8 * i + chip, 1), :]
        BQ[i] = jnp.broadcast_to(row, (128, 128)).T
    pair(3, WB.at[:, 1 - f], WB.at[:, 1 - f]).wait_recv()
    WHT[...] = WB[...].reshape(D, 256).T

    def lanes(n):
        return pl.ds(pl.multiple_of(n * CHUNK, CHUNK), CHUNK)

    def turn(u, cosine, sine):
        a, b = u[0:32], u[32:64]
        return jnp.concatenate([a * cosine - b * sine, b * cosine + a * sine], axis=0)

    def unturn(u, cosine, sine):
        a, b = u[0:32], u[32:64]
        return jnp.concatenate([a * cosine + b * sine, b * cosine - a * sine], axis=0)

    @pl.loop(0, 8)
    def _(it):
        m = lax.div(it, 4)
        n = lax.rem(it, 4)
        xs = XF[m, pl.ds(2 * n, 2)].reshape(CHUNK, D)
        joined = nt(WHT[0:192, :], xs)
        cosine = rope_ref[0, :, lanes(n)]
        sine = rope_ref[1, :, lanes(n)]
        q = joined[0:64] + BQ[0, pl.ds(mine, BLK), 0:1]
        k = joined[64:128] + BQ[1, pl.ds(mine, BLK), 0:1]
        v = joined[128:192] + BQ[2, pl.ds(mine, BLK), 0:1]
        q = turn(q, cosine, sine)
        k = turn(k, cosine, sine)
        rows = pl.ds(pl.multiple_of(n * CHUNK, CHUNK), CHUNK)
        QT[m, :, lanes(n)] = q.astype(BF16)
        KT[m, :, lanes(n)] = k.astype(BF16)
        VT[m, :, lanes(n)] = v.astype(BF16)
        KN[m, rows, :] = k.T.astype(BF16)
        VN[m, rows, :] = v.T.astype(BF16)

    @pl.loop(0, 8)
    def _(it):
        @pl.when(lax.rem(it, 2) == 0)
        def _():
            gather_wo(4 + lax.div(it, 2))

        @pl.when(it == 5)
        def _():
            recv_all(8, WU.at[0:15, 0])
            pair(10, WU.at[:, f], WU.at[:, f]).start()

        m = lax.div(it, 4)
        n = lax.rem(it, 4)
        s = nn(KN[m], QT[m, :, lanes(n)]) * 0.125
        e = jnp.exp(s - jnp.max(s, axis=0, keepdims=True))
        p = (e * (1.0 / jnp.sum(e, axis=0, keepdims=True))).astype(BF16)
        PT[m, :, lanes(n)] = p
        ATD[m, :, lanes(n)] = nn(VT[m], p)

    for j in range(8):
        a0 = ATD[0, :, 128 * j : 128 * j + 128]
        a1 = ATD[1, :, 128 * j : 128 * j + 128]
        ATS[2 * j] = jnp.where(low_half, a0, pltpu.roll(a1, 64, 1)).astype(BF16)
        ATS[2 * j + 1] = jnp.where(low_half, pltpu.roll(a0, 64, 1), a1).astype(BF16)
    AT[c] = ATS[c]
    send_all(2, lambda to: ATS.at[to], AT.at[c])

    remote(WO.at[0:8], WO.at[0:8], wos_s, wos_r, "ctx", sib).wait_recv()
    recv_all(2, AT.at[0:15])

    att_rows = AT[...].reshape(D, 128).T
    resid = x_ref[...].reshape(128, D).astype(F32) + nn(att_rows, WO[...].reshape(D, D)) + VF[2:3, :]
    center = resid - row_mean(resid)
    root = lax.rsqrt(row_mean(center * center) + 1e-05)
    z = center * root
    hidden = z * VF[4:5, :] + VF[5:6, :]
    Z1[...] = z
    R1[...] = jnp.broadcast_to(root, (128, 128))
    H1[...] = hidden
    hidden_low = hidden.astype(BF16)
    for m in range(2):
        HF[m, chip, pl.ds(mine, BLK)] = hidden_low[m * BLK : (m + 1) * BLK]

    pair(2, WD.at[1 - f], WD.at[1 - f]).wait_recv()
    pair(10, WU.at[:, 1 - f], WU.at[:, 1 - f]).wait_recv()

    def ring(p, buf, make, extra, finish):
        def first(k):
            slot = 2 - lax.div(k + 7, 8) * (2 - lax.rem(k, 2))
            for d in range(2):
                ch = chip_of(d, k)
                if buf is not None:
                    at = block(buf, d, ch, mine)

                    @pl.when(k > 0)
                    def _():
                        remote(at, at, ag_s, ag_r.at[d, k - 1], "ctx", target(d)).wait_recv()

                    @pl.when(k < 7)
                    def _():
                        remote(at, at, ag_s, ag_r.at[d, k], "ctx", target(d)).start()

                    remote(at, at, sb_s, sb_r.at[d, k], "ctx", sib).start()
            for d in range(2):
                ch = chip_of(d, k)
                if buf is not None:
                    at = block(buf, d, ch, other)
                    remote(at, at, sb_s, sb_r.at[d, k], "ctx", sib).wait_recv()
                PB[d, slot] = make(d, ch)
                SS[d, k] = PB[d, slot, pl.ds(other, BLK)].astype(BF16)
                remote(SS.at[d, k], SR.at[d, k], ss_s, ss_r.at[d, k], "ctx", sib).start()

        def sums(d, k):
            at = SR.at[d, k]
            remote(at, at, ss_s, ss_r.at[d, k], "ctx", sib).wait_recv()

        def arrived(d, q, k):
            got = RR.at[d, k, rows_of(q)]
            remote(got, got, rs_s, rs_r.at[d, k * RQS + q], "ctx", sib).wait_recv()

        def rows_of(q):
            return pl.ds(q * ROWS, ROWS if p < 2 or q < RQS - 1 else ROWS + 16)

        def second(k):
            slot = lax.rem(k, 2)
            for d in range(2):
                sums(d, k)
            for q in range(RQS):
                for d in range(2):
                    part = pl.ds(q * ROWS, ROWS)
                    total = PB[d, slot, pl.ds(pl.multiple_of(core * BLK + q * ROWS, ROWS), ROWS)] + SR[d, k, part].astype(F32)
                    rider = p == 2 and q == RQS - 1
                    if rider:
                        ride = riders(d, chip_of(d, k))

                    @pl.when(k > 1)
                    def _():
                        arrived(d, q, k - 1)
                        RSD[d, k, part] = (total + RR[d, k - 1, part].astype(F32)).astype(BF16)
                        if rider:
                            RSD[d, k, BLK : BLK + 16] = (ride + RR[d, k - 1, BLK : BLK + 16].astype(F32)).astype(BF16)

                    @pl.when(k == 1)
                    def _():
                        RSD[d, k, part] = total.astype(BF16)
                        if rider:
                            RSD[d, k, BLK : BLK + 16] = ride.astype(BF16)

                    remote(
                        RSD.at[d, k, rows_of(q)], RR.at[d, k, rows_of(q)], rs_s, rs_r.at[d, k * RQS + q],
                        "ctx", target(d),
                    ).start()

        @pl.loop(0, 9)
        def _(it):
            @pl.when(it < 8)
            def _():
                first(it)

            @pl.when(it > 1)
            def _():
                second(it - 1)

            extra(it)

        for d in range(2):
            sums(d, 0)
            for q in range(RQS):
                arrived(d, q, 7)
            finish(d, PB[d, 2, pl.ds(mine, BLK)] + SR[d, 0].astype(F32) + RR[d, 7, 0:BLK].astype(F32))

        if buf is not None:
            remote(buf.at[0, 0:7], buf.at[0, 0:7], ag_s, sbx_r, "ctx", sib).wait_send()
            remote(buf.at[0], buf.at[0], sb_s, sbx_r, "ctx", sib).wait_send()
        remote(SS, SS, ss_s, sbx_r, "ctx", sib).wait_send()
        sent = SS.at[:, 0:7] if p < 2 else RSD.at[:, 0:7]
        remote(sent, sent, rs_s, sbx_r, "ctx", sib).wait_send()

    def nothing(it):
        pass

    def up_w():
        return WU[...].reshape(D, UNITS)

    def down_w():
        return WD[...].reshape(UNITS, D)

    def make_up(m, ch):
        u = nn(HF[m, ch], up_w()) + UB[0:1, :]
        phi = 0.5 * (1.0 + lax.erf(u * 0.7071067811865476))
        a = (u * phi).astype(BF16)
        DG[m, ch] = phi + u * (jnp.exp(-0.5 * u * u) * 0.3989422804014327)
        ACT[m, ch] = a
        return nn(a, down_w())

    def finish_up(d, total):
        rows = slice(d * BLK, (d + 1) * BLK)
        SEC[rows, :] = H1[rows, :] + total + VF[3:4, :]

    ring(0, HF, make_up, nothing, finish_up)

    resid = SEC[...]
    center = resid - row_mean(resid)
    root = lax.rsqrt(row_mean(center * center) + 1e-05)
    z = center * root
    out_ref[...] = (z * VF[6:7, :] + VF[7:8, :]).astype(BF16).reshape(2, BLK, D)
    cot = ct_ref[...].reshape(128, D).astype(F32)
    SG[...] = jnp.zeros((8, D), F32)
    SG[4:5, :] = col_sum(cot * z)
    SG[5:6, :] = col_sum(cot)
    u = cot * VF[6:7, :]
    grad = (u - row_mean(u) - z * row_mean(u * z)) * root
    G2[...] = grad
    grad_low = grad.astype(BF16)
    SG[1:2, :] = col_sum(grad_low.astype(F32))
    for m in range(2):
        BG[m, chip, pl.ds(mine, BLK)] = grad_low[m * BLK : (m + 1) * BLK]

    def make_down(m, ch):
        pg = (nt(BG[m, ch], down_w()) * DG[m, ch]).astype(BF16)
        PG[m, ch] = pg
        return nt(pg, up_w())

    def finish_down(d, total):
        rows = slice(d * BLK, (d + 1) * BLK)
        SEC[rows, :] = G2[rows, :] + total

    def ff_grads():
        TT[...] = ACT[...].reshape(2048, UNITS).T
        for n in range(4):
            g = nn(TT[...], BG[:, :, :, CHUNK * n : CHUNK * (n + 1)].reshape(2048, CHUNK))
            GD[:, :, CHUNK * n : CHUNK * (n + 1)] = g.reshape(2, 128, CHUNK)
        XSD[...] = GD[1 - f].astype(BF16)
        pair(7, XSD, XRD).start()
        ones = jnp.ones((8, 2048), BF16)
        SG[6:7, 0:256] = nn(ones, PG[...].reshape(2048, UNITS))[0:1, :]
        TT[...] = PG[...].reshape(2048, UNITS).T
        for n in range(4):
            g = nn(TT[...], HF[:, :, :, CHUNK * n : CHUNK * (n + 1)].reshape(2048, CHUNK))
            GU[4 * n : 4 * n + 4] = g.T.reshape(4, 2, 32, UNITS)
        XSU[...] = GU[:, 1 - f].astype(BF16)
        pair(6, XSU, XRU).start()

    ring(1, BG, make_down, lambda it: pl.when(it == 8)(ff_grads), finish_down)

    hid = SEC[...]
    z = Z1[...]
    SG[2:3, :] = col_sum(hid * z)
    SG[3:4, :] = col_sum(hid)
    u = hid * VF[4:5, :]
    grad = (u - row_mean(u) - z * row_mean(u * z)) * R1[:, 0:1]
    H1[...] = grad
    proj = grad.astype(BF16)
    SG[0:1, :] = col_sum(proj.astype(F32))
    sent_all(2, ATS.at[0:15])
    ATS[...] = nt(WO[...].reshape(D, D), proj).astype(BF16).reshape(NCTX, HEAD, 128)
    AGT[c] = ATS[c]
    send_all(3, lambda to: ATS.at[to], AGT.at[c])

    for j in range(NCHIP):
        SSO[j] = nn(AT[2 * j + 1 - core], proj).astype(BF16)
    remote(SSO, SRO, po_s, po_r, "ctx", sib).start()
    pair(4, SG, SGR).start()
    for j in range(NCHIP):
        GO[j] = nn(AT[2 * j + core], proj)
    remote(SRO, SRO, po_s, po_r, "ctx", sib).wait_recv()
    for j in range(NCHIP):
        GO[j] = GO[j] + SRO[j].astype(F32)
        XSO[j] = GO[j, pl.ds(pl.multiple_of((1 - f) * 32, 32), 32)].astype(BF16)
    pair(5, XSO, XRO).start()
    recv_all(3, AGT.at[0:15])
    sent_all(3, ATS.at[0:15])

    for j in range(8):
        t0 = AGT[2 * j].astype(F32)
        t1 = AGT[2 * j + 1].astype(F32)
        AGQ[0, :, 128 * j : 128 * j + 128] = jnp.where(low_half, t0, pltpu.roll(t1, 64, 1)).astype(BF16)
        AGQ[1, :, 128 * j : 128 * j + 128] = jnp.where(low_half, pltpu.roll(t0, 64, 1), t1).astype(BF16)

    DK[...] = jnp.zeros((2, HEAD, D), F32)
    DV[...] = jnp.zeros((2, HEAD, D), F32)

    def small_push():
        pair(4, SGR, SGR).wait_recv()
        SGT[...] = SG[...] + SGR[...]
        SGC[c] = SGT[:, pl.ds(pl.multiple_of(chip * 128, 128), 128)]
        send_all(4, lambda to: SGT.at[:, pl.ds(pl.multiple_of(lax.div(to, 2) * 128, 128), 128)], SGC.at[c])

    def up_push():
        pair(6, XRU, XRU).wait_recv()
        AU[...] = (GU[:, f] + XRU[...].astype(F32)).astype(BF16)
        RU[c] = AU[c]
        send_all(5, lambda to: AU.at[to], RU.at[c])

    @pl.loop(0, 8)
    def _(it):
        pl.when(it == 2)(small_push)
        pl.when(it == 4)(up_push)
        m = lax.div(it, 4)
        n = lax.rem(it, 4)
        q = QT[m, :, lanes(n)]
        g = AGQ[m, :, lanes(n)]
        delta = jnp.sum(g.astype(F32) * ATD[m, :, lanes(n)], axis=0, keepdims=True)
        p = PT[m, :, lanes(n)]
        ds = (p.astype(F32) * (nn(VN[m], g) - delta)).astype(BF16)
        DK[m] = DK[m] + nt(q, ds)
        DV[m] = DV[m] + nt(g, p)
        dq = nn(KT[m], ds) * 0.125
        JG[m, 0:64, lanes(n)] = unturn(dq, rope_ref[0, :, lanes(n)], rope_ref[1, :, lanes(n)]).astype(BF16)

    for m in range(2):
        JG[m, 64:128, :] = unturn(DK[m] * 0.125, rope_ref[0], rope_ref[1]).astype(BF16)
        JG[m, 128:192, :] = DV[m].astype(BF16)

    def make_token(m, ch):
        jg = JG[m, :, pl.ds(pl.multiple_of(ch * 128, 128), 128)]
        return tn(jg, WHT[0:192, :])

    def finish_token(d, total):
        tg_ref[d] = H1[d * BLK : (d + 1) * BLK, :] + total
        go_ref[16 * d : 16 * d + 16, :] = riders(d, chip) + RR[d, 7, BLK : BLK + 16].astype(F32)

    def qkv_grad():
        for n in range(4):
            cols = slice(CHUNK * n, CHUNK * (n + 1))
            g = nn(JG[0], XF[0, :, :, cols].reshape(D, CHUNK)) + nn(JG[1], XF[1, :, :, cols].reshape(D, CHUNK))
            g = jnp.concatenate([g, jnp.zeros((64, CHUNK), F32)], axis=0)
            GU[4 * n : 4 * n + 4] = g.T.reshape(4, 2, 32, UNITS)
        XSQ[...] = GU[:, 1 - f].astype(BF16)
        pair(8, XSQ, XRQ).start()
        ones8 = jnp.ones((8, D), BF16)
        b = nt(ones8, JG[0]) + nt(ones8, JG[1])
        QB1[...] = jnp.concatenate([b, jnp.zeros((8, 64), F32)], axis=1)
        pair(9, QB1, QB2).start()

    def qkv_push():
        pair(8, XRQ, XRQ).wait_recv()
        AQ[...] = (GU[:, f] + XRQ[...].astype(F32)).astype(BF16)
        RQ[c] = AQ[c]
        send_all(6, lambda to: AQ.at[to], RQ.at[c])
        pair(9, QB2, QB2).wait_recv()
        pair(9, QB1, QB1).wait_send()
        QB1[...] = QB1[...] + QB2[...]
        QB3[c] = QB1[...]
        send_all(7, lambda to: QB1, QB3.at[c])

    def riders(d, ch):
        return GO[ch, pl.ds(pl.multiple_of(f * 32 + 16 * d, 16), 16)] + XRO[ch, 16 * d : 16 * d + 16].astype(F32)

    def small_rest():
        recv_all(4, SGC.at[0:15])
        total = SGC[0]
        for w in range(1, NCTX):
            total = total + SGC[w]
        gs_ref[...] = total
        gs_ref[6:7, :] = SGT[6:7, pl.ds(pl.multiple_of(f * 128, 128), 128)]
        pair(7, XRD, XRD).wait_recv()
        gd_ref[...] = GD[f] + XRD[...].astype(F32)

    def up_rest():
        recv_all(5, RU.at[0:15])
        for w in range(NCTX):
            gu_ref[:, UNITS * w : UNITS * (w + 1)] = RU[w].astype(F32)

    def on_the_way(it):
        pl.when(it == 1)(qkv_grad)
        pl.when(it == 3)(small_rest)
        pl.when(it == 4)(qkv_push)
        pl.when(it == 6)(up_rest)

    pair(5, XRO, XRO).wait_recv()
    ring(2, None, make_token, on_the_way, finish_token)

    recv_all(6, RQ.at[0:15])
    for j in range(8):
        a = RQ[2 * j].astype(F32)
        b = RQ[2 * j + 1].astype(F32)
        cols = slice(128 * j, 128 * (j + 1))
        gq_ref[:, cols] = jnp.where(low_half, a[:, 0:128], pltpu.roll(b[:, 0:128], 64, 1))
        gq_ref[:, D + 128 * j : D + 128 * (j + 1)] = jnp.where(low_half, pltpu.roll(a[:, 0:128], 64, 1), b[:, 0:128])
        gq_ref[:, 2 * D + 128 * j : 2 * D + 128 * (j + 1)] = jnp.where(low_half, a[:, 128:256], pltpu.roll(b[:, 128:256], 64, 1))
    recv_all(7, QB3.at[0:15])
    for j in range(8):
        a = QB3[2 * j]
        b = QB3[2 * j + 1]
        rows = (
            jnp.where(low_half, a[:, 0:128], pltpu.roll(b[:, 0:128], 64, 1)),
            jnp.where(low_half, pltpu.roll(a[:, 0:128], 64, 1), b[:, 0:128]),
            jnp.where(low_half, a[:, 128:256], pltpu.roll(b[:, 128:256], 64, 1)),
        )
        for i in range(3):
            gb_ref[8 * i + j : 8 * i + j + 1, :] = rows[i][0:1, :]

    remote(XF.at[0, 0:7], XF.at[0, 0:7], agx_s, sbx_r, "ctx", sib).wait_send()
    remote(XF.at[0], XF.at[0], sbx_s, sbx_r, "ctx", sib).wait_send()
    remote(WO.at[0:7], WO.at[0:7], wo_s, sbx_r, "ctx", sib).wait_send()
    remote(WO.at[0:8], WO.at[0:8], wos_s, sbx_r, "ctx", sib).wait_send()
    sent_all(0, WP.at[0:15])
    sent_all(1, VB.at[0:15])
    sent_all(4, SGC.at[0:15])
    sent_all(5, AU.at[0:15])
    sent_all(6, AQ.at[0:15])
    sent_all(7, QB3.at[0:15])
    remote(SSO, SSO, po_s, po_r, "ctx", sib).wait_send()
    sent_all(8, WU.at[0:15, 0])
    for i, at in enumerate((VEC, wo_ref, wd_ref, WB.at[:, f], SG, XSO, XSU, XSD, XSQ)):
        pair(i, at, at).wait_send()
    pair(10, WU.at[:, f], WU.at[:, f]).wait_send()


def rope_tables():
    freqs = (np.float32(10000.0) ** (-np.arange(0, HEAD, 2, dtype=np.float32) / np.float32(HEAD))).astype(np.float32)
    angles = freqs[:, None] * np.arange(1024, dtype=np.float32)[None, :]
    return np.stack([np.cos(angles), np.sin(angles)]).astype(np.float32)


def fused_body(
    tokens, cotangent, qkv_weight, out_weight, up_weight, down_weight, qkv_bias, out_bias, up_bias, down_bias,
    first_gain, first_shift, second_gain, second_shift,
):
    scratch = [
        ((8, 128), F32),
        ((2, 8, 128, D), BF16), ((2, 8, 128, D), BF16), ((2, 8, 128, D), BF16),
        ((16, 32, 256), BF16), ((16, 2, 32, 256), BF16), ((16, 2, 32, UNITS), BF16), ((16, 2, 32, D), BF16), ((2, 128, D), BF16),
        ((16, 2, 8, 128), F32), ((8, D), F32), ((8, UNITS), F32), ((24, 128), F32), ((3, 128, 128), F32),
        ((256, D), BF16),
        ((2, 64, D), BF16), ((2, 64, D), BF16), ((2, 64, D), BF16), ((2, D, 64), BF16), ((2, D, 64), BF16),
        ((2, D, D), BF16), ((2, 64, D), F32),
        ((16, 64, 128), BF16), ((16, 64, 128), BF16), ((16, 64, 128), BF16),
        ((128, D), F32), ((128, D), F32), ((128, 128), F32), ((128, D), F32), ((128, D), F32),
        ((2, 8, 128, UNITS), F32), ((2, 8, 128, UNITS), BF16), ((2, 8, 128, UNITS), BF16),
        ((2, 3, 128, D), F32),
        ((2, 8, BLK, D), BF16), ((2, 8, BLK, D), BF16), ((2, 8, 80, D), BF16), ((2, 8, 80, D), BF16),
        ((UNITS, 2048), BF16),
        ((16, 2, 32, UNITS), F32), ((16, 32, UNITS), BF16), ((16, 32, UNITS), BF16), ((16, 32, UNITS), BF16), ((16, 32, UNITS), BF16),
        ((2, 128, D), F32), ((128, D), BF16), ((128, D), BF16),
        ((8, BLK, D), F32), ((8, 32, D), BF16), ((8, 32, D), BF16), ((8, BLK, D), BF16), ((8, BLK, D), BF16),
        ((8, D), F32), ((8, D), F32), ((8, D), F32), ((16, 8, 128), F32), ((2, 64, D), BF16),
        ((2, 64, D), F32), ((2, 64, D), F32), ((2, 192, D), BF16),
        ((16, 32, UNITS), BF16), ((16, 32, UNITS), BF16), ((16, 32, UNITS), BF16), ((16, 32, UNITS), BF16),
        ((8, 256), F32), ((8, 256), F32), ((16, 8, 256), F32),
    ]
    sems = [(12,), (2, 8 * AQS), (2, 8), (2, 8), (2, 8 * RQS), (2, 8), (9,), (9,), (11,), (11,)]
    vmem = pl.BlockSpec(memory_space=pltpu.VMEM)
    shapes = [((2, BLK, D), BF16), ((2, BLK, D), F32), ((32, 3 * D), F32), ((32, D), F32), ((32, 4 * D), F32), ((128, D), F32), ((8, 128), F32), ((24, 128), F32)]
    bias = (up_bias, qkv_bias, out_bias, down_bias, first_gain, first_shift, second_gain, second_shift)
    made = pl.pallas_call(
        layer_kernel,
        out_shape=[jax.ShapeDtypeStruct(s, t) for s, t in shapes],
        in_specs=[vmem] * 15,
        out_specs=[vmem] * 8,
        scratch_shapes=[pltpu.VMEM(s, t) for s, t in scratch] + [pltpu.SemaphoreType.DMA(s) for s in sems],
        compiler_params=pltpu.CompilerParams(collective_id=0, has_side_effects=True, vmem_limit_bytes=VMEM_LIMIT),
        name="layer",
    )(
        tokens[:, 0], cotangent[:, 0], qkv_weight, out_weight, up_weight, down_weight, jnp.asarray(rope_tables()),
        *(v[None] for v in bias),
    )
    anywhere = pl.BlockSpec(memory_space=pl.ANY)
    widths = (96, 32, 128, 32, 32, 32, 32, 32)
    last = pl.pallas_call(
        finish_kernel,
        out_shape=[jax.ShapeDtypeStruct(s, t) for s, t in shapes[:6]] + [jax.ShapeDtypeStruct((1, w), F32) for w in widths],
        in_specs=[anywhere] * 6 + [vmem] * 2,
        out_specs=[vmem] * 14,
        scratch_shapes=[pltpu.SemaphoreType.DMA((6,))],
        name="finish",
    )(*made)
    return (last[0][:, None], last[1][:, None], *last[2:6], *(v[0] for v in last[6:]))


def finish_kernel(*refs):
    big, (gs, gb), done, small, sems = refs[:6], refs[6:8], refs[8:14], refs[14:22], refs[22]
    copies = [pltpu.make_async_copy(a, b, sems.at[i]) for i, (a, b) in enumerate(zip(big, done))]
    for copy in copies:
        copy.start()
    index = lax.axis_index("ctx") * 2 + lax.axis_index("fsdp")
    place = lax.rem(index, 4)
    turned = pltpu.roll(gs[...], lax.rem(128 - 32 * place, 128), 1)
    for ref, row in zip(small[1:], (0, 6, 1, 2, 3, 4, 5)):
        ref[...] = gs[6:7, :] if row == 6 else turned[row : row + 1, 0:32]
    offset = lax.rem(96 * index, 128)
    row = lax.div(96 * index, 128)
    lane = lax.broadcasted_iota(jnp.int32, (1, 128), 1)
    back = lax.rem(128 - offset, 128)
    one = pltpu.roll(gb[pl.ds(row, 1), :], back, 1)
    two = pltpu.roll(gb[pl.ds(lax.rem(row + 1, 24), 1), :], back, 1)
    small[0][...] = jnp.where(lane < 128 - offset, one, two)[:, 0:96]
    for copy in copies:
        copy.wait()


VMEM_LIMIT = 63 * 1024 * 1024


def layernorm(resid, gain, shift):
    center = resid - jnp.mean(resid, axis=-1, keepdims=True)
    spread = jnp.mean(center * center, axis=-1, keepdims=True)
    return center * lax.rsqrt(spread + 1e-05) * gain + shift


def tables(position):
    freqs = 10000.0 ** (-jnp.arange(0, HEAD, 2, dtype=jnp.float32) / HEAD)
    angles = position[:, None] * freqs[None, :]
    return (jnp.cos(angles)[:, None, :], jnp.sin(angles)[:, None, :])


def rotate(heads_in, cosine, sine):
    middle = heads_in.shape[-1] // 2
    first = heads_in[..., :middle]
    second = heads_in[..., middle:]
    return jnp.concatenate(
        [first * cosine - second * sine, second * cosine + first * sine], axis=-1
    )


def unrotate(heads_in, cosine, sine):
    middle = heads_in.shape[-1] // 2
    first = heads_in[..., :middle]
    second = heads_in[..., middle:]
    return jnp.concatenate(
        [first * cosine + second * sine, second * cosine - first * sine], axis=-1
    )


def split_heads(flat_rows):
    return flat_rows.reshape(flat_rows.shape[0], HEADS, HEAD)


def over_blocks(update, carried, count, limit):
    size = math.gcd(count, limit)

    def advance(block_idx, state):
        return update(state, block_idx * size, size)

    return lax.fori_loop(0, count // size, advance, carried)


def column_sum(matrix):
    return jnp.sum(matrix.astype(jnp.float32), axis=0)


def forward_local(sequence, weights_now, cosine, sine, group):
    (
        qkv_full,
        out_full,
        up_full,
        down_full,
        qkv_vector,
        out_vector,
        up_vector,
        down_vector,
        gain_first,
        shift_first,
        gain_second,
        shift_second,
    ) = weights_now
    rows = sequence.shape[0]
    width = sequence.shape[1]
    joined = jnp.dot(sequence, qkv_full, preferred_element_type=jnp.float32) + qkv_vector.astype(
        jnp.float32
    )
    query_flat = (
        rotate(split_heads(joined[:, :width]), cosine, sine)
        .astype(jnp.bfloat16)
        .reshape(rows, width)
    )
    keys_flat = (
        rotate(split_heads(joined[:, width : 2 * width]), cosine, sine)
        .astype(jnp.bfloat16)
        .reshape(rows, width)
    )
    values_flat = joined[:, 2 * width :].astype(jnp.bfloat16)
    query_heads = split_heads(query_flat)
    start_state = (
        jnp.full((HEADS, rows), -1e30, jnp.float32),
        jnp.zeros((HEADS, rows), jnp.float32),
        jnp.zeros((rows, HEADS, HEAD), jnp.float32),
    )
    keys_piece = lax.all_gather(keys_flat, "ctx", axis=0, tiled=True)
    values_piece = lax.all_gather(values_flat, "ctx", axis=0, tiled=True)

    def absorb_block(state, offset, size):
        running, total, accum = state
        key_block = split_heads(lax.dynamic_slice_in_dim(keys_piece, offset, size, 0))
        value_block = split_heads(lax.dynamic_slice_in_dim(values_piece, offset, size, 0))
        scores = (
            jnp.einsum("qhd,khd->hqk", query_heads, key_block, preferred_element_type=jnp.float32)
            * 0.125
        )
        highest_new = jnp.maximum(running, jnp.max(scores, axis=-1))
        factor = jnp.exp(running - highest_new)
        expo = jnp.exp(scores - highest_new[:, :, None])
        total = total * factor + jnp.sum(expo, axis=-1)
        accum = accum * factor.T[:, :, None] + jnp.einsum(
            "hqk,khd->qhd",
            expo.astype(jnp.bfloat16),
            value_block,
            preferred_element_type=jnp.float32,
        )
        return (highest_new, total, accum)

    running, total, accum = over_blocks(absorb_block, start_state, keys_piece.shape[0], group)
    attended = accum / total.T[:, :, None]
    logsum = running + jnp.log(total)
    att_low = attended.reshape(rows, width).astype(jnp.bfloat16)
    projected = jnp.dot(att_low, out_full, preferred_element_type=jnp.float32) + out_vector.astype(
        jnp.float32
    )
    resid_first = sequence.astype(jnp.float32) + projected
    hidden = layernorm(resid_first, gain_first.astype(jnp.float32), shift_first.astype(jnp.float32))
    hidden_low = hidden.astype(jnp.bfloat16)
    preact = jnp.dot(hidden_low, up_full, preferred_element_type=jnp.float32) + up_vector.astype(
        jnp.float32
    )
    activ_low = jax.nn.gelu(preact, approximate=False).astype(jnp.bfloat16)
    branch = jnp.dot(activ_low, down_full, preferred_element_type=jnp.float32) + down_vector.astype(
        jnp.float32
    )
    resid_second = hidden + branch
    output = layernorm(
        resid_second, gain_second.astype(jnp.float32), shift_second.astype(jnp.float32)
    )
    saved = (
        query_flat,
        keys_flat,
        values_flat,
        attended,
        logsum,
        att_low,
        resid_first,
        hidden_low,
        preact,
        activ_low,
        resid_second,
    )
    return (output.astype(jnp.bfloat16), saved)


def body(
    tokens,
    cotangent,
    qkv_weight,
    out_weight,
    up_weight,
    down_weight,
    qkv_bias,
    out_bias,
    up_bias,
    down_bias,
    first_gain,
    first_shift,
    second_gain,
    second_shift,
):
    gathered = (
        lax.all_gather(qkv_weight, ("ctx", "fsdp"), axis=0, tiled=True),
        lax.all_gather(out_weight, ("ctx", "fsdp"), axis=0, tiled=True),
        lax.all_gather(up_weight, ("ctx", "fsdp"), axis=0, tiled=True),
        lax.all_gather(down_weight, ("ctx", "fsdp"), axis=0, tiled=True),
        lax.all_gather(qkv_bias, ("ctx", "fsdp"), axis=0, tiled=True),
        lax.all_gather(out_bias, ("ctx", "fsdp"), axis=0, tiled=True),
        lax.all_gather(up_bias, ("ctx", "fsdp"), axis=0, tiled=True),
        lax.all_gather(down_bias, ("ctx", "fsdp"), axis=0, tiled=True),
        lax.all_gather(first_gain, ("ctx", "fsdp"), axis=0, tiled=True),
        lax.all_gather(first_shift, ("ctx", "fsdp"), axis=0, tiled=True),
        lax.all_gather(second_gain, ("ctx", "fsdp"), axis=0, tiled=True),
        lax.all_gather(second_shift, ("ctx", "fsdp"), axis=0, tiled=True),
    )
    rows = tokens.shape[2]
    width = tokens.shape[3]
    cycle_size = lax.axis_size("ctx")
    group = rows * math.gcd(cycle_size, 8)
    length = rows * cycle_size
    position = (lax.axis_index("ctx") * rows + jnp.arange(rows)).astype(jnp.float32)
    cosine, sine = tables(position)
    outputs = []
    savings = []
    for micro_idx in range(MICRO):
        output, saved = forward_local(tokens[micro_idx, 0], gathered, cosine, sine, group)
        outputs.append(output)
        savings.append(saved)
    weights_back = (
        lax.all_gather(qkv_weight, ("ctx", "fsdp"), axis=0, tiled=True),
        lax.all_gather(out_weight, ("ctx", "fsdp"), axis=0, tiled=True),
        lax.all_gather(up_weight, ("ctx", "fsdp"), axis=0, tiled=True),
        lax.all_gather(down_weight, ("ctx", "fsdp"), axis=0, tiled=True),
        lax.all_gather(qkv_bias, ("ctx", "fsdp"), axis=0, tiled=True),
        lax.all_gather(out_bias, ("ctx", "fsdp"), axis=0, tiled=True),
        lax.all_gather(up_bias, ("ctx", "fsdp"), axis=0, tiled=True),
        lax.all_gather(down_bias, ("ctx", "fsdp"), axis=0, tiled=True),
        lax.all_gather(first_gain, ("ctx", "fsdp"), axis=0, tiled=True),
        lax.all_gather(first_shift, ("ctx", "fsdp"), axis=0, tiled=True),
        lax.all_gather(second_gain, ("ctx", "fsdp"), axis=0, tiled=True),
        lax.all_gather(second_shift, ("ctx", "fsdp"), axis=0, tiled=True),
    )
    (
        qkv_full,
        out_full,
        up_full,
        down_full,
        qkv_vector,
        out_vector,
        up_vector,
        down_vector,
        gain_first,
        shift_first,
        gain_second,
        shift_second,
    ) = weights_back
    token_grads = []
    totals = []
    for micro_idx in range(MICRO):
        (
            query_flat,
            keys_flat,
            values_flat,
            attended,
            logsum,
            att_low,
            resid_first,
            hidden_low,
            preact,
            activ_low,
            resid_second,
        ) = savings[micro_idx]
        sequence = tokens[micro_idx, 0]
        grad_out = cotangent[micro_idx, 0].astype(jnp.float32)
        unused_two, second_back = jax.vjp(
            layernorm,
            resid_second,
            gain_second.astype(jnp.float32),
            shift_second.astype(jnp.float32),
        )
        grad_second, second_gain_grad, second_shift_grad = second_back(grad_out)
        branch_grad = grad_second.astype(jnp.bfloat16)
        down_bias_grad = column_sum(branch_grad)
        down_weight_grad = jnp.einsum(
            "tf,td->fd", activ_low, branch_grad, preferred_element_type=jnp.float32
        )
        activ_grad = jnp.einsum(
            "td,fd->tf", branch_grad, down_full, preferred_element_type=jnp.float32
        )
        unused_gelu, gelu_back = jax.vjp(partial(jax.nn.gelu, approximate=False), preact)
        preact_grad = gelu_back(activ_grad)[0].astype(jnp.bfloat16)
        up_bias_grad = column_sum(preact_grad)
        up_weight_grad = jnp.einsum(
            "td,tf->df", hidden_low, preact_grad, preferred_element_type=jnp.float32
        )
        hidden_grad = grad_second + jnp.einsum(
            "tf,df->td", preact_grad, up_full, preferred_element_type=jnp.float32
        )
        unused_one, first_back = jax.vjp(
            layernorm, resid_first, gain_first.astype(jnp.float32), shift_first.astype(jnp.float32)
        )
        grad_first, first_gain_grad, first_shift_grad = first_back(hidden_grad)
        proj_grad = grad_first.astype(jnp.bfloat16)
        out_bias_grad = column_sum(proj_grad)
        out_weight_grad = jnp.einsum(
            "tc,te->ce", att_low, proj_grad, preferred_element_type=jnp.float32
        )
        att_grad = jnp.einsum(
            "te,ce->tc", proj_grad, out_full, preferred_element_type=jnp.float32
        ).astype(jnp.bfloat16)
        att_heads = split_heads(att_grad)
        query_heads = split_heads(query_flat)
        delta = jnp.sum(att_heads.astype(jnp.float32) * attended, axis=-1).T
        key_all, value_all = (
            lax.all_gather(keys_flat, "ctx", axis=0, tiled=True),
            lax.all_gather(values_flat, "ctx", axis=0, tiled=True),
        )

        def query_update(state, offset, size):
            key_block = split_heads(lax.dynamic_slice_in_dim(key_all, offset, size, 0))
            value_block = split_heads(lax.dynamic_slice_in_dim(value_all, offset, size, 0))
            scores = (
                jnp.einsum(
                    "qhd,khd->hqk", query_heads, key_block, preferred_element_type=jnp.float32
                )
                * 0.125
            )
            chance = jnp.exp(scores - logsum[:, :, None])
            dprob = jnp.einsum(
                "qhd,khd->hqk", att_heads, value_block, preferred_element_type=jnp.float32
            )
            score_grad = (chance * (dprob - delta[:, :, None])).astype(jnp.bfloat16)
            return state + jnp.einsum(
                "hqk,khd->qhd", score_grad, key_block, preferred_element_type=jnp.float32
            )

        query_grad = (
            over_blocks(query_update, jnp.zeros((rows, HEADS, HEAD), jnp.float32), length, group)
            * 0.125
        )

        def fill(state, offset, size):
            key_block = split_heads(lax.dynamic_slice_in_dim(key_all, offset, size, 0))
            value_block = split_heads(lax.dynamic_slice_in_dim(value_all, offset, size, 0))
            scores = (
                jnp.einsum(
                    "qhd,khd->hqk", query_heads, key_block, preferred_element_type=jnp.float32
                )
                * 0.125
            )
            chance = jnp.exp(scores - logsum[:, :, None])
            value_part = jnp.einsum(
                "hqk,qhd->khd",
                chance.astype(jnp.bfloat16),
                att_heads,
                preferred_element_type=jnp.float32,
            )
            dprob = jnp.einsum(
                "qhd,khd->hqk", att_heads, value_block, preferred_element_type=jnp.float32
            )
            score_grad = (chance * (dprob - delta[:, :, None])).astype(jnp.bfloat16)
            key_part = (
                jnp.einsum(
                    "hqk,qhd->khd", score_grad, query_heads, preferred_element_type=jnp.float32
                )
                * 0.125
            )
            piece = jnp.concatenate(
                [key_part.reshape(size, width), value_part.reshape(size, width)], axis=1
            )
            return lax.dynamic_update_slice_in_dim(state, piece, offset, 0)

        combined = lax.psum_scatter(
            over_blocks(
                fill,
                jnp.zeros((lax.axis_size("ctx") * rows, 2 * width), jnp.float32),
                lax.axis_size("ctx") * rows,
                group,
            ),
            "ctx",
            scatter_dimension=0,
            tiled=True,
        )
        key_grad = split_heads(combined[:, :width])
        value_grad = combined[:, width:]
        joined_grad = jnp.concatenate(
            [
                unrotate(query_grad, cosine, sine).reshape(rows, width),
                unrotate(key_grad, cosine, sine).reshape(rows, width),
                value_grad,
            ],
            axis=1,
        ).astype(jnp.bfloat16)
        qkv_bias_grad = column_sum(joined_grad)
        qkv_weight_grad = jnp.einsum(
            "tc,te->ce", sequence, joined_grad, preferred_element_type=jnp.float32
        )
        token_grads.append(
            grad_first
            + jnp.einsum("te,ce->tc", joined_grad, qkv_full, preferred_element_type=jnp.float32)
        )
        fresh = [
            qkv_weight_grad,
            out_weight_grad,
            up_weight_grad,
            down_weight_grad,
            qkv_bias_grad,
            out_bias_grad,
            up_bias_grad,
            down_bias_grad,
            first_gain_grad,
            first_shift_grad,
            second_gain_grad,
            second_shift_grad,
        ]
        if micro_idx == 0:
            totals = fresh
        else:
            totals = [older + newer for older, newer in zip(totals, fresh)]
    summed = (
        lax.psum_scatter(totals[0], ("ctx", "fsdp"), scatter_dimension=0, tiled=True),
        lax.psum_scatter(totals[1], ("ctx", "fsdp"), scatter_dimension=0, tiled=True),
        lax.psum_scatter(totals[2], ("ctx", "fsdp"), scatter_dimension=0, tiled=True),
        lax.psum_scatter(totals[3], ("ctx", "fsdp"), scatter_dimension=0, tiled=True),
        lax.psum_scatter(totals[4], ("ctx", "fsdp"), scatter_dimension=0, tiled=True),
        lax.psum_scatter(totals[5], ("ctx", "fsdp"), scatter_dimension=0, tiled=True),
        lax.psum_scatter(totals[6], ("ctx", "fsdp"), scatter_dimension=0, tiled=True),
        lax.psum_scatter(totals[7], ("ctx", "fsdp"), scatter_dimension=0, tiled=True),
        lax.psum_scatter(totals[8], ("ctx", "fsdp"), scatter_dimension=0, tiled=True),
        lax.psum_scatter(totals[9], ("ctx", "fsdp"), scatter_dimension=0, tiled=True),
        lax.psum_scatter(totals[10], ("ctx", "fsdp"), scatter_dimension=0, tiled=True),
        lax.psum_scatter(totals[11], ("ctx", "fsdp"), scatter_dimension=0, tiled=True),
    )
    output_all = jnp.stack(outputs)[:, None]
    token_all = jnp.stack(token_grads)[:, None]
    return (
        output_all,
        token_all,
        summed[0],
        summed[1],
        summed[2],
        summed[3],
        summed[4],
        summed[5],
        summed[6],
        summed[7],
        summed[8],
        summed[9],
        summed[10],
        summed[11],
    )


def solution(mesh):
    in_specs = (
        P(None, "fsdp", "ctx", None),
        P(None, "fsdp", "ctx", None),
        P(("ctx", "fsdp"), None),
        P(("ctx", "fsdp"), None),
        P(("ctx", "fsdp"), None),
        P(("ctx", "fsdp"), None),
        P(("ctx", "fsdp")),
        P(("ctx", "fsdp")),
        P(("ctx", "fsdp")),
        P(("ctx", "fsdp")),
        P(("ctx", "fsdp")),
        P(("ctx", "fsdp")),
        P(("ctx", "fsdp")),
        P(("ctx", "fsdp")),
    )
    out_specs = (
        P(None, "fsdp", "ctx", None),
        P(None, "fsdp", "ctx", None),
        P(("ctx", "fsdp"), None),
        P(("ctx", "fsdp"), None),
        P(("ctx", "fsdp"), None),
        P(("ctx", "fsdp"), None),
        P(("ctx", "fsdp")),
        P(("ctx", "fsdp")),
        P(("ctx", "fsdp")),
        P(("ctx", "fsdp")),
        P(("ctx", "fsdp")),
        P(("ctx", "fsdp")),
        P(("ctx", "fsdp")),
        P(("ctx", "fsdp")),
    )
    fused = mesh.shape["ctx"] == NCTX and mesh.shape["fsdp"] == 2
    return jax.shard_map(fused_body if fused else body, mesh=mesh, in_specs=in_specs, out_specs=out_specs, check_vma=False)
```

```python
from functools import partial
import math

import jax
import jax.numpy as jnp
from jax import lax
from jax.experimental import pallas as pl
from jax.experimental.pallas import tpu as pltpu
from jax.sharding import PartitionSpec as P
import numpy as np

HEADS = 16
HEAD = 64
MICRO = 2
MESH = pl.DeviceIdType.MESH
F32 = jnp.float32
BF16 = jnp.bfloat16


NCTX = 16
NCHIP = 8
BLK = 64
D = 1024
UNITS = 256
FF_UNITS = 512
CHUNK = 256
AQS = 2
RQS = 4
ROWS = BLK // RQS


def chip_at(place):
    row = lax.div(place, 4)
    return ((1 - row) * place + row * (7 - place)) * 2 + row


def nn(a, b):
    return jnp.dot(a, b, preferred_element_type=F32)


def nt(a, b):
    return lax.dot_general(a, b, (((1,), (1,)), ((), ())), preferred_element_type=F32)


def tn(a, b):
    return lax.dot_general(a, b, (((0,), (0,)), ((), ())), preferred_element_type=F32)


def row_mean(v):
    return jnp.sum(v, axis=1, keepdims=True) * (1.0 / D)


def col_sum(v):
    return jnp.sum(v, axis=0, keepdims=True)


def layer_kernel(
    x_ref, ct_ref, wq_ref, wo_ref, wu_ref, wd_ref, rope_ref, v0, v1, v2, v3, v4, v5, v6, v7,
    out_ref, tg_ref, RQ, go_ref, RU, gd_ref, gs_ref,
    VEC, XF, HF, BG, WP, WB, WUS, WU, WO, WD, VB, VF, UB, QBR, BQ, WHT, QT, KT, VT, KN, VN, PT, ATD, ATS, AT, AGT,
    H1, Z1, R1, SEC, G2, DG, ACT, PG, PB, SS, SR, RSD, RR, TT,
    GU, PUS, DWU, DWD, ZRU, ZRD, GO, XSO, XRO, SSO, SRO, SG, SGR, SGT, SGC, AGQ,
    DK, DV, JG, XSQ, XRQ, AQ, QBP,
    one, ag_r, ss_r, rs_r, wo_r, all_s, all_r, pair_s, pair_r, plane_s, plane_r,
    pa_r, pb_r, ps_r, pr_r, z_s, z_r, q_s, q_r,
):
    c = lax.axis_index("ctx")
    f = lax.axis_index("fsdp")
    core = lax.rem(c, 2)
    chip = lax.div(c, 2)
    yy = lax.rem(chip, 2)
    zz = lax.div(chip, 2)
    r = (1 - yy) * zz + yy * (7 - zz)
    nxt = chip_at(lax.rem(r + 1, 8)) * 2 + core
    prv = chip_at(lax.rem(r + 7, 8)) * 2 + core
    sib = c + 1 - 2 * core
    mine = pl.multiple_of(core * BLK, BLK)
    other = pl.multiple_of((1 - core) * BLK, BLK)
    lane = lax.broadcasted_iota(jnp.int32, (1, 128), 1)
    low_half = lane < 64

    def remote(src, dst, ss, rs, axis, to):
        return pltpu.make_async_remote_copy(
            src_ref=src, dst_ref=dst, send_sem=ss, recv_sem=rs, device_id={axis: to}, device_id_type=MESH
        )

    def target(d):
        return nxt if d == 0 else prv

    def chip_of(d, k):
        return chip_at(lax.rem(r - k + 8, 8) if d == 0 else lax.rem(r + k, 8))

    def send_all(e, src_at, dst):
        @pl.loop(1, NCTX)
        def _(o):
            to = lax.rem(c + o, NCTX)
            remote(src_at(to), dst, all_s.at[e], all_r.at[e], "ctx", to).start()

    def recv_all(e, slab):
        remote(slab, slab, all_s.at[e], all_r.at[e], "ctx", sib).wait_recv()

    def sent_all(e, slab):
        remote(slab, slab, all_s.at[e], all_r.at[e], "ctx", sib).wait_send()

    pp = lax.rem(c, 4) * 2 + f
    grp = yy * 2 + f

    def send_plane(e, src_at, dst):
        @pl.loop(1, 8)
        def _(o):
            to = lax.rem(pp + o, 8)
            pltpu.make_async_remote_copy(
                src_ref=src_at(to), dst_ref=dst, send_sem=plane_s.at[e], recv_sem=plane_r.at[e],
                device_id={"ctx": zz * 4 + lax.div(to, 2), "fsdp": lax.rem(to, 2)}, device_id_type=MESH,
            ).start()

    def recv_plane(e, slab):
        remote(slab, slab, plane_s.at[e], plane_r.at[e], "ctx", sib).wait_recv()

    def sent_plane(e, slab):
        remote(slab, slab, plane_s.at[e], plane_r.at[e], "ctx", sib).wait_send()

    def at_plane(body):
        for place in range(4):

            @pl.when(zz == place)
            def _():
                body(place)

    def z_block(kd, b, dr, s, place):
        at = (WU, WD)[kd].at[b]
        return remote(at, at, z_s.at[kd, dr * 3 + s], z_r.at[kd, b], "ctx", c + (4 if dr == 0 else -4))

    def z_gather(kd, s, sent=False):
        def body(place):
            for dr in range(2):
                b = place - s if dr == 0 else place + s
                more = place < 3 if dr == 0 else place > 0
                if not 0 <= b < 4:
                    continue
                if s > 0 and not sent:
                    z_block(kd, b, dr, s - 1, place).wait_recv()
                if s < 3 and more:
                    copy = z_block(kd, b, dr, s, place)
                    copy.wait_send() if sent else copy.start()

        at_plane(body)

    def z_slot(source, t):
        return (source - t) % 4 - 1

    def z_term(kd, t, there, slot, place):
        src, got = ((DWU, ZRU), (DWD, ZRD))[kd]
        return remote(src.at[t], got.at[slot], q_s.at[kd, t], q_r.at[kd, slot], "ctx", c + 4 * (there - place))

    def z_start(kd, sent=False):
        def body(place):
            for t in (3, 2, 1, 0) if place < 2 else (0, 1, 2, 3):
                if t == place or (place, t) in ((1, 3), (2, 0)):
                    continue
                far = (place, t) in ((0, 3), (3, 0))
                there = (1 if place == 0 else 2) if far else t
                copy = z_term(kd, t, there, 3 if far else z_slot(place, t), place)
                copy.wait_send() if sent else copy.start()

        at_plane(body)

    def z_relay(kd, sent=False):
        def body(place):
            if place in (1, 2):
                t = 3 if place == 1 else 0
                src, got = ((DWU, ZRU), (DWD, ZRD))[kd]
                copy = z_term(kd, t, t, z_slot(place, t), place)
                if sent:
                    copy.wait_send()
                else:
                    z_term(kd, t, t, 3, place).wait_recv()
                    src[t] = (src[t].astype(F32) + got[3].astype(F32)).astype(BF16)
                    copy.start()

        at_plane(body)

    def z_total(kd, put):
        def body(place):
            src, got = ((DWU, ZRU), (DWD, ZRD))[kd]
            total = src[place].astype(F32)
            for source in range(4):
                if source != place and (source, place) not in ((0, 3), (3, 0)):
                    slot = z_slot(source, place)
                    z_term(kd, place, place, slot, place).wait_recv()
                    total = total + got[slot].astype(F32)
            put(total)

        at_plane(body)

    def pair(i, src, dst):
        return remote(src, dst, pair_s.at[i], pair_r.at[i], "fsdp", 1 - f)

    agx_s, sbx_s, sbx_r, ss_s, rs_s, wo_s, wos_s, wos_r, po_s, po_r, pa_s, pb_s, ps_s, pr_s = (one.at[i] for i in range(14))
    barrier = pltpu.get_barrier_semaphore()

    @pl.loop(1, NCTX)
    def _(o):
        pl.semaphore_signal(barrier, inc=1, device_id={"ctx": lax.rem(c + o, NCTX)}, device_id_type=MESH)

    @pl.loop(0, 4)
    def _(o):
        there = lax.div(c, 4) * 4 + lax.rem(c + o, 4)
        pl.semaphore_signal(barrier, inc=1, device_id={"ctx": there, "fsdp": 1 - f}, device_id_type=MESH)

    pl.semaphore_wait(barrier, NCTX + 3)

    def block(buf, m, ch, row0):
        return buf.at[m, ch, pl.ds(row0, BLK)]

    def sub(m, ch, q):
        return XF.at[m, ch, pl.ds(pl.multiple_of(core * BLK + (BLK // AQS) * q, BLK // AQS), BLK // AQS)]

    for m in range(2):
        XF[m, chip, pl.ds(mine, BLK)] = x_ref[m]
    WO[c, f] = wo_ref[...]
    WD[zz] = wd_ref[...]
    VEC[...] = jnp.zeros((8, 128), F32)
    for i, v in enumerate((v0, v1, v2, v3, v4, v5, v6, v7)):
        VEC[i : i + 1, 0 : v.shape[1]] = v[...].astype(F32)
    VB[c, f] = VEC[...]

    def gather_x(k):
        for d in range(2):
            ch = chip_of(d, k)
            for q in range(AQS):
                at = sub(d, ch, q)

                @pl.when(k > 0)
                def _():
                    remote(at, at, agx_s, ag_r.at[d, (k - 1) * AQS + q], "ctx", target(d)).wait_recv()

                @pl.when(k < 7)
                def _():
                    remote(at, at, agx_s, ag_r.at[d, k * AQS + q], "ctx", target(d)).start()

            whole = block(XF, d, ch, mine)
            remote(whole, whole, sbx_s, sbx_r, "ctx", sib).start()

    def gather_wo(k):
        for d in range(2):
            at = WO.at[chip_of(d, k) * 2 + core, d]

            @pl.when(k > 0)
            def _():
                remote(at, at, wo_s, wo_r.at[d, k - 1], "ctx", target(d)).wait_recv()

            @pl.when(k < 7)
            def _():
                remote(at, at, wo_s, wo_r.at[d, k], "ctx", target(d)).start()

            remote(at, at, wos_s, wos_r, "ctx", sib).start()

    pl.loop(0, 1)(gather_x)
    pair(0, VEC, VB.at[c, f]).start()
    pair(1, wo_ref, WO.at[c, f]).start()

    for j in range(8):
        qt = wq_ref[:, 128 * j : 128 * j + 128].astype(F32)
        kt = wq_ref[:, D + 128 * j : D + 128 * j + 128].astype(F32)
        vt = wq_ref[:, 2 * D + 128 * j : 2 * D + 128 * j + 128].astype(F32)
        for e in range(2):
            w = 2 * j + e
            qk = jnp.where(low_half, qt, pltpu.roll(kt, 64, 1)) if e == 0 else jnp.where(low_half, pltpu.roll(qt, 64, 1), kt)
            WP[w, :, 0:128] = qk.astype(BF16)
            WP[w, :, 128:256] = (vt if e == 0 else pltpu.roll(vt, 64, 1)).astype(BF16)
    WB[c, f] = WP[c]
    send_all(0, lambda to: WP.at[to], WB.at[c, f])
    for w in range(8):
        for i in range(4):
            WUS[w, :, 128 * i : 128 * (i + 1)] = wu_ref[:, 128 * (8 * i + w) : 128 * (8 * i + w + 1)]
    WU[zz, pp] = WUS[pp]
    send_plane(0, lambda to: WUS.at[to], WU.at[zz, pp])
    pl.loop(1, 4)(gather_x)
    pair(0, VB.at[c, 1 - f], VB.at[c, 1 - f]).wait_recv()
    send_all(1, lambda to: VB.at[c], VB.at[c])
    recv_all(0, WB.at[0:15, 0])
    pair(3, WB.at[:, f], WB.at[:, f]).start()
    pair(1, WO.at[c, 1 - f], WO.at[c, 1 - f]).wait_recv()
    recv_plane(0, WU.at[zz, 0:7])

    @pl.loop(4, 8)
    def _(k):
        gather_x(k)
        gather_wo(k - 4)
        pl.when(k == 4)(lambda: z_gather(0, 0))
        pl.when(k == 6)(lambda: z_gather(1, 0))


    remote(XF.at[0], XF.at[0], sbx_s, sbx_r, "ctx", sib).wait_recv()
    recv_all(1, VB.at[0:15])

    for j in range(8):
        tiles = [VB[2 * j + q // 2, q % 2] for q in range(4)]
        total = tiles[0]
        for q in range(1, 4):
            total = total + pltpu.roll(tiles[q], 32 * q, 1)
        VF[:, 128 * j : 128 * j + 128] = total
        v1 = pltpu.roll(tiles[1], 96, 1)
        v2 = pltpu.roll(tiles[2], 64, 1)
        v3 = pltpu.roll(tiles[3], 32, 1)
        rows = (
            tiles[0] + jnp.where(lane >= 96, v1, 0.0),
            jnp.where(lane < 64, v1, 0.0) + jnp.where(lane >= 64, v2, 0.0),
            jnp.where(lane < 32, v2, 0.0) + v3,
        )
        for i in range(3):
            QBR[3 * j + i : 3 * j + i + 1, :] = rows[i][1:2, :]
    for i in range(4):
        UB[0:1, 128 * i : 128 * (i + 1)] = VB[4 * i + lax.rem(c, 4), f, 0:1, :]
    for i in range(3):
        row = QBR[pl.ds(8 * i + chip, 1), :]
        BQ[i] = jnp.broadcast_to(row, (128, 128)).T
    pair(3, WB.at[:, 1 - f], WB.at[:, 1 - f]).wait_recv()
    WHT[...] = WB[...].reshape(D, 256).T

    def lanes(n):
        return pl.ds(pl.multiple_of(n * CHUNK, CHUNK), CHUNK)

    def turn(u, cosine, sine):
        a, b = u[0:32], u[32:64]
        return jnp.concatenate([a * cosine - b * sine, b * cosine + a * sine], axis=0)

    def unturn(u, cosine, sine):
        a, b = u[0:32], u[32:64]
        return jnp.concatenate([a * cosine + b * sine, b * cosine - a * sine], axis=0)

    @pl.loop(0, 8)
    def _(it):
        m = lax.div(it, 4)
        n = lax.rem(it, 4)
        xs = XF[m, pl.ds(2 * n, 2)].reshape(CHUNK, D)
        joined = nt(WHT[0:192, :], xs)
        cosine = rope_ref[0, :, lanes(n)]
        sine = rope_ref[1, :, lanes(n)]
        q = joined[0:64] + BQ[0, pl.ds(mine, BLK), 0:1]
        k = joined[64:128] + BQ[1, pl.ds(mine, BLK), 0:1]
        v = joined[128:192] + BQ[2, pl.ds(mine, BLK), 0:1]
        q = turn(q, cosine, sine)
        k = turn(k, cosine, sine)
        rows = pl.ds(pl.multiple_of(n * CHUNK, CHUNK), CHUNK)
        QT[m, :, lanes(n)] = q.astype(BF16)
        KT[m, :, lanes(n)] = k.astype(BF16)
        VT[m, :, lanes(n)] = v.astype(BF16)
        KN[m, rows, :] = k.T.astype(BF16)
        VN[m, rows, :] = v.T.astype(BF16)

    @pl.loop(0, 8)
    def _(it):
        @pl.when(lax.rem(it, 2) == 0)
        def _():
            gather_wo(4 + lax.div(it, 2))

        @pl.when(it == 4)
        def _():
            pass

        pl.when(it == 0)(lambda: z_gather(0, 1))
        pl.when(it == 5)(lambda: z_gather(1, 1))
        m = lax.div(it, 4)
        n = lax.rem(it, 4)
        s = nn(KN[m], QT[m, :, lanes(n)]) * 0.125
        e = jnp.exp(s - jnp.max(s, axis=0, keepdims=True))
        p = (e * (1.0 / jnp.sum(e, axis=0, keepdims=True))).astype(BF16)
        PT[m, :, lanes(n)] = p
        ATD[m, :, lanes(n)] = nn(VT[m], p)

    for j in range(8):
        a0 = ATD[0, :, 128 * j : 128 * j + 128]
        a1 = ATD[1, :, 128 * j : 128 * j + 128]
        ATS[2 * j] = jnp.where(low_half, a0, pltpu.roll(a1, 64, 1)).astype(BF16)
        ATS[2 * j + 1] = jnp.where(low_half, pltpu.roll(a0, 64, 1), a1).astype(BF16)
    AT[c] = ATS[c]
    send_all(2, lambda to: ATS.at[to], AT.at[c])

    remote(WO.at[0:8], WO.at[0:8], wos_s, wos_r, "ctx", sib).wait_recv()
    z_gather(0, 2)
    recv_all(2, AT.at[0:15])

    z_gather(1, 2)
    att_rows = AT[...].reshape(D, 128).T
    resid = x_ref[...].reshape(128, D).astype(F32) + nn(att_rows, WO[...].reshape(D, D)) + VF[2:3, :]
    center = resid - row_mean(resid)
    root = lax.rsqrt(row_mean(center * center) + 1e-05)
    z = center * root
    hidden = z * VF[4:5, :] + VF[5:6, :]
    Z1[...] = z
    R1[...] = jnp.broadcast_to(root, (128, 128))
    H1[...] = hidden
    hidden_low = hidden.astype(BF16)
    for m in range(2):
        HF[grp, m, pl.ds(mine, BLK)] = hidden_low[m * BLK : (m + 1) * BLK]

    def plane(buf, make, ready, after_one, after_two, finish):
        far = ((yy * 2 + 1 - f), ((1 - yy) * 2 + f))
        groups = tuple((grp, far[m], far[1 - m], (1 - yy) * 2 + 1 - f) for m in range(2))

        def to(axis, src, dst, ss, rs):
            if axis == 0:
                return remote(src, dst, ss, rs, "fsdp", 1 - f)
            return remote(src, dst, ss, rs, "ctx", c + 2 - 4 * yy)

        def at(m, i, row0):
            return buf.at[groups[m][i], m, pl.ds(row0, BLK)]

        def hand_over(m, i):
            remote(at(m, i, mine), at(m, i, mine), pb_s, pb_r.at[m, i], "ctx", sib).start()

        def arrive(m, i, n):
            to(m, at(m, i, mine), at(m, i, mine), pa_s, pa_r.at[m, n]).wait_recv()

        def work(m, i):
            remote(at(m, i, other), at(m, i, other), pb_s, pb_r.at[m, i], "ctx", sib).wait_recv()
            PB[m, i] = make(groups[m][i], m)
            SS[m, i] = PB[m, i, pl.ds(other, BLK)].astype(BF16)
            remote(SS.at[m, i], SR.at[m, i], ps_s, ps_r.at[m, i], "ctx", sib).start()

        def share(m, i):
            remote(SR.at[m, i], SR.at[m, i], ps_s, ps_r.at[m, i], "ctx", sib).wait_recv()
            return PB[m, i, pl.ds(mine, BLK)] + SR[m, i].astype(F32)

        def push(m, n, value, axis):
            RSD[m, n, 0:BLK] = value.astype(BF16)
            to(axis, RSD.at[m, n, pl.ds(0, BLK)], RR.at[m, n, pl.ds(0, BLK)], pr_s, pr_r.at[m, n]).start()

        def pulled(m, n):
            got = RR.at[m, n, pl.ds(0, BLK)]
            to(m, got, got, pr_s, pr_r.at[m, n]).wait_recv()
            return RR[m, n, 0:BLK].astype(F32)

        for m in range(2):
            to(m, at(m, 0, mine), at(m, 0, mine), pa_s, pa_r.at[m, 0]).start()
        for m in range(2):
            hand_over(m, 0)
            to(1 - m, at(m, 0, mine), at(m, 0, mine), pa_s, pa_r.at[m, 1]).start()
        if ready is None:
            for m in range(2):
                work(m, 0)
        for m in range(2):
            arrive(m, 1, 0)
            to(1 - m, at(m, 1, mine), at(m, 1, mine), pa_s, pa_r.at[m, 2]).start()
            hand_over(m, 1)
        for m in range(2):
            arrive(m, 2, 1)
            hand_over(m, 2)
        if ready is None:
            for m in range(2):
                work(m, 1)
        for m in range(2):
            arrive(m, 3, 2)
            hand_over(m, 3)
        if ready is not None:
            ready()
        for i in (2, 3) if ready is None else (3, 2, 1, 0):
            for m in range(2):
                work(m, i)
        for m in range(2):
            push(m, 1, share(m, 3), 1 - m)
        for m in range(2):
            push(m, 0, share(m, 2), 1 - m)
        after_one()
        for m in range(2):
            push(m, 2, share(m, 1) + pulled(m, 1), m)
        after_two()
        for m in range(2):
            finish(m, share(m, 0) + pulled(m, 0) + pulled(m, 2))
        remote(XF.at[0, 0:3], XF.at[0, 0:3], pa_s, sbx_r, "ctx", sib).wait_send()
        remote(XF.at[0, 0:4], XF.at[0, 0:4], pb_s, sbx_r, "ctx", sib).wait_send()
        remote(XF.at[0, 0:4], XF.at[0, 0:4], ps_s, sbx_r, "ctx", sib).wait_send()
        remote(XF.at[0, 0:3], XF.at[0, 0:3], pr_s, sbx_r, "ctx", sib).wait_send()

    def ring(make, extra, finish):
        def first(k):
            slot = 2 - lax.div(k + 7, 8) * (2 - lax.rem(k, 2))
            for d in range(2):
                ch = chip_of(d, k)
                PB[d, slot] = make(d, ch)
                SS[d, k] = PB[d, slot, pl.ds(other, BLK)].astype(BF16)
                remote(SS.at[d, k], SR.at[d, k], ss_s, ss_r.at[d, k], "ctx", sib).start()

        def sums(d, k):
            at = SR.at[d, k]
            remote(at, at, ss_s, ss_r.at[d, k], "ctx", sib).wait_recv()

        def arrived(d, q, k):
            got = RR.at[d, k, rows_of(q)]
            remote(got, got, rs_s, rs_r.at[d, k * RQS + q], "ctx", sib).wait_recv()

        def rows_of(q):
            return pl.ds(q * ROWS, ROWS if q < RQS - 1 else ROWS + 16)

        def second(k):
            slot = lax.rem(k, 2)
            for d in range(2):
                sums(d, k)
            for q in range(RQS):
                for d in range(2):
                    part = pl.ds(q * ROWS, ROWS)
                    total = PB[d, slot, pl.ds(pl.multiple_of(core * BLK + q * ROWS, ROWS), ROWS)] + SR[d, k, part].astype(F32)
                    rider = q == RQS - 1
                    if rider:
                        ride = riders(d, chip_of(d, k))

                    @pl.when(k > 1)
                    def _():
                        arrived(d, q, k - 1)
                        RSD[d, k, part] = (total + RR[d, k - 1, part].astype(F32)).astype(BF16)
                        if rider:
                            RSD[d, k, BLK : BLK + 16] = (ride + RR[d, k - 1, BLK : BLK + 16].astype(F32)).astype(BF16)

                    @pl.when(k == 1)
                    def _():
                        RSD[d, k, part] = total.astype(BF16)
                        if rider:
                            RSD[d, k, BLK : BLK + 16] = ride.astype(BF16)

                    remote(
                        RSD.at[d, k, rows_of(q)], RR.at[d, k, rows_of(q)], rs_s, rs_r.at[d, k * RQS + q],
                        "ctx", target(d),
                    ).start()

        @pl.loop(0, 9)
        def _(it):
            @pl.when(it < 8)
            def _():
                first(it)

            @pl.when(it > 1)
            def _():
                second(it - 1)

            extra(it)

        for d in range(2):
            sums(d, 0)
            for q in range(RQS):
                arrived(d, q, 7)
            finish(d, PB[d, 2, pl.ds(mine, BLK)] + SR[d, 0].astype(F32) + RR[d, 7, 0:BLK].astype(F32))

        remote(SS, SS, ss_s, sbx_r, "ctx", sib).wait_send()
        remote(RSD.at[:, 0:7], RSD.at[:, 0:7], rs_s, sbx_r, "ctx", sib).wait_send()

    def nothing():
        pass

    def up_w():
        return WU[...].reshape(D, FF_UNITS)

    def down_w():
        return WD[...].reshape(FF_UNITS, D)

    def make_up(g, m):
        u = nn(HF[g, m], up_w()) + UB[0:1, :]
        phi = 0.5 * (1.0 + lax.erf(u * 0.7071067811865476))
        a = (u * phi).astype(BF16)
        DG[g, m] = phi + u * (jnp.exp(-0.5 * u * u) * 0.3989422804014327)
        ACT[g, m] = a
        return nn(a, down_w())

    def finish_up(d, total):
        rows = slice(d * BLK, (d + 1) * BLK)
        SEC[rows, :] = H1[rows, :] + total + VF[3:4, :]

    def weights_in():
        z_gather(0, 3)
        z_gather(1, 3)

    plane(HF, make_up, weights_in, nothing, nothing, finish_up)

    resid = SEC[...]
    center = resid - row_mean(resid)
    root = lax.rsqrt(row_mean(center * center) + 1e-05)
    z = center * root
    out_ref[...] = (z * VF[6:7, :] + VF[7:8, :]).astype(BF16).reshape(2, BLK, D)
    cot = ct_ref[...].reshape(128, D).astype(F32)
    SG[...] = jnp.zeros((8, D), F32)
    SG[4:5, :] = col_sum(cot * z)
    SG[5:6, :] = col_sum(cot)
    u = cot * VF[6:7, :]
    grad = (u - row_mean(u) - z * row_mean(u * z)) * root
    G2[...] = grad
    grad_low = grad.astype(BF16)
    SG[1:2, :] = col_sum(grad_low.astype(F32))
    for m in range(2):
        BG[grp, m, pl.ds(mine, BLK)] = grad_low[m * BLK : (m + 1) * BLK]

    def make_down(g, m):
        pg = (nt(BG[g, m], down_w()) * DG[g, m]).astype(BF16)
        PG[g, m] = pg
        return nt(pg, up_w())

    def finish_down(d, total):
        rows = slice(d * BLK, (d + 1) * BLK)
        SEC[rows, :] = G2[rows, :] + total

    def down_grads():
        TT[...] = ACT[...].reshape(1024, FF_UNITS).T
        for i in range(4):
            DWD[i] = nn(TT[128 * i : 128 * (i + 1), :], BG[...].reshape(1024, D)).astype(BF16)
        z_start(1)

    def up_grads():
        TT[...] = PG[...].reshape(1024, FF_UNITS).T
        for i in range(4):
            g = nn(TT[...], HF[:, :, :, CHUNK * i : CHUNK * (i + 1)].reshape(1024, CHUNK))
            DWU[i] = g.T.astype(BF16).reshape(8, 32, FF_UNITS)
        z_start(0)
        sums = nn(jnp.ones((8, 1024), BF16), PG[...].reshape(1024, FF_UNITS))[0:1, :]
        for i in range(8):
            SG[6:7, 128 * i : 128 * (i + 1)] = sums[:, 128 * (i // 2) : 128 * (i // 2) + 128]

    plane(BG, make_down, None, down_grads, up_grads, finish_down)

    hid = SEC[...]
    z = Z1[...]
    SG[2:3, :] = col_sum(hid * z)
    SG[3:4, :] = col_sum(hid)
    u = hid * VF[4:5, :]
    grad = (u - row_mean(u) - z * row_mean(u * z)) * R1[:, 0:1]
    H1[...] = grad
    proj = grad.astype(BF16)
    SG[0:1, :] = col_sum(proj.astype(F32))
    sent_all(2, ATS.at[0:15])
    ATS[...] = nt(WO[...].reshape(D, D), proj).astype(BF16).reshape(NCTX, HEAD, 128)
    AGT[c] = ATS[c]
    send_all(3, lambda to: ATS.at[to], AGT.at[c])

    for j in range(NCHIP):
        SSO[j] = nn(AT[2 * j + 1 - core], proj).astype(BF16)
    remote(SSO, SRO, po_s, po_r, "ctx", sib).start()
    pair(4, SG, SGR).start()
    for j in range(NCHIP):
        GO[j] = nn(AT[2 * j + core], proj)
    remote(SRO, SRO, po_s, po_r, "ctx", sib).wait_recv()
    for j in range(NCHIP):
        GO[j] = GO[j] + SRO[j].astype(F32)
        XSO[j] = GO[j, pl.ds(pl.multiple_of((1 - f) * 32, 32), 32)].astype(BF16)
    pair(5, XSO, XRO).start()
    recv_all(3, AGT.at[0:15])
    sent_all(3, ATS.at[0:15])

    for j in range(8):
        t0 = AGT[2 * j].astype(F32)
        t1 = AGT[2 * j + 1].astype(F32)
        AGQ[0, :, 128 * j : 128 * j + 128] = jnp.where(low_half, t0, pltpu.roll(t1, 64, 1)).astype(BF16)
        AGQ[1, :, 128 * j : 128 * j + 128] = jnp.where(low_half, pltpu.roll(t0, 64, 1), t1).astype(BF16)

    DK[...] = jnp.zeros((2, HEAD, D), F32)
    DV[...] = jnp.zeros((2, HEAD, D), F32)

    def small_push():
        pair(4, SGR, SGR).wait_recv()
        SGT[...] = SG[...] + SGR[...]
        SGT[6:7, :] = SG[6:7, :]
        SGC[c] = SGT[:, pl.ds(pl.multiple_of(chip * 128, 128), 128)]
        send_all(4, lambda to: SGT.at[:, pl.ds(pl.multiple_of(lax.div(to, 2) * 128, 128), 128)], SGC.at[c])

    def up_push():
        def put(total):
            PUS[...] = total.astype(BF16)

        z_total(0, put)
        RU[pp] = PUS[pp]
        send_plane(1, lambda to: PUS.at[to], RU.at[pp])

    @pl.loop(0, 8)
    def _(it):
        pl.when(it == 2)(small_push)
        pl.when(it == 0)(lambda: z_relay(1))
        pl.when(it == 5)(lambda: z_relay(0))
        m = lax.div(it, 4)
        n = lax.rem(it, 4)
        q = QT[m, :, lanes(n)]
        g = AGQ[m, :, lanes(n)]
        delta = jnp.sum(g.astype(F32) * ATD[m, :, lanes(n)], axis=0, keepdims=True)
        p = PT[m, :, lanes(n)]
        ds = (p.astype(F32) * (nn(VN[m], g) - delta)).astype(BF16)
        DK[m] = DK[m] + nt(q, ds)
        DV[m] = DV[m] + nt(g, p)
        dq = nn(KT[m], ds) * 0.125
        JG[m, 0:64, lanes(n)] = unturn(dq, rope_ref[0, :, lanes(n)], rope_ref[1, :, lanes(n)]).astype(BF16)

    for m in range(2):
        JG[m, 64:128, :] = unturn(DK[m] * 0.125, rope_ref[0], rope_ref[1]).astype(BF16)
        JG[m, 128:192, :] = DV[m].astype(BF16)

    def make_token(m, ch):
        jg = JG[m, :, pl.ds(pl.multiple_of(ch * 128, 128), 128)]
        return tn(jg, WHT[0:192, :])

    def finish_token(d, total):
        tg_ref[d] = H1[d * BLK : (d + 1) * BLK, :] + total
        go_ref[16 * d : 16 * d + 16, :] = riders(d, chip) + RR[d, 7, BLK : BLK + 16].astype(F32)

    def qkv_bias_rows():
        b = nt(jnp.ones((8, D), BF16), JG[0]) + nt(jnp.ones((8, D), BF16), JG[1])
        b = jnp.concatenate([b, jnp.zeros((8, 64), F32)], axis=1)
        QBP[...] = jnp.zeros((32, UNITS), F32)
        QBP[0:1, 128:256] = jnp.where(low_half, 0.0, pltpu.roll(b[0:1, 0:128], 64, 1))
        QBP[1:2, 128:256] = jnp.where(low_half, 0.0, b[0:1, 0:128])
        QBP[2:3, 128:256] = jnp.where(low_half, 0.0, pltpu.roll(b[0:1, 128:256], 64, 1))

    def qkv_grad(n):
        cols = slice(CHUNK * n, CHUNK * (n + 1))
        g = nn(JG[0], XF[0, :, :, cols].reshape(D, CHUNK)) + nn(JG[1], XF[1, :, :, cols].reshape(D, CHUNK))
        g = jnp.concatenate([g, jnp.zeros((64, CHUNK), F32)], axis=0)
        GU[4 * n : 4 * n + 4] = g.T.reshape(4, 2, 32, UNITS) + QBP[...]

    def qkv_pair():
        XSQ[...] = GU[:, 1 - f].astype(BF16)
        pair(8, XSQ, XRQ).start()

    def qkv_push():
        pair(8, XRQ, XRQ).wait_recv()
        AQ[...] = (GU[:, f] + XRQ[...].astype(F32)).astype(BF16)
        RQ[c] = AQ[c]
        send_all(6, lambda to: AQ.at[to], RQ.at[c])

    def riders(d, ch):
        return GO[ch, pl.ds(pl.multiple_of(f * 32 + 16 * d, 16), 16)] + XRO[ch, 16 * d : 16 * d + 16].astype(F32)

    def small_rest():
        recv_all(4, SGC.at[0:15])
        total = SGC[0]
        for w in range(1, NCTX):
            total = total + SGC[w]
        gs_ref[...] = total
        here = lax.rem(c, 4)
        gs_ref[6:7, :] = SGC[here, 6:7, :] + SGC[4 + here, 6:7, :] + SGC[8 + here, 6:7, :] + SGC[12 + here, 6:7, :]

    def down_rest():
        def put(total):
            gd_ref[...] = total

        z_total(1, put)

    def on_the_way(it):
        pl.when(it == 0)(qkv_bias_rows)
        for n in range(4):
            pl.when(it == n)(partial(qkv_grad, n))
        pl.when(it == 3)(qkv_pair)
        pl.when(it == 4)(small_rest)
        pl.when(it == 5)(qkv_push)
        pl.when(it == 6)(down_rest)
        pl.when(it == 8)(up_push)

    pair(5, XRO, XRO).wait_recv()
    ring(make_token, on_the_way, finish_token)
    recv_plane(1, RU.at[0:7])
    recv_all(6, RQ.at[0:15])

    remote(XF.at[0, 0:7], XF.at[0, 0:7], agx_s, sbx_r, "ctx", sib).wait_send()
    remote(XF.at[0], XF.at[0], sbx_s, sbx_r, "ctx", sib).wait_send()
    remote(WO.at[0:7], WO.at[0:7], wo_s, sbx_r, "ctx", sib).wait_send()
    remote(WO.at[0:8], WO.at[0:8], wos_s, sbx_r, "ctx", sib).wait_send()
    sent_all(0, WP.at[0:15])
    sent_all(1, VB.at[0:15])
    sent_all(4, SGC.at[0:15])
    sent_all(6, AQ.at[0:15])
    remote(SSO, SSO, po_s, po_r, "ctx", sib).wait_send()
    sent_plane(0, WUS.at[0:7])
    sent_plane(1, PUS.at[0:7])
    for kd in range(2):
        for s in range(3):
            z_gather(kd, s, True)
        z_start(kd, True)
        z_relay(kd, True)
    for i, at in ((0, VEC), (1, wo_ref), (3, WB.at[:, f]), (4, SG), (5, XSO), (8, XSQ)):
        pair(i, at, at).wait_send()


def rope_tables():
    freqs = (np.float32(10000.0) ** (-np.arange(0, HEAD, 2, dtype=np.float32) / np.float32(HEAD))).astype(np.float32)
    angles = freqs[:, None] * np.arange(1024, dtype=np.float32)[None, :]
    return np.stack([np.cos(angles), np.sin(angles)]).astype(np.float32)


def fused_body(
    tokens, cotangent, qkv_weight, out_weight, up_weight, down_weight, qkv_bias, out_bias, up_bias, down_bias,
    first_gain, first_shift, second_gain, second_shift,
):
    scratch = [
        ((8, 128), F32),
        ((2, 8, 128, D), BF16), ((4, 2, 128, D), BF16), ((4, 2, 128, D), BF16),
        ((16, 32, 256), BF16), ((16, 2, 32, 256), BF16), ((8, 32, FF_UNITS), BF16), ((4, 8, 32, FF_UNITS), BF16),
        ((16, 2, 32, D), BF16), ((4, 128, D), BF16),
        ((16, 2, 8, 128), F32), ((8, D), F32), ((8, FF_UNITS), F32), ((24, 128), F32), ((3, 128, 128), F32),
        ((256, D), BF16),
        ((2, 64, D), BF16), ((2, 64, D), BF16), ((2, 64, D), BF16), ((2, D, 64), BF16), ((2, D, 64), BF16),
        ((2, D, D), BF16), ((2, 64, D), F32),
        ((16, 64, 128), BF16), ((16, 64, 128), BF16), ((16, 64, 128), BF16),
        ((128, D), F32), ((128, D), F32), ((128, 128), F32), ((128, D), F32), ((128, D), F32),
        ((4, 2, 128, FF_UNITS), F32), ((4, 2, 128, FF_UNITS), BF16), ((4, 2, 128, FF_UNITS), BF16),
        ((2, 4, 128, D), F32),
        ((2, 8, BLK, D), BF16), ((2, 8, BLK, D), BF16), ((2, 8, 80, D), BF16), ((2, 8, 80, D), BF16),
        ((FF_UNITS, 1024), BF16),
        ((16, 2, 32, UNITS), F32), ((8, 32, FF_UNITS), BF16),
        ((4, 8, 32, FF_UNITS), BF16), ((4, 128, D), BF16), ((4, 8, 32, FF_UNITS), BF16), ((4, 128, D), BF16),
        ((8, BLK, D), F32), ((8, 32, D), BF16), ((8, 32, D), BF16), ((8, BLK, D), BF16), ((8, BLK, D), BF16),
        ((8, D), F32), ((8, D), F32), ((8, D), F32), ((16, 8, 128), F32), ((2, 64, D), BF16),
        ((2, 64, D), F32), ((2, 64, D), F32), ((2, 192, D), BF16),
        ((16, 32, UNITS), BF16), ((16, 32, UNITS), BF16), ((16, 32, UNITS), BF16), ((32, UNITS), F32),
    ]
    sems = [(14,), (2, 8 * AQS), (2, 8), (2, 8 * RQS), (2, 8), (9,), (9,), (11,), (11,), (2,), (2,)]
    sems += [(2, 3), (2, 4), (2, 4), (2, 3), (2, 6), (2, 4), (2, 4), (2, 4)]
    vmem = pl.BlockSpec(memory_space=pltpu.VMEM)
    shapes = [((2, BLK, D), BF16), ((2, BLK, D), F32), ((16, 32, UNITS), BF16), ((32, D), F32), ((8, 32, FF_UNITS), BF16), ((128, D), F32), ((8, 128), F32)]
    final = shapes[:2] + [((32, 3 * D), F32), shapes[3], ((32, 4 * D), F32), shapes[5]]
    bias = (up_bias, qkv_bias, out_bias, down_bias, first_gain, first_shift, second_gain, second_shift)
    made = pl.pallas_call(
        layer_kernel,
        out_shape=[jax.ShapeDtypeStruct(s, t) for s, t in shapes],
        in_specs=[vmem] * 15,
        out_specs=[vmem] * 7,
        scratch_shapes=[pltpu.VMEM(s, t) for s, t in scratch] + [pltpu.SemaphoreType.DMA(s) for s in sems],
        compiler_params=pltpu.CompilerParams(collective_id=0, has_side_effects=True, vmem_limit_bytes=VMEM_LIMIT),
        name="layer",
    )(
        tokens[:, 0], cotangent[:, 0], qkv_weight, out_weight, up_weight, down_weight, jnp.asarray(rope_tables()),
        *(v[None] for v in bias),
    )
    anywhere = pl.BlockSpec(memory_space=pl.ANY)
    widths = (96, 32, 128, 32, 32, 32, 32, 32)
    last = pl.pallas_call(
        finish_kernel,
        out_shape=[jax.ShapeDtypeStruct(s, t) for s, t in final] + [jax.ShapeDtypeStruct((1, w), F32) for w in widths],
        in_specs=[anywhere, anywhere, vmem, anywhere, vmem, anywhere, vmem],
        out_specs=[vmem] * 14,
        scratch_shapes=[pltpu.VMEM((24, 128), F32), pltpu.SemaphoreType.DMA((4,))],
        name="finish",
    )(*made)
    return (last[0][:, None], last[1][:, None], *last[2:6], *(v[0] for v in last[6:]))


def finish_kernel(*refs):
    (out, tg, rq, go, ru, gd, gs), done, small, (gb, sems) = refs[:7], refs[7:13], refs[13:21], refs[21:]
    pairs = ((out, done[0]), (tg, done[1]), (go, done[3]), (gd, done[5]))
    copies = [pltpu.make_async_copy(a, b, sems.at[i]) for i, (a, b) in enumerate(pairs)]
    for copy in copies:
        copy.start()
    gq, gu = done[2], done[4]
    low_half = lax.broadcasted_iota(jnp.int32, (1, 128), 1) < 64
    for j in range(8):
        a = rq[2 * j].astype(F32)
        b = rq[2 * j + 1].astype(F32)
        a0, a1, b0, b1 = a[:, 0:128], a[:, 128:256], b[:, 0:128], b[:, 128:256]
        v = pltpu.roll(b1, 64, 1)
        gq[:, 128 * j : 128 * (j + 1)] = jnp.where(low_half, a0, pltpu.roll(b0, 64, 1))
        gq[:, D + 128 * j : D + 128 * (j + 1)] = jnp.where(low_half, pltpu.roll(a0, 64, 1), b0)
        gq[:, 2 * D + 128 * j : 2 * D + 128 * (j + 1)] = jnp.where(low_half, a1, v)
        bias = jnp.where(low_half, pltpu.roll(a1, 64, 1), b1)
        for i in range(3):
            gb[8 * i + j : 8 * i + j + 1, :] = bias[i : i + 1, :]
    for w in range(8):
        for i in range(4):
            gu[:, 128 * (8 * i + w) : 128 * (8 * i + w + 1)] = ru[w, :, 128 * i : 128 * (i + 1)].astype(F32)
    index = lax.axis_index("ctx") * 2 + lax.axis_index("fsdp")
    place = lax.rem(index, 4)
    turned = pltpu.roll(gs[...], lax.rem(128 - 32 * place, 128), 1)
    for ref, row in zip(small[1:], (0, 6, 1, 2, 3, 4, 5)):
        ref[...] = gs[6:7, :] if row == 6 else turned[row : row + 1, 0:32]
    offset = lax.rem(96 * index, 128)
    row = lax.div(96 * index, 128)
    lane = lax.broadcasted_iota(jnp.int32, (1, 128), 1)
    back = lax.rem(128 - offset, 128)
    one = pltpu.roll(gb[pl.ds(row, 1), :], back, 1)
    two = pltpu.roll(gb[pl.ds(lax.rem(row + 1, 24), 1), :], back, 1)
    small[0][...] = jnp.where(lane < 128 - offset, one, two)[:, 0:96]
    for copy in copies:
        copy.wait()


VMEM_LIMIT = 63 * 1024 * 1024


def layernorm(resid, gain, shift):
    center = resid - jnp.mean(resid, axis=-1, keepdims=True)
    spread = jnp.mean(center * center, axis=-1, keepdims=True)
    return center * lax.rsqrt(spread + 1e-05) * gain + shift


def tables(position):
    freqs = 10000.0 ** (-jnp.arange(0, HEAD, 2, dtype=jnp.float32) / HEAD)
    angles = position[:, None] * freqs[None, :]
    return (jnp.cos(angles)[:, None, :], jnp.sin(angles)[:, None, :])


def rotate(heads_in, cosine, sine):
    middle = heads_in.shape[-1] // 2
    first = heads_in[..., :middle]
    second = heads_in[..., middle:]
    return jnp.concatenate(
        [first * cosine - second * sine, second * cosine + first * sine], axis=-1
    )


def unrotate(heads_in, cosine, sine):
    middle = heads_in.shape[-1] // 2
    first = heads_in[..., :middle]
    second = heads_in[..., middle:]
    return jnp.concatenate(
        [first * cosine + second * sine, second * cosine - first * sine], axis=-1
    )


def split_heads(flat_rows):
    return flat_rows.reshape(flat_rows.shape[0], HEADS, HEAD)


def over_blocks(update, carried, count, limit):
    size = math.gcd(count, limit)

    def advance(block_idx, state):
        return update(state, block_idx * size, size)

    return lax.fori_loop(0, count // size, advance, carried)


def column_sum(matrix):
    return jnp.sum(matrix.astype(jnp.float32), axis=0)


def forward_local(sequence, weights_now, cosine, sine, group):
    (
        qkv_full,
        out_full,
        up_full,
        down_full,
        qkv_vector,
        out_vector,
        up_vector,
        down_vector,
        gain_first,
        shift_first,
        gain_second,
        shift_second,
    ) = weights_now
    rows = sequence.shape[0]
    width = sequence.shape[1]
    joined = jnp.dot(sequence, qkv_full, preferred_element_type=jnp.float32) + qkv_vector.astype(
        jnp.float32
    )
    query_flat = (
        rotate(split_heads(joined[:, :width]), cosine, sine)
        .astype(jnp.bfloat16)
        .reshape(rows, width)
    )
    keys_flat = (
        rotate(split_heads(joined[:, width : 2 * width]), cosine, sine)
        .astype(jnp.bfloat16)
        .reshape(rows, width)
    )
    values_flat = joined[:, 2 * width :].astype(jnp.bfloat16)
    query_heads = split_heads(query_flat)
    start_state = (
        jnp.full((HEADS, rows), -1e30, jnp.float32),
        jnp.zeros((HEADS, rows), jnp.float32),
        jnp.zeros((rows, HEADS, HEAD), jnp.float32),
    )
    keys_piece = lax.all_gather(keys_flat, "ctx", axis=0, tiled=True)
    values_piece = lax.all_gather(values_flat, "ctx", axis=0, tiled=True)

    def absorb_block(state, offset, size):
        running, total, accum = state
        key_block = split_heads(lax.dynamic_slice_in_dim(keys_piece, offset, size, 0))
        value_block = split_heads(lax.dynamic_slice_in_dim(values_piece, offset, size, 0))
        scores = (
            jnp.einsum("qhd,khd->hqk", query_heads, key_block, preferred_element_type=jnp.float32)
            * 0.125
        )
        highest_new = jnp.maximum(running, jnp.max(scores, axis=-1))
        factor = jnp.exp(running - highest_new)
        expo = jnp.exp(scores - highest_new[:, :, None])
        total = total * factor + jnp.sum(expo, axis=-1)
        accum = accum * factor.T[:, :, None] + jnp.einsum(
            "hqk,khd->qhd",
            expo.astype(jnp.bfloat16),
            value_block,
            preferred_element_type=jnp.float32,
        )
        return (highest_new, total, accum)

    running, total, accum = over_blocks(absorb_block, start_state, keys_piece.shape[0], group)
    attended = accum / total.T[:, :, None]
    logsum = running + jnp.log(total)
    att_low = attended.reshape(rows, width).astype(jnp.bfloat16)
    projected = jnp.dot(att_low, out_full, preferred_element_type=jnp.float32) + out_vector.astype(
        jnp.float32
    )
    resid_first = sequence.astype(jnp.float32) + projected
    hidden = layernorm(resid_first, gain_first.astype(jnp.float32), shift_first.astype(jnp.float32))
    hidden_low = hidden.astype(jnp.bfloat16)
    preact = jnp.dot(hidden_low, up_full, preferred_element_type=jnp.float32) + up_vector.astype(
        jnp.float32
    )
    activ_low = jax.nn.gelu(preact, approximate=False).astype(jnp.bfloat16)
    branch = jnp.dot(activ_low, down_full, preferred_element_type=jnp.float32) + down_vector.astype(
        jnp.float32
    )
    resid_second = hidden + branch
    output = layernorm(
        resid_second, gain_second.astype(jnp.float32), shift_second.astype(jnp.float32)
    )
    saved = (
        query_flat,
        keys_flat,
        values_flat,
        attended,
        logsum,
        att_low,
        resid_first,
        hidden_low,
        preact,
        activ_low,
        resid_second,
    )
    return (output.astype(jnp.bfloat16), saved)


def body(
    tokens,
    cotangent,
    qkv_weight,
    out_weight,
    up_weight,
    down_weight,
    qkv_bias,
    out_bias,
    up_bias,
    down_bias,
    first_gain,
    first_shift,
    second_gain,
    second_shift,
):
    gathered = (
        lax.all_gather(qkv_weight, ("ctx", "fsdp"), axis=0, tiled=True),
        lax.all_gather(out_weight, ("ctx", "fsdp"), axis=0, tiled=True),
        lax.all_gather(up_weight, ("ctx", "fsdp"), axis=0, tiled=True),
        lax.all_gather(down_weight, ("ctx", "fsdp"), axis=0, tiled=True),
        lax.all_gather(qkv_bias, ("ctx", "fsdp"), axis=0, tiled=True),
        lax.all_gather(out_bias, ("ctx", "fsdp"), axis=0, tiled=True),
        lax.all_gather(up_bias, ("ctx", "fsdp"), axis=0, tiled=True),
        lax.all_gather(down_bias, ("ctx", "fsdp"), axis=0, tiled=True),
        lax.all_gather(first_gain, ("ctx", "fsdp"), axis=0, tiled=True),
        lax.all_gather(first_shift, ("ctx", "fsdp"), axis=0, tiled=True),
        lax.all_gather(second_gain, ("ctx", "fsdp"), axis=0, tiled=True),
        lax.all_gather(second_shift, ("ctx", "fsdp"), axis=0, tiled=True),
    )
    rows = tokens.shape[2]
    width = tokens.shape[3]
    cycle_size = lax.axis_size("ctx")
    group = rows * math.gcd(cycle_size, 8)
    length = rows * cycle_size
    position = (lax.axis_index("ctx") * rows + jnp.arange(rows)).astype(jnp.float32)
    cosine, sine = tables(position)
    outputs = []
    savings = []
    for micro_idx in range(MICRO):
        output, saved = forward_local(tokens[micro_idx, 0], gathered, cosine, sine, group)
        outputs.append(output)
        savings.append(saved)
    weights_back = (
        lax.all_gather(qkv_weight, ("ctx", "fsdp"), axis=0, tiled=True),
        lax.all_gather(out_weight, ("ctx", "fsdp"), axis=0, tiled=True),
        lax.all_gather(up_weight, ("ctx", "fsdp"), axis=0, tiled=True),
        lax.all_gather(down_weight, ("ctx", "fsdp"), axis=0, tiled=True),
        lax.all_gather(qkv_bias, ("ctx", "fsdp"), axis=0, tiled=True),
        lax.all_gather(out_bias, ("ctx", "fsdp"), axis=0, tiled=True),
        lax.all_gather(up_bias, ("ctx", "fsdp"), axis=0, tiled=True),
        lax.all_gather(down_bias, ("ctx", "fsdp"), axis=0, tiled=True),
        lax.all_gather(first_gain, ("ctx", "fsdp"), axis=0, tiled=True),
        lax.all_gather(first_shift, ("ctx", "fsdp"), axis=0, tiled=True),
        lax.all_gather(second_gain, ("ctx", "fsdp"), axis=0, tiled=True),
        lax.all_gather(second_shift, ("ctx", "fsdp"), axis=0, tiled=True),
    )
    (
        qkv_full,
        out_full,
        up_full,
        down_full,
        qkv_vector,
        out_vector,
        up_vector,
        down_vector,
        gain_first,
        shift_first,
        gain_second,
        shift_second,
    ) = weights_back
    token_grads = []
    totals = []
    for micro_idx in range(MICRO):
        (
            query_flat,
            keys_flat,
            values_flat,
            attended,
            logsum,
            att_low,
            resid_first,
            hidden_low,
            preact,
            activ_low,
            resid_second,
        ) = savings[micro_idx]
        sequence = tokens[micro_idx, 0]
        grad_out = cotangent[micro_idx, 0].astype(jnp.float32)
        unused_two, second_back = jax.vjp(
            layernorm,
            resid_second,
            gain_second.astype(jnp.float32),
            shift_second.astype(jnp.float32),
        )
        grad_second, second_gain_grad, second_shift_grad = second_back(grad_out)
        branch_grad = grad_second.astype(jnp.bfloat16)
        down_bias_grad = column_sum(branch_grad)
        down_weight_grad = jnp.einsum(
            "tf,td->fd", activ_low, branch_grad, preferred_element_type=jnp.float32
        )
        activ_grad = jnp.einsum(
            "td,fd->tf", branch_grad, down_full, preferred_element_type=jnp.float32
        )
        unused_gelu, gelu_back = jax.vjp(partial(jax.nn.gelu, approximate=False), preact)
        preact_grad = gelu_back(activ_grad)[0].astype(jnp.bfloat16)
        up_bias_grad = column_sum(preact_grad)
        up_weight_grad = jnp.einsum(
            "td,tf->df", hidden_low, preact_grad, preferred_element_type=jnp.float32
        )
        hidden_grad = grad_second + jnp.einsum(
            "tf,df->td", preact_grad, up_full, preferred_element_type=jnp.float32
        )
        unused_one, first_back = jax.vjp(
            layernorm, resid_first, gain_first.astype(jnp.float32), shift_first.astype(jnp.float32)
        )
        grad_first, first_gain_grad, first_shift_grad = first_back(hidden_grad)
        proj_grad = grad_first.astype(jnp.bfloat16)
        out_bias_grad = column_sum(proj_grad)
        out_weight_grad = jnp.einsum(
            "tc,te->ce", att_low, proj_grad, preferred_element_type=jnp.float32
        )
        att_grad = jnp.einsum(
            "te,ce->tc", proj_grad, out_full, preferred_element_type=jnp.float32
        ).astype(jnp.bfloat16)
        att_heads = split_heads(att_grad)
        query_heads = split_heads(query_flat)
        delta = jnp.sum(att_heads.astype(jnp.float32) * attended, axis=-1).T
        key_all, value_all = (
            lax.all_gather(keys_flat, "ctx", axis=0, tiled=True),
            lax.all_gather(values_flat, "ctx", axis=0, tiled=True),
        )

        def query_update(state, offset, size):
            key_block = split_heads(lax.dynamic_slice_in_dim(key_all, offset, size, 0))
            value_block = split_heads(lax.dynamic_slice_in_dim(value_all, offset, size, 0))
            scores = (
                jnp.einsum(
                    "qhd,khd->hqk", query_heads, key_block, preferred_element_type=jnp.float32
                )
                * 0.125
            )
            chance = jnp.exp(scores - logsum[:, :, None])
            dprob = jnp.einsum(
                "qhd,khd->hqk", att_heads, value_block, preferred_element_type=jnp.float32
            )
            score_grad = (chance * (dprob - delta[:, :, None])).astype(jnp.bfloat16)
            return state + jnp.einsum(
                "hqk,khd->qhd", score_grad, key_block, preferred_element_type=jnp.float32
            )

        query_grad = (
            over_blocks(query_update, jnp.zeros((rows, HEADS, HEAD), jnp.float32), length, group)
            * 0.125
        )

        def fill(state, offset, size):
            key_block = split_heads(lax.dynamic_slice_in_dim(key_all, offset, size, 0))
            value_block = split_heads(lax.dynamic_slice_in_dim(value_all, offset, size, 0))
            scores = (
                jnp.einsum(
                    "qhd,khd->hqk", query_heads, key_block, preferred_element_type=jnp.float32
                )
                * 0.125
            )
            chance = jnp.exp(scores - logsum[:, :, None])
            value_part = jnp.einsum(
                "hqk,qhd->khd",
                chance.astype(jnp.bfloat16),
                att_heads,
                preferred_element_type=jnp.float32,
            )
            dprob = jnp.einsum(
                "qhd,khd->hqk", att_heads, value_block, preferred_element_type=jnp.float32
            )
            score_grad = (chance * (dprob - delta[:, :, None])).astype(jnp.bfloat16)
            key_part = (
                jnp.einsum(
                    "hqk,qhd->khd", score_grad, query_heads, preferred_element_type=jnp.float32
                )
                * 0.125
            )
            piece = jnp.concatenate(
                [key_part.reshape(size, width), value_part.reshape(size, width)], axis=1
            )
            return lax.dynamic_update_slice_in_dim(state, piece, offset, 0)

        combined = lax.psum_scatter(
            over_blocks(
                fill,
                jnp.zeros((lax.axis_size("ctx") * rows, 2 * width), jnp.float32),
                lax.axis_size("ctx") * rows,
                group,
            ),
            "ctx",
            scatter_dimension=0,
            tiled=True,
        )
        key_grad = split_heads(combined[:, :width])
        value_grad = combined[:, width:]
        joined_grad = jnp.concatenate(
            [
                unrotate(query_grad, cosine, sine).reshape(rows, width),
                unrotate(key_grad, cosine, sine).reshape(rows, width),
                value_grad,
            ],
            axis=1,
        ).astype(jnp.bfloat16)
        qkv_bias_grad = column_sum(joined_grad)
        qkv_weight_grad = jnp.einsum(
            "tc,te->ce", sequence, joined_grad, preferred_element_type=jnp.float32
        )
        token_grads.append(
            grad_first
            + jnp.einsum("te,ce->tc", joined_grad, qkv_full, preferred_element_type=jnp.float32)
        )
        fresh = [
            qkv_weight_grad,
            out_weight_grad,
            up_weight_grad,
            down_weight_grad,
            qkv_bias_grad,
            out_bias_grad,
            up_bias_grad,
            down_bias_grad,
            first_gain_grad,
            first_shift_grad,
            second_gain_grad,
            second_shift_grad,
        ]
        if micro_idx == 0:
            totals = fresh
        else:
            totals = [older + newer for older, newer in zip(totals, fresh)]
    summed = (
        lax.psum_scatter(totals[0], ("ctx", "fsdp"), scatter_dimension=0, tiled=True),
        lax.psum_scatter(totals[1], ("ctx", "fsdp"), scatter_dimension=0, tiled=True),
        lax.psum_scatter(totals[2], ("ctx", "fsdp"), scatter_dimension=0, tiled=True),
        lax.psum_scatter(totals[3], ("ctx", "fsdp"), scatter_dimension=0, tiled=True),
        lax.psum_scatter(totals[4], ("ctx", "fsdp"), scatter_dimension=0, tiled=True),
        lax.psum_scatter(totals[5], ("ctx", "fsdp"), scatter_dimension=0, tiled=True),
        lax.psum_scatter(totals[6], ("ctx", "fsdp"), scatter_dimension=0, tiled=True),
        lax.psum_scatter(totals[7], ("ctx", "fsdp"), scatter_dimension=0, tiled=True),
        lax.psum_scatter(totals[8], ("ctx", "fsdp"), scatter_dimension=0, tiled=True),
        lax.psum_scatter(totals[9], ("ctx", "fsdp"), scatter_dimension=0, tiled=True),
        lax.psum_scatter(totals[10], ("ctx", "fsdp"), scatter_dimension=0, tiled=True),
        lax.psum_scatter(totals[11], ("ctx", "fsdp"), scatter_dimension=0, tiled=True),
    )
    output_all = jnp.stack(outputs)[:, None]
    token_all = jnp.stack(token_grads)[:, None]
    return (
        output_all,
        token_all,
        summed[0],
        summed[1],
        summed[2],
        summed[3],
        summed[4],
        summed[5],
        summed[6],
        summed[7],
        summed[8],
        summed[9],
        summed[10],
        summed[11],
    )


def solution(mesh):
    in_specs = (
        P(None, "fsdp", "ctx", None),
        P(None, "fsdp", "ctx", None),
        P(("ctx", "fsdp"), None),
        P(("ctx", "fsdp"), None),
        P(("ctx", "fsdp"), None),
        P(("ctx", "fsdp"), None),
        P(("ctx", "fsdp")),
        P(("ctx", "fsdp")),
        P(("ctx", "fsdp")),
        P(("ctx", "fsdp")),
        P(("ctx", "fsdp")),
        P(("ctx", "fsdp")),
        P(("ctx", "fsdp")),
        P(("ctx", "fsdp")),
    )
    out_specs = (
        P(None, "fsdp", "ctx", None),
        P(None, "fsdp", "ctx", None),
        P(("ctx", "fsdp"), None),
        P(("ctx", "fsdp"), None),
        P(("ctx", "fsdp"), None),
        P(("ctx", "fsdp"), None),
        P(("ctx", "fsdp")),
        P(("ctx", "fsdp")),
        P(("ctx", "fsdp")),
        P(("ctx", "fsdp")),
        P(("ctx", "fsdp")),
        P(("ctx", "fsdp")),
        P(("ctx", "fsdp")),
        P(("ctx", "fsdp")),
    )
    fused = mesh.shape["ctx"] == NCTX and mesh.shape["fsdp"] == 2
    return jax.shard_map(fused_body if fused else body, mesh=mesh, in_specs=in_specs, out_specs=out_specs, check_vma=False)
```

```python
from functools import partial
import math

import jax
import jax.numpy as jnp
from jax import lax
from jax.experimental import pallas as pl
from jax.experimental.pallas import tpu as pltpu
from jax.sharding import PartitionSpec as P
import numpy as np

HEADS = 16
HEAD = 64
MICRO = 2
MESH = pl.DeviceIdType.MESH
F32 = jnp.float32
BF16 = jnp.bfloat16


NCTX = 16
NCHIP = 8
BLK = 64
D = 1024
UNITS = 256
FF_UNITS = 512
CHUNK = 256
AQS = 4
RQS = 4
ROWS = BLK // RQS


def chip_at(place):
    row = lax.div(place, 4)
    return ((1 - row) * place + row * (7 - place)) * 2 + row


def nn(a, b):
    return jnp.dot(a, b, preferred_element_type=F32)


def nt(a, b):
    return lax.dot_general(a, b, (((1,), (1,)), ((), ())), preferred_element_type=F32)


def tn(a, b):
    return lax.dot_general(a, b, (((0,), (0,)), ((), ())), preferred_element_type=F32)


def row_mean(v):
    return jnp.sum(v, axis=1, keepdims=True) * (1.0 / D)


def col_sum(v):
    return jnp.sum(v, axis=0, keepdims=True)


def layer_kernel(
    x_ref, ct_ref, wq_ref, wo_ref, wu_ref, wd_ref, rope_ref, v0, v1, v2, v3, v4, v5, v6, v7,
    out_ref, tg_ref, RQ, go_ref, RU, gd_ref, gs_ref,
    VEC, XF, HF, BG, WP, WB, WUS, WU, WO, WD, VB, VF, UB, QBR, BQ, WHT, QT, KT, VT, KN, VN, PT, ATD, ATS, AT, AGT,
    H1, Z1, R1, SEC, G2, DG, ACT, PG, PB, SS, SR, RSD, RR, TT,
    GU, PUS, DWU, DWD, ZRU, ZRD, GO, XSO, XRO, SSO, SRO, SG, SGR, SGT, SGC, AGQ,
    DK, DV, JG, XSQ, XRQ, AQ, QBP,
    one, ag_r, ss_r, rs_r, wo_r, all_s, all_r, pair_s, pair_r, plane_s, plane_r,
    pa_r, pb_r, ps_r, pr_r, z_s, z_r, q_s, q_r,
):
    c = lax.axis_index("ctx")
    f = lax.axis_index("fsdp")
    core = lax.rem(c, 2)
    chip = lax.div(c, 2)
    yy = lax.rem(chip, 2)
    zz = lax.div(chip, 2)
    r = (1 - yy) * zz + yy * (7 - zz)
    nxt = chip_at(lax.rem(r + 1, 8)) * 2 + core
    prv = chip_at(lax.rem(r + 7, 8)) * 2 + core
    sib = c + 1 - 2 * core
    mine = pl.multiple_of(core * BLK, BLK)
    other = pl.multiple_of((1 - core) * BLK, BLK)
    lane = lax.broadcasted_iota(jnp.int32, (1, 128), 1)
    low_half = lane < 64

    def remote(src, dst, ss, rs, axis, to):
        return pltpu.make_async_remote_copy(
            src_ref=src, dst_ref=dst, send_sem=ss, recv_sem=rs, device_id={axis: to}, device_id_type=MESH
        )

    def target(d):
        return nxt if d == 0 else prv

    def chip_of(d, k):
        return chip_at(lax.rem(r - k + 8, 8) if d == 0 else lax.rem(r + k, 8))

    def send_all(e, src_at, dst):
        @pl.loop(1, NCTX)
        def _(o):
            to = lax.rem(c + o, NCTX)
            remote(src_at(to), dst, all_s.at[e], all_r.at[e], "ctx", to).start()

    def recv_all(e, slab):
        remote(slab, slab, all_s.at[e], all_r.at[e], "ctx", sib).wait_recv()

    def sent_all(e, slab):
        remote(slab, slab, all_s.at[e], all_r.at[e], "ctx", sib).wait_send()

    pp = lax.rem(c, 4) * 2 + f
    grp = yy * 2 + f

    def send_plane(e, src_at, dst):
        @pl.loop(1, 8)
        def _(o):
            to = lax.rem(pp + o, 8)
            pltpu.make_async_remote_copy(
                src_ref=src_at(to), dst_ref=dst, send_sem=plane_s.at[e], recv_sem=plane_r.at[e],
                device_id={"ctx": zz * 4 + lax.div(to, 2), "fsdp": lax.rem(to, 2)}, device_id_type=MESH,
            ).start()

    def recv_plane(e, slab):
        remote(slab, slab, plane_s.at[e], plane_r.at[e], "ctx", sib).wait_recv()

    def sent_plane(e, slab):
        remote(slab, slab, plane_s.at[e], plane_r.at[e], "ctx", sib).wait_send()

    def at_plane(body):
        for place in range(4):

            @pl.when(zz == place)
            def _():
                body(place)

    def z_block(kd, b, dr, s, place):
        at = WU.at[b, pl.ds(4 * kd, 4)] if kd < 2 else WD.at[b, pl.ds(64 * kd - 128, 64)]
        return remote(at, at, z_s.at[kd, dr * 3 + s], z_r.at[kd, b], "ctx", c + (4 if dr == 0 else -4))

    def z_gather(kd, s, sent=False):
        def body(place):
            for dr in range(2):
                b = place - s if dr == 0 else place + s
                more = place < 3 if dr == 0 else place > 0
                if not 0 <= b < 4:
                    continue
                if s > 0 and not sent:
                    z_block(kd, b, dr, s - 1, place).wait_recv()
                if s < 3 and more:
                    copy = z_block(kd, b, dr, s, place)
                    copy.wait_send() if sent else copy.start()

        at_plane(body)

    def z_slot(source, t):
        return (source - t) % 4 - 1

    def z_term(kd, t, there, slot, place):
        src, got = ((DWU, ZRU), (DWD, ZRD))[kd]
        return remote(src.at[t], got.at[slot], q_s.at[kd, t], q_r.at[kd, slot], "ctx", c + 4 * (there - place))

    def z_start(kd, sent=False):
        def body(place):
            for t in (3, 2, 1, 0) if place < 2 else (0, 1, 2, 3):
                if t == place or (place, t) in ((1, 3), (2, 0)):
                    continue
                far = (place, t) in ((0, 3), (3, 0))
                there = (1 if place == 0 else 2) if far else t
                copy = z_term(kd, t, there, 3 if far else z_slot(place, t), place)
                copy.wait_send() if sent else copy.start()

        at_plane(body)

    def z_relay(kd, sent=False):
        def body(place):
            if place in (1, 2):
                t = 3 if place == 1 else 0
                src, got = ((DWU, ZRU), (DWD, ZRD))[kd]
                copy = z_term(kd, t, t, z_slot(place, t), place)
                if sent:
                    copy.wait_send()
                else:
                    z_term(kd, t, t, 3, place).wait_recv()
                    src[t] = (src[t].astype(F32) + got[3].astype(F32)).astype(BF16)
                    copy.start()

        at_plane(body)

    def z_total(kd, put):
        def body(place):
            src, got = ((DWU, ZRU), (DWD, ZRD))[kd]
            total = src[place].astype(F32)
            for source in range(4):
                if source != place and (source, place) not in ((0, 3), (3, 0)):
                    slot = z_slot(source, place)
                    z_term(kd, place, place, slot, place).wait_recv()
                    total = total + got[slot].astype(F32)
            put(total)

        at_plane(body)

    def pair(i, src, dst):
        return remote(src, dst, pair_s.at[i], pair_r.at[i], "fsdp", 1 - f)

    agx_s, sbx_s, sbx_r, ss_s, rs_s, wo_s, wos_s, wos_r, po_s, po_r, pa_s, pb_s, ps_s, pr_s = (one.at[i] for i in range(14))
    barrier = pltpu.get_barrier_semaphore()

    @pl.loop(1, NCTX)
    def _(o):
        pl.semaphore_signal(barrier, inc=1, device_id={"ctx": lax.rem(c + o, NCTX)}, device_id_type=MESH)

    @pl.loop(0, 4)
    def _(o):
        there = lax.div(c, 4) * 4 + lax.rem(c + o, 4)
        pl.semaphore_signal(barrier, inc=1, device_id={"ctx": there, "fsdp": 1 - f}, device_id_type=MESH)

    pl.semaphore_wait(barrier, NCTX + 3)

    def block(buf, m, ch, row0):
        return buf.at[m, ch, pl.ds(row0, BLK)]

    def sub(m, ch, q):
        return XF.at[m, ch, pl.ds(pl.multiple_of(core * BLK + (BLK // AQS) * q, BLK // AQS), BLK // AQS)]

    for m in range(2):
        XF[m, chip, pl.ds(mine, BLK)] = x_ref[m]
    WO[chip, core, f] = wo_ref[...]
    WD[zz] = wd_ref[...]
    VEC[...] = jnp.zeros((8, 128), F32)
    for i, v in enumerate((v0, v1, v2, v3, v4, v5, v6, v7)):
        VEC[i : i + 1, 0 : v.shape[1]] = v[...].astype(F32)
    VB[c, f] = VEC[...]

    def gather_x(k):
        for d in range(2):
            ch = chip_of(d, k)
            for q in range(AQS):
                at = sub(d, ch, q)

                @pl.when(k > 0)
                def _():
                    remote(at, at, agx_s, ag_r.at[d, (k - 1) * AQS + q], "ctx", target(d)).wait_recv()

                @pl.when(k < 7)
                def _():
                    remote(at, at, agx_s, ag_r.at[d, k * AQS + q], "ctx", target(d)).start()

            whole = block(XF, d, ch, mine)
            remote(whole, whole, sbx_s, sbx_r, "ctx", sib).start()

    def gather_wo(k):
        for d in range(2):
            at = WO.at[chip_of(d, k), core, f, pl.ds(16 * d, 16)]

            @pl.when(k > 0)
            def _():
                remote(at, at, wo_s, wo_r.at[d, k - 1], "ctx", target(d)).wait_recv()

            @pl.when(k < 7)
            def _():
                remote(at, at, wo_s, wo_r.at[d, k], "ctx", target(d)).start()

    pl.loop(0, 1)(gather_x)
    pair(0, VEC, VB.at[c, f]).start()

    for j in range(8):
        qt = wq_ref[:, 128 * j : 128 * j + 128].astype(F32)
        kt = wq_ref[:, D + 128 * j : D + 128 * j + 128].astype(F32)
        vt = wq_ref[:, 2 * D + 128 * j : 2 * D + 128 * j + 128].astype(F32)
        for e in range(2):
            w = 2 * j + e
            qk = jnp.where(low_half, qt, pltpu.roll(kt, 64, 1)) if e == 0 else jnp.where(low_half, pltpu.roll(qt, 64, 1), kt)
            WP[w, :, 0:128] = qk.astype(BF16)
            WP[w, :, 128:256] = (vt if e == 0 else pltpu.roll(vt, 64, 1)).astype(BF16)
    WB[c, f] = WP[c]
    send_all(0, lambda to: WP.at[to], WB.at[c, f])
    for w in range(8):
        for i in range(4):
            WUS[w, :, 128 * i : 128 * (i + 1)] = wu_ref[:, 128 * (8 * i + w) : 128 * (8 * i + w + 1)]
    WU[zz, pp] = WUS[pp]
    send_plane(0, lambda to: WUS.at[to], WU.at[zz, pp])

    @pl.loop(1, 4)
    def _(k):
        gather_x(k)
        gather_wo(k - 1)

    pair(0, VB.at[c, 1 - f], VB.at[c, 1 - f]).wait_recv()
    send_all(1, lambda to: VB.at[c], VB.at[c])
    recv_all(0, WB.at[0:15, 0])
    pair(3, WB.at[:, f], WB.at[:, f]).start()
    recv_plane(0, WU.at[zz, 0:7])

    def head_weights():
        pair(3, WB.at[:, 1 - f], WB.at[:, 1 - f]).wait_recv()
        WHT[...] = WB[...].reshape(D, 256).T

    def vectors():
        recv_all(1, VB.at[0:15])
        for j in range(8):
            tiles = [VB[2 * j + q // 2, q % 2] for q in range(4)]
            total = tiles[0]
            for q in range(1, 4):
                total = total + pltpu.roll(tiles[q], 32 * q, 1)
            VF[:, 128 * j : 128 * j + 128] = total
            v1 = pltpu.roll(tiles[1], 96, 1)
            v2 = pltpu.roll(tiles[2], 64, 1)
            v3 = pltpu.roll(tiles[3], 32, 1)
            rows = (
                tiles[0] + jnp.where(lane >= 96, v1, 0.0),
                jnp.where(lane < 64, v1, 0.0) + jnp.where(lane >= 64, v2, 0.0),
                jnp.where(lane < 32, v2, 0.0) + v3,
            )
            for i in range(3):
                QBR[3 * j + i : 3 * j + i + 1, :] = rows[i][1:2, :]
        for i in range(4):
            UB[0:1, 128 * i : 128 * (i + 1)] = VB[4 * i + lax.rem(c, 4), f, 0:1, :]
        for i in range(3):
            row = QBR[pl.ds(8 * i + chip, 1), :]
            BQ[i] = jnp.broadcast_to(row, (128, 128)).T

    @pl.loop(4, 8)
    def _(k):
        gather_x(k)
        gather_wo(k - 1)
        pl.when(k == 6)(vectors)
        pl.when(k == 7)(head_weights)

        @pl.when(k == 6)
        def _():
            z_gather(0, 0)
            z_gather(1, 0)


    gather_wo(jnp.int32(7))
    pair(1, WO.at[:, core, f], WO.at[:, core, f]).start()
    z_gather(2, 0)
    z_gather(3, 0)
    remote(XF.at[0], XF.at[0], sbx_s, sbx_r, "ctx", sib).wait_recv()


    def lanes(n):
        return pl.ds(pl.multiple_of(n * CHUNK, CHUNK), CHUNK)

    def turn(u, cosine, sine):
        a, b = u[0:32], u[32:64]
        return jnp.concatenate([a * cosine - b * sine, b * cosine + a * sine], axis=0)

    def unturn(u, cosine, sine):
        a, b = u[0:32], u[32:64]
        return jnp.concatenate([a * cosine + b * sine, b * cosine - a * sine], axis=0)

    @pl.loop(0, 8)
    def _(it):
        m = lax.div(it, 4)
        n = lax.rem(it, 4)
        xs = XF[m, pl.ds(2 * n, 2)].reshape(CHUNK, D)
        joined = nt(WHT[0:192, :], xs)
        cosine = rope_ref[0, :, lanes(n)]
        sine = rope_ref[1, :, lanes(n)]
        q = joined[0:64] + BQ[0, pl.ds(mine, BLK), 0:1]
        k = joined[64:128] + BQ[1, pl.ds(mine, BLK), 0:1]
        v = joined[128:192] + BQ[2, pl.ds(mine, BLK), 0:1]
        q = turn(q, cosine, sine)
        k = turn(k, cosine, sine)
        rows = pl.ds(pl.multiple_of(n * CHUNK, CHUNK), CHUNK)
        QT[m, :, lanes(n)] = q.astype(BF16)
        KT[m, :, lanes(n)] = k.astype(BF16)
        VT[m, :, lanes(n)] = v.astype(BF16)
        KN[m, rows, :] = k.T.astype(BF16)
        VN[m, rows, :] = v.T.astype(BF16)

    @pl.loop(0, 8)
    def _(it):
        @pl.when(it == 0)
        def _():
            z_gather(0, 1)
            z_gather(1, 1)

        @pl.when(it == 4)
        def _():
            z_gather(2, 1)
            z_gather(3, 1)

        @pl.when(it == 5)
        def _():
            pair(1, WO.at[:, core, 1 - f], WO.at[:, core, 1 - f]).wait_recv()
            remote(WO.at[:, core], WO.at[:, core], wos_s, wos_r, "ctx", sib).start()

        m = lax.div(it, 4)
        n = lax.rem(it, 4)
        s = nn(KN[m], QT[m, :, lanes(n)]) * 0.125
        e = jnp.exp(s - jnp.max(s, axis=0, keepdims=True))
        p = (e * (1.0 / jnp.sum(e, axis=0, keepdims=True))).astype(BF16)
        PT[m, :, lanes(n)] = p
        ATD[m, :, lanes(n)] = nn(VT[m], p)

    for j in range(8):
        a0 = ATD[0, :, 128 * j : 128 * j + 128]
        a1 = ATD[1, :, 128 * j : 128 * j + 128]
        ATS[2 * j] = jnp.where(low_half, a0, pltpu.roll(a1, 64, 1)).astype(BF16)
        ATS[2 * j + 1] = jnp.where(low_half, pltpu.roll(a0, 64, 1), a1).astype(BF16)
    AT[c] = ATS[c]
    send_all(2, lambda to: ATS.at[to], AT.at[c])

    z_gather(0, 2)
    z_gather(1, 2)
    remote(WO.at[:, 1 - core], WO.at[:, 1 - core], wos_s, wos_r, "ctx", sib).wait_recv()
    recv_all(2, AT.at[0:15])

    z_gather(2, 2)
    z_gather(3, 2)
    att_rows = AT[...].reshape(D, 128).T
    resid = x_ref[...].reshape(128, D).astype(F32) + nn(att_rows, WO[...].reshape(D, D)) + VF[2:3, :]
    center = resid - row_mean(resid)
    root = lax.rsqrt(row_mean(center * center) + 1e-05)
    z = center * root
    hidden = z * VF[4:5, :] + VF[5:6, :]
    Z1[...] = z
    R1[...] = jnp.broadcast_to(root, (128, 128))
    H1[...] = hidden
    hidden_low = hidden.astype(BF16)
    for m in range(2):
        HF[grp, m, pl.ds(mine, BLK)] = hidden_low[m * BLK : (m + 1) * BLK]

    def plane(buf, make, early, ready, after_one, after_two, finish):
        far = ((yy * 2 + 1 - f), ((1 - yy) * 2 + f))
        groups = tuple((grp, far[m], far[1 - m], (1 - yy) * 2 + 1 - f) for m in range(2))

        def to(axis, src, dst, ss, rs):
            if axis == 0:
                return remote(src, dst, ss, rs, "fsdp", 1 - f)
            return remote(src, dst, ss, rs, "ctx", c + 2 - 4 * yy)

        def at(m, i, row0):
            return buf.at[groups[m][i], m, pl.ds(row0, BLK)]

        def hand_over(m, i):
            remote(at(m, i, mine), at(m, i, mine), pb_s, pb_r.at[m, i], "ctx", sib).start()

        def arrive(m, i, n):
            to(m, at(m, i, mine), at(m, i, mine), pa_s, pa_r.at[m, n]).wait_recv()

        def work(m, i):
            PB[m, i] = make(groups[m][i], m)
            SS[m, i] = PB[m, i, pl.ds(other, BLK)].astype(BF16)
            remote(SS.at[m, i], SR.at[m, i], ps_s, ps_r.at[m, i], "ctx", sib).start()

        def both(m, i):
            remote(at(m, i, other), at(m, i, other), pb_s, pb_r.at[m, i], "ctx", sib).wait_recv()

        def share(m, i):
            remote(SR.at[m, i], SR.at[m, i], ps_s, ps_r.at[m, i], "ctx", sib).wait_recv()
            return PB[m, i, pl.ds(mine, BLK)] + SR[m, i].astype(F32)

        def push(m, n, value, axis):
            RSD[m, n, 0:BLK] = value.astype(BF16)
            to(axis, RSD.at[m, n, pl.ds(0, BLK)], RR.at[m, n, pl.ds(0, BLK)], pr_s, pr_r.at[m, n]).start()

        def pulled(m, n):
            got = RR.at[m, n, pl.ds(0, BLK)]
            to(m, got, got, pr_s, pr_r.at[m, n]).wait_recv()
            return RR[m, n, 0:BLK].astype(F32)

        for m in range(2):
            to(m, at(m, 0, mine), at(m, 0, mine), pa_s, pa_r.at[m, 0]).start()
        for m in range(2):
            hand_over(m, 0)
            to(1 - m, at(m, 0, mine), at(m, 0, mine), pa_s, pa_r.at[m, 1]).start()
        for m in range(2):
            both(m, 0)
        if early is not None:
            for m in range(2):
                work(m, 0)
        for m in range(2):
            arrive(m, 1, 0)
            to(1 - m, at(m, 1, mine), at(m, 1, mine), pa_s, pa_r.at[m, 2]).start()
            hand_over(m, 1)
        for m in range(2):
            arrive(m, 2, 1)
            hand_over(m, 2)
        for m in range(2):
            both(m, 1)
        if early is not None:
            for m in range(2):
                work(m, 1)
        for m in range(2):
            arrive(m, 3, 2)
            hand_over(m, 3)
        for m in range(2):
            both(m, 2)
            both(m, 3)
        if ready is not None:
            ready()
        for i in (3, 2, 1, 0) if early is None else (3, 2):
            for m in range(2):
                work(m, i)
        if early is not None:
            early()
        for m in range(2):
            push(m, 1, share(m, 3), 1 - m)
        for m in range(2):
            push(m, 0, share(m, 2), 1 - m)
        after_one()
        for m in range(2):
            push(m, 2, share(m, 1) + pulled(m, 1), m)
        after_two()
        for m in range(2):
            finish(m, share(m, 0) + pulled(m, 0) + pulled(m, 2))
        remote(XF.at[0, 0:3], XF.at[0, 0:3], pa_s, sbx_r, "ctx", sib).wait_send()
        remote(XF.at[0, 0:4], XF.at[0, 0:4], pb_s, sbx_r, "ctx", sib).wait_send()
        remote(XF.at[0, 0:4], XF.at[0, 0:4], ps_s, sbx_r, "ctx", sib).wait_send()
        remote(XF.at[0, 0:3], XF.at[0, 0:3], pr_s, sbx_r, "ctx", sib).wait_send()

    def ring(make, extra, finish):
        def first(k):
            slot = 2 - lax.div(k + 7, 8) * (2 - lax.rem(k, 2))
            for d in range(2):
                ch = chip_of(d, k)
                PB[d, slot] = make(d, ch)
                SS[d, k] = PB[d, slot, pl.ds(other, BLK)].astype(BF16)
                remote(SS.at[d, k], SR.at[d, k], ss_s, ss_r.at[d, k], "ctx", sib).start()

        def sums(d, k):
            at = SR.at[d, k]
            remote(at, at, ss_s, ss_r.at[d, k], "ctx", sib).wait_recv()

        def arrived(d, q, k):
            got = RR.at[d, k, rows_of(q)]
            remote(got, got, rs_s, rs_r.at[d, k * RQS + q], "ctx", sib).wait_recv()

        def rows_of(q):
            return pl.ds(q * ROWS, ROWS if q < RQS - 1 else ROWS + 16)

        def second(k):
            slot = lax.rem(k, 2)
            for d in range(2):
                sums(d, k)
            for q in range(RQS):
                for d in range(2):
                    part = pl.ds(q * ROWS, ROWS)
                    total = PB[d, slot, pl.ds(pl.multiple_of(core * BLK + q * ROWS, ROWS), ROWS)] + SR[d, k, part].astype(F32)
                    rider = q == RQS - 1
                    if rider:
                        ride = riders(d, chip_of(d, k))

                    @pl.when(k > 1)
                    def _():
                        arrived(d, q, k - 1)
                        RSD[d, k, part] = (total + RR[d, k - 1, part].astype(F32)).astype(BF16)
                        if rider:
                            RSD[d, k, BLK : BLK + 16] = (ride + RR[d, k - 1, BLK : BLK + 16].astype(F32)).astype(BF16)

                    @pl.when(k == 1)
                    def _():
                        RSD[d, k, part] = total.astype(BF16)
                        if rider:
                            RSD[d, k, BLK : BLK + 16] = ride.astype(BF16)

                    remote(
                        RSD.at[d, k, rows_of(q)], RR.at[d, k, rows_of(q)], rs_s, rs_r.at[d, k * RQS + q],
                        "ctx", target(d),
                    ).start()

        @pl.loop(0, 9)
        def _(it):
            @pl.when(it < 8)
            def _():
                first(it)

            @pl.when(it > 1)
            def _():
                second(it - 1)

            extra(it)

        for d in range(2):
            sums(d, 0)
            for q in range(RQS):
                arrived(d, q, 7)
            finish(d, PB[d, 2, pl.ds(mine, BLK)] + SR[d, 0].astype(F32) + RR[d, 7, 0:BLK].astype(F32))

        remote(SS, SS, ss_s, sbx_r, "ctx", sib).wait_send()
        remote(RSD.at[:, 0:7], RSD.at[:, 0:7], rs_s, sbx_r, "ctx", sib).wait_send()

    def nothing():
        pass

    def up_w():
        return WU[...].reshape(D, FF_UNITS)

    def down_w():
        return WD[...].reshape(FF_UNITS, D)

    def make_up(g, m):
        u = nn(HF[g, m], up_w()) + UB[0:1, :]
        phi = 0.5 * (1.0 + lax.erf(u * 0.7071067811865476))
        a = (u * phi).astype(BF16)
        DG[g, m] = phi + u * (jnp.exp(-0.5 * u * u) * 0.3989422804014327)
        ACT[g, m] = a
        return nn(a, down_w())

    def finish_up(d, total):
        rows = slice(d * BLK, (d + 1) * BLK)
        SEC[rows, :] = H1[rows, :] + total + VF[3:4, :]

    def weights_in():
        for kd in range(4):
            z_gather(kd, 3)

    plane(HF, make_up, None, weights_in, nothing, nothing, finish_up)

    resid = SEC[...]
    center = resid - row_mean(resid)
    root = lax.rsqrt(row_mean(center * center) + 1e-05)
    z = center * root
    out_ref[...] = (z * VF[6:7, :] + VF[7:8, :]).astype(BF16).reshape(2, BLK, D)
    cot = ct_ref[...].reshape(128, D).astype(F32)
    SG[...] = jnp.zeros((8, D), F32)
    SG[4:5, :] = col_sum(cot * z)
    SG[5:6, :] = col_sum(cot)
    u = cot * VF[6:7, :]
    grad = (u - row_mean(u) - z * row_mean(u * z)) * root
    G2[...] = grad
    grad_low = grad.astype(BF16)
    SG[1:2, :] = col_sum(grad_low.astype(F32))
    for m in range(2):
        BG[grp, m, pl.ds(mine, BLK)] = grad_low[m * BLK : (m + 1) * BLK]

    def make_down(g, m):
        pg = (nt(BG[g, m], down_w()) * DG[g, m]).astype(BF16)
        PG[g, m] = pg
        return nt(pg, up_w())

    def finish_down(d, total):
        rows = slice(d * BLK, (d + 1) * BLK)
        SEC[rows, :] = G2[rows, :] + total

    def down_grads():
        TT[...] = ACT[...].reshape(1024, FF_UNITS).T
        for i in range(4):
            DWD[i] = nn(TT[128 * i : 128 * (i + 1), :], BG[...].reshape(1024, D)).astype(BF16)
        z_start(1)

    def up_grads():
        TT[...] = PG[...].reshape(1024, FF_UNITS).T
        for i in range(4):
            g = nn(TT[...], HF[:, :, :, CHUNK * i : CHUNK * (i + 1)].reshape(1024, CHUNK))
            DWU[i] = g.T.astype(BF16).reshape(8, 32, FF_UNITS)
        sums = nn(jnp.ones((8, 1024), BF16), PG[...].reshape(1024, FF_UNITS))[0:1, :]
        for i in range(8):
            SG[6:7, 128 * i : 128 * (i + 1)] = sums[:, 128 * (i // 2) : 128 * (i // 2) + 128]

    plane(BG, make_down, nothing, down_grads, nothing, up_grads, finish_down)

    hid = SEC[...]
    z = Z1[...]
    SG[2:3, :] = col_sum(hid * z)
    SG[3:4, :] = col_sum(hid)
    u = hid * VF[4:5, :]
    grad = (u - row_mean(u) - z * row_mean(u * z)) * R1[:, 0:1]
    H1[...] = grad
    proj = grad.astype(BF16)
    SG[0:1, :] = col_sum(proj.astype(F32))
    sent_all(2, ATS.at[0:15])
    ATS[...] = nt(WO[...].reshape(D, D), proj).astype(BF16).reshape(NCTX, HEAD, 128)
    AGT[c] = ATS[c]
    send_all(3, lambda to: ATS.at[to], AGT.at[c])

    for j in range(NCHIP):
        SSO[j] = nn(AT[2 * j + 1 - core], proj).astype(BF16)
    remote(SSO, SRO, po_s, po_r, "ctx", sib).start()
    pair(4, SG, SGR).start()
    for j in range(NCHIP):
        GO[j] = nn(AT[2 * j + core], proj)
    remote(SRO, SRO, po_s, po_r, "ctx", sib).wait_recv()
    for j in range(NCHIP):
        GO[j] = GO[j] + SRO[j].astype(F32)
        XSO[j] = GO[j, pl.ds(pl.multiple_of((1 - f) * 32, 32), 32)].astype(BF16)
    pair(5, XSO, XRO).start()
    recv_all(3, AGT.at[0:15])
    z_start(0)
    sent_all(3, ATS.at[0:15])

    for j in range(8):
        t0 = AGT[2 * j].astype(F32)
        t1 = AGT[2 * j + 1].astype(F32)
        AGQ[0, :, 128 * j : 128 * j + 128] = jnp.where(low_half, t0, pltpu.roll(t1, 64, 1)).astype(BF16)
        AGQ[1, :, 128 * j : 128 * j + 128] = jnp.where(low_half, pltpu.roll(t0, 64, 1), t1).astype(BF16)

    DK[...] = jnp.zeros((2, HEAD, D), F32)
    DV[...] = jnp.zeros((2, HEAD, D), F32)

    def small_push():
        pair(4, SGR, SGR).wait_recv()
        SGT[...] = SG[...] + SGR[...]
        SGT[6:7, :] = SG[6:7, :]
        SGC[c] = SGT[:, pl.ds(pl.multiple_of(chip * 128, 128), 128)]
        send_all(4, lambda to: SGT.at[:, pl.ds(pl.multiple_of(lax.div(to, 2) * 128, 128), 128)], SGC.at[c])

    def up_push():
        def put(total):
            PUS[...] = total.astype(BF16)

        z_total(0, put)
        RU[pp] = PUS[pp]
        send_plane(1, lambda to: PUS.at[to], RU.at[pp])

    @pl.loop(0, 8)
    def _(it):
        pl.when(it == 2)(small_push)
        pl.when(it == 0)(lambda: z_relay(1))
        pl.when(it == 5)(lambda: z_relay(0))
        m = lax.div(it, 4)
        n = lax.rem(it, 4)
        q = QT[m, :, lanes(n)]
        g = AGQ[m, :, lanes(n)]
        delta = jnp.sum(g.astype(F32) * ATD[m, :, lanes(n)], axis=0, keepdims=True)
        p = PT[m, :, lanes(n)]
        ds = (p.astype(F32) * (nn(VN[m], g) - delta)).astype(BF16)
        DK[m] = DK[m] + nt(q, ds)
        DV[m] = DV[m] + nt(g, p)
        dq = nn(KT[m], ds) * 0.125
        JG[m, 0:64, lanes(n)] = unturn(dq, rope_ref[0, :, lanes(n)], rope_ref[1, :, lanes(n)]).astype(BF16)

    for m in range(2):
        JG[m, 64:128, :] = unturn(DK[m] * 0.125, rope_ref[0], rope_ref[1]).astype(BF16)
        JG[m, 128:192, :] = DV[m].astype(BF16)

    def make_token(m, ch):
        jg = JG[m, :, pl.ds(pl.multiple_of(ch * 128, 128), 128)]
        return tn(jg, WHT[0:192, :])

    def finish_token(d, total):
        tg_ref[d] = H1[d * BLK : (d + 1) * BLK, :] + total
        go_ref[16 * d : 16 * d + 16, :] = riders(d, chip) + RR[d, 7, BLK : BLK + 16].astype(F32)

    def qkv_bias_rows():
        b = nt(jnp.ones((8, D), BF16), JG[0]) + nt(jnp.ones((8, D), BF16), JG[1])
        b = jnp.concatenate([b, jnp.zeros((8, 64), F32)], axis=1)
        QBP[...] = jnp.zeros((32, UNITS), F32)
        QBP[0:1, 128:256] = jnp.where(low_half, 0.0, pltpu.roll(b[0:1, 0:128], 64, 1))
        QBP[1:2, 128:256] = jnp.where(low_half, 0.0, b[0:1, 0:128])
        QBP[2:3, 128:256] = jnp.where(low_half, 0.0, pltpu.roll(b[0:1, 128:256], 64, 1))

    def qkv_grad(n):
        cols = slice(CHUNK * n, CHUNK * (n + 1))
        g = nn(JG[0], XF[0, :, :, cols].reshape(D, CHUNK)) + nn(JG[1], XF[1, :, :, cols].reshape(D, CHUNK))
        g = jnp.concatenate([g, jnp.zeros((64, CHUNK), F32)], axis=0)
        GU[4 * n : 4 * n + 4] = g.T.reshape(4, 2, 32, UNITS) + QBP[...]

    def qkv_pair():
        XSQ[...] = GU[:, 1 - f].astype(BF16)
        pair(8, XSQ, XRQ).start()

    def qkv_push():
        pair(8, XRQ, XRQ).wait_recv()
        AQ[...] = (GU[:, f] + XRQ[...].astype(F32)).astype(BF16)
        RQ[c] = AQ[c]
        send_all(6, lambda to: AQ.at[to], RQ.at[c])

    def riders(d, ch):
        return GO[ch, pl.ds(pl.multiple_of(f * 32 + 16 * d, 16), 16)] + XRO[ch, 16 * d : 16 * d + 16].astype(F32)

    def small_rest():
        recv_all(4, SGC.at[0:15])
        total = SGC[0]
        for w in range(1, NCTX):
            total = total + SGC[w]
        gs_ref[...] = total
        here = lax.rem(c, 4)
        gs_ref[6:7, :] = SGC[here, 6:7, :] + SGC[4 + here, 6:7, :] + SGC[8 + here, 6:7, :] + SGC[12 + here, 6:7, :]

    def down_rest():
        def put(total):
            gd_ref[...] = total

        z_total(1, put)

    def on_the_way(it):
        pl.when(it == 0)(qkv_bias_rows)
        for n in range(4):
            pl.when(it == n)(partial(qkv_grad, n))
        pl.when(it == 3)(qkv_pair)
        pl.when(it == 4)(small_rest)
        pl.when(it == 5)(qkv_push)
        pl.when(it == 6)(down_rest)
        pl.when(it == 8)(up_push)

    pair(5, XRO, XRO).wait_recv()
    ring(make_token, on_the_way, finish_token)
    recv_plane(1, RU.at[0:7])
    recv_all(6, RQ.at[0:15])

    remote(XF.at[0, 0:7], XF.at[0, 0:7], agx_s, sbx_r, "ctx", sib).wait_send()
    remote(XF.at[0], XF.at[0], sbx_s, sbx_r, "ctx", sib).wait_send()
    remote(WO.at[0:7, 0, 0], WO.at[0:7, 0, 0], wo_s, sbx_r, "ctx", sib).wait_send()
    remote(WO.at[:, 0], WO.at[:, 0], wos_s, sbx_r, "ctx", sib).wait_send()
    sent_all(0, WP.at[0:15])
    sent_all(1, VB.at[0:15])
    sent_all(4, SGC.at[0:15])
    sent_all(6, AQ.at[0:15])
    remote(SSO, SSO, po_s, po_r, "ctx", sib).wait_send()
    sent_plane(0, WUS.at[0:7])
    sent_plane(1, PUS.at[0:7])
    for kd in range(2):
        for s in range(3):
            z_gather(kd, s, True)
            z_gather(kd + 2, s, True)
        z_start(kd, True)
        z_relay(kd, True)
    for i, at in ((0, VEC), (1, WO.at[:, core, f]), (3, WB.at[:, f]), (4, SG), (5, XSO), (8, XSQ)):
        pair(i, at, at).wait_send()


def rope_tables():
    freqs = (np.float32(10000.0) ** (-np.arange(0, HEAD, 2, dtype=np.float32) / np.float32(HEAD))).astype(np.float32)
    angles = freqs[:, None] * np.arange(1024, dtype=np.float32)[None, :]
    return np.stack([np.cos(angles), np.sin(angles)]).astype(np.float32)


def fused_body(
    tokens, cotangent, qkv_weight, out_weight, up_weight, down_weight, qkv_bias, out_bias, up_bias, down_bias,
    first_gain, first_shift, second_gain, second_shift,
):
    scratch = [
        ((8, 128), F32),
        ((2, 8, 128, D), BF16), ((4, 2, 128, D), BF16), ((4, 2, 128, D), BF16),
        ((16, 32, 256), BF16), ((16, 2, 32, 256), BF16), ((8, 32, FF_UNITS), BF16), ((4, 8, 32, FF_UNITS), BF16),
        ((8, 2, 2, 32, D), BF16), ((4, 128, D), BF16),
        ((16, 2, 8, 128), F32), ((8, D), F32), ((8, FF_UNITS), F32), ((24, 128), F32), ((3, 128, 128), F32),
        ((256, D), BF16),
        ((2, 64, D), BF16), ((2, 64, D), BF16), ((2, 64, D), BF16), ((2, D, 64), BF16), ((2, D, 64), BF16),
        ((2, D, D), BF16), ((2, 64, D), F32),
        ((16, 64, 128), BF16), ((16, 64, 128), BF16), ((16, 64, 128), BF16),
        ((128, D), F32), ((128, D), F32), ((128, 128), F32), ((128, D), F32), ((128, D), F32),
        ((4, 2, 128, FF_UNITS), F32), ((4, 2, 128, FF_UNITS), BF16), ((4, 2, 128, FF_UNITS), BF16),
        ((2, 4, 128, D), F32),
        ((2, 8, BLK, D), BF16), ((2, 8, BLK, D), BF16), ((2, 8, 80, D), BF16), ((2, 8, 80, D), BF16),
        ((FF_UNITS, 1024), BF16),
        ((16, 2, 32, UNITS), F32), ((8, 32, FF_UNITS), BF16),
        ((4, 8, 32, FF_UNITS), BF16), ((4, 128, D), BF16), ((4, 8, 32, FF_UNITS), BF16), ((4, 128, D), BF16),
        ((8, BLK, D), F32), ((8, 32, D), BF16), ((8, 32, D), BF16), ((8, BLK, D), BF16), ((8, BLK, D), BF16),
        ((8, D), F32), ((8, D), F32), ((8, D), F32), ((16, 8, 128), F32), ((2, 64, D), BF16),
        ((2, 64, D), F32), ((2, 64, D), F32), ((2, 192, D), BF16),
        ((16, 32, UNITS), BF16), ((16, 32, UNITS), BF16), ((16, 32, UNITS), BF16), ((32, UNITS), F32),
    ]
    sems = [(14,), (2, 8 * AQS), (2, 8), (2, 8 * RQS), (2, 8), (9,), (9,), (11,), (11,), (2,), (2,)]
    sems += [(2, 3), (2, 4), (2, 4), (2, 3), (4, 6), (4, 4), (2, 4), (2, 4)]
    vmem = pl.BlockSpec(memory_space=pltpu.VMEM)
    shapes = [((2, BLK, D), BF16), ((2, BLK, D), F32), ((16, 32, UNITS), BF16), ((32, D), F32), ((8, 32, FF_UNITS), BF16), ((128, D), F32), ((8, 128), F32)]
    final = shapes[:2] + [((32, 3 * D), F32), shapes[3], ((32, 4 * D), F32), shapes[5]]
    bias = (up_bias, qkv_bias, out_bias, down_bias, first_gain, first_shift, second_gain, second_shift)
    made = pl.pallas_call(
        layer_kernel,
        out_shape=[jax.ShapeDtypeStruct(s, t) for s, t in shapes],
        in_specs=[vmem] * 15,
        out_specs=[vmem] * 7,
        scratch_shapes=[pltpu.VMEM(s, t) for s, t in scratch] + [pltpu.SemaphoreType.DMA(s) for s in sems],
        compiler_params=pltpu.CompilerParams(collective_id=0, has_side_effects=True, vmem_limit_bytes=VMEM_LIMIT),
        name="layer",
    )(
        tokens[:, 0], cotangent[:, 0], qkv_weight, out_weight, up_weight, down_weight, jnp.asarray(rope_tables()),
        *(v[None] for v in bias),
    )
    anywhere = pl.BlockSpec(memory_space=pl.ANY)
    widths = (96, 32, 128, 32, 32, 32, 32, 32)
    last = pl.pallas_call(
        finish_kernel,
        out_shape=[jax.ShapeDtypeStruct(s, t) for s, t in final] + [jax.ShapeDtypeStruct((1, w), F32) for w in widths],
        in_specs=[anywhere, anywhere, vmem, anywhere, vmem, anywhere, vmem],
        out_specs=[vmem] * 14,
        scratch_shapes=[pltpu.VMEM((24, 128), F32), pltpu.SemaphoreType.DMA((4,))],
        name="finish",
    )(*made)
    return (last[0][:, None], last[1][:, None], *last[2:6], *(v[0] for v in last[6:]))


def finish_kernel(*refs):
    (out, tg, rq, go, ru, gd, gs), done, small, (gb, sems) = refs[:7], refs[7:13], refs[13:21], refs[21:]
    pairs = ((out, done[0]), (tg, done[1]), (go, done[3]), (gd, done[5]))
    copies = [pltpu.make_async_copy(a, b, sems.at[i]) for i, (a, b) in enumerate(pairs)]
    for copy in copies:
        copy.start()
    gq, gu = done[2], done[4]
    low_half = lax.broadcasted_iota(jnp.int32, (1, 128), 1) < 64
    for j in range(8):
        a = rq[2 * j].astype(F32)
        b = rq[2 * j + 1].astype(F32)
        a0, a1, b0, b1 = a[:, 0:128], a[:, 128:256], b[:, 0:128], b[:, 128:256]
        v = pltpu.roll(b1, 64, 1)
        gq[:, 128 * j : 128 * (j + 1)] = jnp.where(low_half, a0, pltpu.roll(b0, 64, 1))
        gq[:, D + 128 * j : D + 128 * (j + 1)] = jnp.where(low_half, pltpu.roll(a0, 64, 1), b0)
        gq[:, 2 * D + 128 * j : 2 * D + 128 * (j + 1)] = jnp.where(low_half, a1, v)
        bias = jnp.where(low_half, pltpu.roll(a1, 64, 1), b1)
        for i in range(3):
            gb[8 * i + j : 8 * i + j + 1, :] = bias[i : i + 1, :]
    for w in range(8):
        for i in range(4):
            gu[:, 128 * (8 * i + w) : 128 * (8 * i + w + 1)] = ru[w, :, 128 * i : 128 * (i + 1)].astype(F32)
    index = lax.axis_index("ctx") * 2 + lax.axis_index("fsdp")
    place = lax.rem(index, 4)
    turned = pltpu.roll(gs[...], lax.rem(128 - 32 * place, 128), 1)
    for ref, row in zip(small[1:], (0, 6, 1, 2, 3, 4, 5)):
        ref[...] = gs[6:7, :] if row == 6 else turned[row : row + 1, 0:32]
    offset = lax.rem(96 * index, 128)
    row = lax.div(96 * index, 128)
    lane = lax.broadcasted_iota(jnp.int32, (1, 128), 1)
    back = lax.rem(128 - offset, 128)
    one = pltpu.roll(gb[pl.ds(row, 1), :], back, 1)
    two = pltpu.roll(gb[pl.ds(lax.rem(row + 1, 24), 1), :], back, 1)
    small[0][...] = jnp.where(lane < 128 - offset, one, two)[:, 0:96]
    for copy in copies:
        copy.wait()


VMEM_LIMIT = 63 * 1024 * 1024


def layernorm(resid, gain, shift):
    center = resid - jnp.mean(resid, axis=-1, keepdims=True)
    spread = jnp.mean(center * center, axis=-1, keepdims=True)
    return center * lax.rsqrt(spread + 1e-05) * gain + shift


def tables(position):
    freqs = 10000.0 ** (-jnp.arange(0, HEAD, 2, dtype=jnp.float32) / HEAD)
    angles = position[:, None] * freqs[None, :]
    return (jnp.cos(angles)[:, None, :], jnp.sin(angles)[:, None, :])


def rotate(heads_in, cosine, sine):
    middle = heads_in.shape[-1] // 2
    first = heads_in[..., :middle]
    second = heads_in[..., middle:]
    return jnp.concatenate(
        [first * cosine - second * sine, second * cosine + first * sine], axis=-1
    )


def unrotate(heads_in, cosine, sine):
    middle = heads_in.shape[-1] // 2
    first = heads_in[..., :middle]
    second = heads_in[..., middle:]
    return jnp.concatenate(
        [first * cosine + second * sine, second * cosine - first * sine], axis=-1
    )


def split_heads(flat_rows):
    return flat_rows.reshape(flat_rows.shape[0], HEADS, HEAD)


def over_blocks(update, carried, count, limit):
    size = math.gcd(count, limit)

    def advance(block_idx, state):
        return update(state, block_idx * size, size)

    return lax.fori_loop(0, count // size, advance, carried)


def column_sum(matrix):
    return jnp.sum(matrix.astype(jnp.float32), axis=0)


def forward_local(sequence, weights_now, cosine, sine, group):
    (
        qkv_full,
        out_full,
        up_full,
        down_full,
        qkv_vector,
        out_vector,
        up_vector,
        down_vector,
        gain_first,
        shift_first,
        gain_second,
        shift_second,
    ) = weights_now
    rows = sequence.shape[0]
    width = sequence.shape[1]
    joined = jnp.dot(sequence, qkv_full, preferred_element_type=jnp.float32) + qkv_vector.astype(
        jnp.float32
    )
    query_flat = (
        rotate(split_heads(joined[:, :width]), cosine, sine)
        .astype(jnp.bfloat16)
        .reshape(rows, width)
    )
    keys_flat = (
        rotate(split_heads(joined[:, width : 2 * width]), cosine, sine)
        .astype(jnp.bfloat16)
        .reshape(rows, width)
    )
    values_flat = joined[:, 2 * width :].astype(jnp.bfloat16)
    query_heads = split_heads(query_flat)
    start_state = (
        jnp.full((HEADS, rows), -1e30, jnp.float32),
        jnp.zeros((HEADS, rows), jnp.float32),
        jnp.zeros((rows, HEADS, HEAD), jnp.float32),
    )
    keys_piece = lax.all_gather(keys_flat, "ctx", axis=0, tiled=True)
    values_piece = lax.all_gather(values_flat, "ctx", axis=0, tiled=True)

    def absorb_block(state, offset, size):
        running, total, accum = state
        key_block = split_heads(lax.dynamic_slice_in_dim(keys_piece, offset, size, 0))
        value_block = split_heads(lax.dynamic_slice_in_dim(values_piece, offset, size, 0))
        scores = (
            jnp.einsum("qhd,khd->hqk", query_heads, key_block, preferred_element_type=jnp.float32)
            * 0.125
        )
        highest_new = jnp.maximum(running, jnp.max(scores, axis=-1))
        factor = jnp.exp(running - highest_new)
        expo = jnp.exp(scores - highest_new[:, :, None])
        total = total * factor + jnp.sum(expo, axis=-1)
        accum = accum * factor.T[:, :, None] + jnp.einsum(
            "hqk,khd->qhd",
            expo.astype(jnp.bfloat16),
            value_block,
            preferred_element_type=jnp.float32,
        )
        return (highest_new, total, accum)

    running, total, accum = over_blocks(absorb_block, start_state, keys_piece.shape[0], group)
    attended = accum / total.T[:, :, None]
    logsum = running + jnp.log(total)
    att_low = attended.reshape(rows, width).astype(jnp.bfloat16)
    projected = jnp.dot(att_low, out_full, preferred_element_type=jnp.float32) + out_vector.astype(
        jnp.float32
    )
    resid_first = sequence.astype(jnp.float32) + projected
    hidden = layernorm(resid_first, gain_first.astype(jnp.float32), shift_first.astype(jnp.float32))
    hidden_low = hidden.astype(jnp.bfloat16)
    preact = jnp.dot(hidden_low, up_full, preferred_element_type=jnp.float32) + up_vector.astype(
        jnp.float32
    )
    activ_low = jax.nn.gelu(preact, approximate=False).astype(jnp.bfloat16)
    branch = jnp.dot(activ_low, down_full, preferred_element_type=jnp.float32) + down_vector.astype(
        jnp.float32
    )
    resid_second = hidden + branch
    output = layernorm(
        resid_second, gain_second.astype(jnp.float32), shift_second.astype(jnp.float32)
    )
    saved = (
        query_flat,
        keys_flat,
        values_flat,
        attended,
        logsum,
        att_low,
        resid_first,
        hidden_low,
        preact,
        activ_low,
        resid_second,
    )
    return (output.astype(jnp.bfloat16), saved)


def body(
    tokens,
    cotangent,
    qkv_weight,
    out_weight,
    up_weight,
    down_weight,
    qkv_bias,
    out_bias,
    up_bias,
    down_bias,
    first_gain,
    first_shift,
    second_gain,
    second_shift,
):
    gathered = (
        lax.all_gather(qkv_weight, ("ctx", "fsdp"), axis=0, tiled=True),
        lax.all_gather(out_weight, ("ctx", "fsdp"), axis=0, tiled=True),
        lax.all_gather(up_weight, ("ctx", "fsdp"), axis=0, tiled=True),
        lax.all_gather(down_weight, ("ctx", "fsdp"), axis=0, tiled=True),
        lax.all_gather(qkv_bias, ("ctx", "fsdp"), axis=0, tiled=True),
        lax.all_gather(out_bias, ("ctx", "fsdp"), axis=0, tiled=True),
        lax.all_gather(up_bias, ("ctx", "fsdp"), axis=0, tiled=True),
        lax.all_gather(down_bias, ("ctx", "fsdp"), axis=0, tiled=True),
        lax.all_gather(first_gain, ("ctx", "fsdp"), axis=0, tiled=True),
        lax.all_gather(first_shift, ("ctx", "fsdp"), axis=0, tiled=True),
        lax.all_gather(second_gain, ("ctx", "fsdp"), axis=0, tiled=True),
        lax.all_gather(second_shift, ("ctx", "fsdp"), axis=0, tiled=True),
    )
    rows = tokens.shape[2]
    width = tokens.shape[3]
    cycle_size = lax.axis_size("ctx")
    group = rows * math.gcd(cycle_size, 8)
    length = rows * cycle_size
    position = (lax.axis_index("ctx") * rows + jnp.arange(rows)).astype(jnp.float32)
    cosine, sine = tables(position)
    outputs = []
    savings = []
    for micro_idx in range(MICRO):
        output, saved = forward_local(tokens[micro_idx, 0], gathered, cosine, sine, group)
        outputs.append(output)
        savings.append(saved)
    weights_back = (
        lax.all_gather(qkv_weight, ("ctx", "fsdp"), axis=0, tiled=True),
        lax.all_gather(out_weight, ("ctx", "fsdp"), axis=0, tiled=True),
        lax.all_gather(up_weight, ("ctx", "fsdp"), axis=0, tiled=True),
        lax.all_gather(down_weight, ("ctx", "fsdp"), axis=0, tiled=True),
        lax.all_gather(qkv_bias, ("ctx", "fsdp"), axis=0, tiled=True),
        lax.all_gather(out_bias, ("ctx", "fsdp"), axis=0, tiled=True),
        lax.all_gather(up_bias, ("ctx", "fsdp"), axis=0, tiled=True),
        lax.all_gather(down_bias, ("ctx", "fsdp"), axis=0, tiled=True),
        lax.all_gather(first_gain, ("ctx", "fsdp"), axis=0, tiled=True),
        lax.all_gather(first_shift, ("ctx", "fsdp"), axis=0, tiled=True),
        lax.all_gather(second_gain, ("ctx", "fsdp"), axis=0, tiled=True),
        lax.all_gather(second_shift, ("ctx", "fsdp"), axis=0, tiled=True),
    )
    (
        qkv_full,
        out_full,
        up_full,
        down_full,
        qkv_vector,
        out_vector,
        up_vector,
        down_vector,
        gain_first,
        shift_first,
        gain_second,
        shift_second,
    ) = weights_back
    token_grads = []
    totals = []
    for micro_idx in range(MICRO):
        (
            query_flat,
            keys_flat,
            values_flat,
            attended,
            logsum,
            att_low,
            resid_first,
            hidden_low,
            preact,
            activ_low,
            resid_second,
        ) = savings[micro_idx]
        sequence = tokens[micro_idx, 0]
        grad_out = cotangent[micro_idx, 0].astype(jnp.float32)
        unused_two, second_back = jax.vjp(
            layernorm,
            resid_second,
            gain_second.astype(jnp.float32),
            shift_second.astype(jnp.float32),
        )
        grad_second, second_gain_grad, second_shift_grad = second_back(grad_out)
        branch_grad = grad_second.astype(jnp.bfloat16)
        down_bias_grad = column_sum(branch_grad)
        down_weight_grad = jnp.einsum(
            "tf,td->fd", activ_low, branch_grad, preferred_element_type=jnp.float32
        )
        activ_grad = jnp.einsum(
            "td,fd->tf", branch_grad, down_full, preferred_element_type=jnp.float32
        )
        unused_gelu, gelu_back = jax.vjp(partial(jax.nn.gelu, approximate=False), preact)
        preact_grad = gelu_back(activ_grad)[0].astype(jnp.bfloat16)
        up_bias_grad = column_sum(preact_grad)
        up_weight_grad = jnp.einsum(
            "td,tf->df", hidden_low, preact_grad, preferred_element_type=jnp.float32
        )
        hidden_grad = grad_second + jnp.einsum(
            "tf,df->td", preact_grad, up_full, preferred_element_type=jnp.float32
        )
        unused_one, first_back = jax.vjp(
            layernorm, resid_first, gain_first.astype(jnp.float32), shift_first.astype(jnp.float32)
        )
        grad_first, first_gain_grad, first_shift_grad = first_back(hidden_grad)
        proj_grad = grad_first.astype(jnp.bfloat16)
        out_bias_grad = column_sum(proj_grad)
        out_weight_grad = jnp.einsum(
            "tc,te->ce", att_low, proj_grad, preferred_element_type=jnp.float32
        )
        att_grad = jnp.einsum(
            "te,ce->tc", proj_grad, out_full, preferred_element_type=jnp.float32
        ).astype(jnp.bfloat16)
        att_heads = split_heads(att_grad)
        query_heads = split_heads(query_flat)
        delta = jnp.sum(att_heads.astype(jnp.float32) * attended, axis=-1).T
        key_all, value_all = (
            lax.all_gather(keys_flat, "ctx", axis=0, tiled=True),
            lax.all_gather(values_flat, "ctx", axis=0, tiled=True),
        )

        def query_update(state, offset, size):
            key_block = split_heads(lax.dynamic_slice_in_dim(key_all, offset, size, 0))
            value_block = split_heads(lax.dynamic_slice_in_dim(value_all, offset, size, 0))
            scores = (
                jnp.einsum(
                    "qhd,khd->hqk", query_heads, key_block, preferred_element_type=jnp.float32
                )
                * 0.125
            )
            chance = jnp.exp(scores - logsum[:, :, None])
            dprob = jnp.einsum(
                "qhd,khd->hqk", att_heads, value_block, preferred_element_type=jnp.float32
            )
            score_grad = (chance * (dprob - delta[:, :, None])).astype(jnp.bfloat16)
            return state + jnp.einsum(
                "hqk,khd->qhd", score_grad, key_block, preferred_element_type=jnp.float32
            )

        query_grad = (
            over_blocks(query_update, jnp.zeros((rows, HEADS, HEAD), jnp.float32), length, group)
            * 0.125
        )

        def fill(state, offset, size):
            key_block = split_heads(lax.dynamic_slice_in_dim(key_all, offset, size, 0))
            value_block = split_heads(lax.dynamic_slice_in_dim(value_all, offset, size, 0))
            scores = (
                jnp.einsum(
                    "qhd,khd->hqk", query_heads, key_block, preferred_element_type=jnp.float32
                )
                * 0.125
            )
            chance = jnp.exp(scores - logsum[:, :, None])
            value_part = jnp.einsum(
                "hqk,qhd->khd",
                chance.astype(jnp.bfloat16),
                att_heads,
                preferred_element_type=jnp.float32,
            )
            dprob = jnp.einsum(
                "qhd,khd->hqk", att_heads, value_block, preferred_element_type=jnp.float32
            )
            score_grad = (chance * (dprob - delta[:, :, None])).astype(jnp.bfloat16)
            key_part = (
                jnp.einsum(
                    "hqk,qhd->khd", score_grad, query_heads, preferred_element_type=jnp.float32
                )
                * 0.125
            )
            piece = jnp.concatenate(
                [key_part.reshape(size, width), value_part.reshape(size, width)], axis=1
            )
            return lax.dynamic_update_slice_in_dim(state, piece, offset, 0)

        combined = lax.psum_scatter(
            over_blocks(
                fill,
                jnp.zeros((lax.axis_size("ctx") * rows, 2 * width), jnp.float32),
                lax.axis_size("ctx") * rows,
                group,
            ),
            "ctx",
            scatter_dimension=0,
            tiled=True,
        )
        key_grad = split_heads(combined[:, :width])
        value_grad = combined[:, width:]
        joined_grad = jnp.concatenate(
            [
                unrotate(query_grad, cosine, sine).reshape(rows, width),
                unrotate(key_grad, cosine, sine).reshape(rows, width),
                value_grad,
            ],
            axis=1,
        ).astype(jnp.bfloat16)
        qkv_bias_grad = column_sum(joined_grad)
        qkv_weight_grad = jnp.einsum(
            "tc,te->ce", sequence, joined_grad, preferred_element_type=jnp.float32
        )
        token_grads.append(
            grad_first
            + jnp.einsum("te,ce->tc", joined_grad, qkv_full, preferred_element_type=jnp.float32)
        )
        fresh = [
            qkv_weight_grad,
            out_weight_grad,
            up_weight_grad,
            down_weight_grad,
            qkv_bias_grad,
            out_bias_grad,
            up_bias_grad,
            down_bias_grad,
            first_gain_grad,
            first_shift_grad,
            second_gain_grad,
            second_shift_grad,
        ]
        if micro_idx == 0:
            totals = fresh
        else:
            totals = [older + newer for older, newer in zip(totals, fresh)]
    summed = (
        lax.psum_scatter(totals[0], ("ctx", "fsdp"), scatter_dimension=0, tiled=True),
        lax.psum_scatter(totals[1], ("ctx", "fsdp"), scatter_dimension=0, tiled=True),
        lax.psum_scatter(totals[2], ("ctx", "fsdp"), scatter_dimension=0, tiled=True),
        lax.psum_scatter(totals[3], ("ctx", "fsdp"), scatter_dimension=0, tiled=True),
        lax.psum_scatter(totals[4], ("ctx", "fsdp"), scatter_dimension=0, tiled=True),
        lax.psum_scatter(totals[5], ("ctx", "fsdp"), scatter_dimension=0, tiled=True),
        lax.psum_scatter(totals[6], ("ctx", "fsdp"), scatter_dimension=0, tiled=True),
        lax.psum_scatter(totals[7], ("ctx", "fsdp"), scatter_dimension=0, tiled=True),
        lax.psum_scatter(totals[8], ("ctx", "fsdp"), scatter_dimension=0, tiled=True),
        lax.psum_scatter(totals[9], ("ctx", "fsdp"), scatter_dimension=0, tiled=True),
        lax.psum_scatter(totals[10], ("ctx", "fsdp"), scatter_dimension=0, tiled=True),
        lax.psum_scatter(totals[11], ("ctx", "fsdp"), scatter_dimension=0, tiled=True),
    )
    output_all = jnp.stack(outputs)[:, None]
    token_all = jnp.stack(token_grads)[:, None]
    return (
        output_all,
        token_all,
        summed[0],
        summed[1],
        summed[2],
        summed[3],
        summed[4],
        summed[5],
        summed[6],
        summed[7],
        summed[8],
        summed[9],
        summed[10],
        summed[11],
    )


def solution(mesh):
    in_specs = (
        P(None, "fsdp", "ctx", None),
        P(None, "fsdp", "ctx", None),
        P(("ctx", "fsdp"), None),
        P(("ctx", "fsdp"), None),
        P(("ctx", "fsdp"), None),
        P(("ctx", "fsdp"), None),
        P(("ctx", "fsdp")),
        P(("ctx", "fsdp")),
        P(("ctx", "fsdp")),
        P(("ctx", "fsdp")),
        P(("ctx", "fsdp")),
        P(("ctx", "fsdp")),
        P(("ctx", "fsdp")),
        P(("ctx", "fsdp")),
    )
    out_specs = (
        P(None, "fsdp", "ctx", None),
        P(None, "fsdp", "ctx", None),
        P(("ctx", "fsdp"), None),
        P(("ctx", "fsdp"), None),
        P(("ctx", "fsdp"), None),
        P(("ctx", "fsdp"), None),
        P(("ctx", "fsdp")),
        P(("ctx", "fsdp")),
        P(("ctx", "fsdp")),
        P(("ctx", "fsdp")),
        P(("ctx", "fsdp")),
        P(("ctx", "fsdp")),
        P(("ctx", "fsdp")),
        P(("ctx", "fsdp")),
    )
    fused = mesh.shape["ctx"] == NCTX and mesh.shape["fsdp"] == 2
    return jax.shard_map(fused_body if fused else body, mesh=mesh, in_specs=in_specs, out_specs=out_specs, check_vma=False)
```

```python
from functools import partial
import math

import jax
import jax.numpy as jnp
from jax import lax
from jax.experimental import pallas as pl
from jax.experimental.pallas import tpu as pltpu
from jax.sharding import PartitionSpec as P
import numpy as np

HEADS = 16
HEAD = 64
MICRO = 2
MESH = pl.DeviceIdType.MESH
F32 = jnp.float32
BF16 = jnp.bfloat16


NCTX = 16
NCHIP = 8
BLK = 64
D = 1024
UNITS = 256
FF_UNITS = 512
CHUNK = 256
AQS = 4
RQS = 4
ROWS = BLK // RQS


def chip_at(place):
    row = lax.div(place, 4)
    return ((1 - row) * place + row * (7 - place)) * 2 + row


def nn(a, b):
    return jnp.dot(a, b, preferred_element_type=F32)


def nt(a, b):
    return lax.dot_general(a, b, (((1,), (1,)), ((), ())), preferred_element_type=F32)


def tn(a, b):
    return lax.dot_general(a, b, (((0,), (0,)), ((), ())), preferred_element_type=F32)


def row_mean(v):
    return jnp.sum(v, axis=1, keepdims=True) * (1.0 / D)


def col_sum(v):
    return jnp.sum(v, axis=0, keepdims=True)


def layer_kernel(
    x_ref, ct_ref, wq_ref, wo_ref, wu_ref, wd_ref, rope_ref, v0, v1, v2, v3, v4, v5, v6, v7,
    out_ref, tg_ref, RQ, go_ref, RU, gd_ref, gs_ref,
    VEC, XF, HF, BG, WP, WB, WUS, WU, WO, WD, VB, VF, UB, QBR, BQ, WHT, QT, KT, VT, KN, VN, PT, ATD, ATS, AT, AGT,
    H1, Z1, R1, SEC, G2, DG, ACT, PG, PB, SS, SR, RSD, RR, TT,
    GU, PUS, DWU, DWD, ZRU, ZRD, GO, XSO, XRO, SSO, SRO, SG, SGR, SGT, SGC, AGQ,
    DK, DV, JG, XSQ, XRQ, AQ, QBP,
    one, ag_r, ss_r, rs_r, wo_r, all_s, all_r, pair_s, pair_r, plane_s, plane_r,
    pa_r, pb_r, ps_r, pr_r, z_s, z_r, q_s, q_r,
):
    c = lax.axis_index("ctx")
    f = lax.axis_index("fsdp")
    core = lax.rem(c, 2)
    chip = lax.div(c, 2)
    yy = lax.rem(chip, 2)
    zz = lax.div(chip, 2)
    r = (1 - yy) * zz + yy * (7 - zz)
    nxt = chip_at(lax.rem(r + 1, 8)) * 2 + core
    prv = chip_at(lax.rem(r + 7, 8)) * 2 + core
    sib = c + 1 - 2 * core
    mine = pl.multiple_of(core * BLK, BLK)
    other = pl.multiple_of((1 - core) * BLK, BLK)
    lane = lax.broadcasted_iota(jnp.int32, (1, 128), 1)
    low_half = lane < 64

    def remote(src, dst, ss, rs, axis, to):
        return pltpu.make_async_remote_copy(
            src_ref=src, dst_ref=dst, send_sem=ss, recv_sem=rs, device_id={axis: to}, device_id_type=MESH
        )

    def target(d):
        return nxt if d == 0 else prv

    def chip_of(d, k):
        return chip_at(lax.rem(r - k + 8, 8) if d == 0 else lax.rem(r + k, 8))

    def send_all(e, src_at, dst):
        @pl.loop(1, NCTX)
        def _(o):
            to = lax.rem(c + o, NCTX)
            remote(src_at(to), dst, all_s.at[e], all_r.at[e], "ctx", to).start()

    def recv_all(e, slab):
        remote(slab, slab, all_s.at[e], all_r.at[e], "ctx", sib).wait_recv()

    def sent_all(e, slab):
        remote(slab, slab, all_s.at[e], all_r.at[e], "ctx", sib).wait_send()

    pp = lax.rem(c, 4) * 2 + f
    grp = yy * 2 + f

    def send_plane(e, src_at, dst):
        @pl.loop(1, 8)
        def _(o):
            to = lax.rem(pp + o, 8)
            pltpu.make_async_remote_copy(
                src_ref=src_at(to), dst_ref=dst, send_sem=plane_s.at[e], recv_sem=plane_r.at[e],
                device_id={"ctx": zz * 4 + lax.div(to, 2), "fsdp": lax.rem(to, 2)}, device_id_type=MESH,
            ).start()

    def recv_plane(e, slab):
        remote(slab, slab, plane_s.at[e], plane_r.at[e], "ctx", sib).wait_recv()

    def sent_plane(e, slab):
        remote(slab, slab, plane_s.at[e], plane_r.at[e], "ctx", sib).wait_send()

    def at_plane(body):
        for place in range(4):

            @pl.when(zz == place)
            def _():
                body(place)

    def z_block(kd, b, dr, s, place):
        at = WU.at[b, pl.ds(4 * kd, 4)] if kd < 2 else WD.at[b, pl.ds(64 * kd - 128, 64)]
        return remote(at, at, z_s.at[kd, dr * 3 + s], z_r.at[kd, b], "ctx", c + (4 if dr == 0 else -4))

    def z_gather(kd, s, sent=False):
        def body(place):
            for dr in range(2):
                b = place - s if dr == 0 else place + s
                more = place < 3 if dr == 0 else place > 0
                if not 0 <= b < 4:
                    continue
                if s > 0 and not sent:
                    z_block(kd, b, dr, s - 1, place).wait_recv()
                if s < 3 and more:
                    copy = z_block(kd, b, dr, s, place)
                    copy.wait_send() if sent else copy.start()

        at_plane(body)

    def z_slot(source, t):
        return (source - t) % 4 - 1

    def z_term(kd, t, there, slot, place):
        src, got = ((DWU, ZRU), (DWD, ZRD))[kd]
        return remote(src.at[t], got.at[slot], q_s.at[kd, t], q_r.at[kd, slot], "ctx", c + 4 * (there - place))

    def z_start(kd, sent=False):
        def body(place):
            for t in (3, 2, 1, 0) if place < 2 else (0, 1, 2, 3):
                if t == place or (place, t) in ((1, 3), (2, 0)):
                    continue
                far = (place, t) in ((0, 3), (3, 0))
                there = (1 if place == 0 else 2) if far else t
                copy = z_term(kd, t, there, 3 if far else z_slot(place, t), place)
                copy.wait_send() if sent else copy.start()

        at_plane(body)

    def z_relay(kd, sent=False):
        def body(place):
            if place in (1, 2):
                t = 3 if place == 1 else 0
                src, got = ((DWU, ZRU), (DWD, ZRD))[kd]
                copy = z_term(kd, t, t, z_slot(place, t), place)
                if sent:
                    copy.wait_send()
                else:
                    z_term(kd, t, t, 3, place).wait_recv()
                    src[t] = (src[t].astype(F32) + got[3].astype(F32)).astype(BF16)
                    copy.start()

        at_plane(body)

    def z_total(kd, put):
        def body(place):
            src, got = ((DWU, ZRU), (DWD, ZRD))[kd]
            total = src[place].astype(F32)
            for source in range(4):
                if source != place and (source, place) not in ((0, 3), (3, 0)):
                    slot = z_slot(source, place)
                    z_term(kd, place, place, slot, place).wait_recv()
                    total = total + got[slot].astype(F32)
            put(total)

        at_plane(body)

    def pair(i, src, dst):
        return remote(src, dst, pair_s.at[i], pair_r.at[i], "fsdp", 1 - f)

    agx_s, sbx_s, sbx_r, ss_s, rs_s, wo_s, wos_s, wos_r, po_s, po_r, pa_s, pb_s, ps_s, pr_s = (one.at[i] for i in range(14))
    barrier = pltpu.get_barrier_semaphore()

    @pl.loop(1, NCTX)
    def _(o):
        pl.semaphore_signal(barrier, inc=1, device_id={"ctx": lax.rem(c + o, NCTX)}, device_id_type=MESH)

    @pl.loop(0, 4)
    def _(o):
        there = lax.div(c, 4) * 4 + lax.rem(c + o, 4)
        pl.semaphore_signal(barrier, inc=1, device_id={"ctx": there, "fsdp": 1 - f}, device_id_type=MESH)

    pl.semaphore_wait(barrier, NCTX + 3)

    def block(buf, m, ch, row0):
        return buf.at[m, ch, pl.ds(row0, BLK)]

    def sub(m, ch, q):
        return XF.at[m, ch, pl.ds(pl.multiple_of(core * BLK + (BLK // AQS) * q, BLK // AQS), BLK // AQS)]

    for m in range(2):
        XF[m, chip, pl.ds(mine, BLK)] = x_ref[m]
    WO[chip, core, f] = wo_ref[...]
    WD[zz] = wd_ref[...]
    VEC[...] = jnp.zeros((8, 128), F32)
    for i, v in enumerate((v0, v1, v2, v3, v4, v5, v6, v7)):
        VEC[i : i + 1, 0 : v.shape[1]] = v[...].astype(F32)
    VB[c, f] = VEC[...]

    def gather_x(k):
        for d in range(2):
            ch = chip_of(d, k)
            for q in range(AQS):
                at = sub(d, ch, q)

                @pl.when(k > 0)
                def _():
                    remote(at, at, agx_s, ag_r.at[d, (k - 1) * AQS + q], "ctx", target(d)).wait_recv()

                @pl.when(k < 7)
                def _():
                    remote(at, at, agx_s, ag_r.at[d, k * AQS + q], "ctx", target(d)).start()

            whole = block(XF, d, ch, mine)
            remote(whole, whole, sbx_s, sbx_r, "ctx", sib).start()

    def gather_wo(k):
        for d in range(2):
            at = WO.at[chip_of(d, k), core, f, pl.ds(16 * d, 16)]

            @pl.when(k > 0)
            def _():
                remote(at, at, wo_s, wo_r.at[d, k - 1], "ctx", target(d)).wait_recv()

            @pl.when(k < 7)
            def _():
                remote(at, at, wo_s, wo_r.at[d, k], "ctx", target(d)).start()

            pair(1, at, at).start()

    pl.loop(0, 1)(gather_x)
    pair(0, VEC, VB.at[c, f]).start()

    for j in range(8):
        qt = wq_ref[:, 128 * j : 128 * j + 128].astype(F32)
        kt = wq_ref[:, D + 128 * j : D + 128 * j + 128].astype(F32)
        vt = wq_ref[:, 2 * D + 128 * j : 2 * D + 128 * j + 128].astype(F32)
        for e in range(2):
            w = 2 * j + e
            qk = jnp.where(low_half, qt, pltpu.roll(kt, 64, 1)) if e == 0 else jnp.where(low_half, pltpu.roll(qt, 64, 1), kt)
            WP[w, :, 0:128] = qk.astype(BF16)
            WP[w, :, 128:256] = (vt if e == 0 else pltpu.roll(vt, 64, 1)).astype(BF16)
    WB[c, f] = WP[c]
    send_all(0, lambda to: WP.at[to], WB.at[c, f])
    for w in range(8):
        for i in range(4):
            WUS[w, :, 128 * i : 128 * (i + 1)] = wu_ref[:, 128 * (8 * i + w) : 128 * (8 * i + w + 1)]
    WU[zz, pp] = WUS[pp]
    send_plane(0, lambda to: WUS.at[to], WU.at[zz, pp])

    @pl.loop(1, 4)
    def _(k):
        gather_x(k)
        gather_wo(k - 1)

    pair(0, VB.at[c, 1 - f], VB.at[c, 1 - f]).wait_recv()
    send_all(1, lambda to: VB.at[c], VB.at[c])
    recv_all(0, WB.at[0:15, 0])
    pair(3, WB.at[:, f], WB.at[:, f]).start()
    recv_plane(0, WU.at[zz, 0:7])

    def head_weights():
        pair(3, WB.at[:, 1 - f], WB.at[:, 1 - f]).wait_recv()
        WHT[...] = WB[...].reshape(D, 256).T

    def vectors():
        recv_all(1, VB.at[0:15])
        for j in range(8):
            tiles = [VB[2 * j + q // 2, q % 2] for q in range(4)]
            total = tiles[0]
            for q in range(1, 4):
                total = total + pltpu.roll(tiles[q], 32 * q, 1)
            VF[:, 128 * j : 128 * j + 128] = total
            v1 = pltpu.roll(tiles[1], 96, 1)
            v2 = pltpu.roll(tiles[2], 64, 1)
            v3 = pltpu.roll(tiles[3], 32, 1)
            rows = (
                tiles[0] + jnp.where(lane >= 96, v1, 0.0),
                jnp.where(lane < 64, v1, 0.0) + jnp.where(lane >= 64, v2, 0.0),
                jnp.where(lane < 32, v2, 0.0) + v3,
            )
            for i in range(3):
                QBR[3 * j + i : 3 * j + i + 1, :] = rows[i][1:2, :]
        for i in range(4):
            UB[0:1, 128 * i : 128 * (i + 1)] = VB[4 * i + lax.rem(c, 4), f, 0:1, :]
        for i in range(3):
            row = QBR[pl.ds(8 * i + chip, 1), :]
            BQ[i] = jnp.broadcast_to(row, (128, 128)).T

    @pl.loop(4, 8)
    def _(k):
        gather_x(k)
        gather_wo(k - 1)
        pl.when(k == 6)(vectors)
        pl.when(k == 7)(head_weights)

        @pl.when(k == 6)
        def _():
            z_gather(0, 0)
            z_gather(1, 0)


    gather_wo(jnp.int32(7))
    z_gather(2, 0)
    z_gather(3, 0)
    remote(XF.at[0], XF.at[0], sbx_s, sbx_r, "ctx", sib).wait_recv()


    def lanes(n):
        return pl.ds(pl.multiple_of(n * CHUNK, CHUNK), CHUNK)

    def turn(u, cosine, sine):
        a, b = u[0:32], u[32:64]
        return jnp.concatenate([a * cosine - b * sine, b * cosine + a * sine], axis=0)

    def unturn(u, cosine, sine):
        a, b = u[0:32], u[32:64]
        return jnp.concatenate([a * cosine + b * sine, b * cosine - a * sine], axis=0)

    @pl.loop(0, 8)
    def _(it):
        m = lax.div(it, 4)
        n = lax.rem(it, 4)
        xs = XF[m, pl.ds(2 * n, 2)].reshape(CHUNK, D)
        joined = nt(WHT[0:192, :], xs)
        cosine = rope_ref[0, :, lanes(n)]
        sine = rope_ref[1, :, lanes(n)]
        q = joined[0:64] + BQ[0, pl.ds(mine, BLK), 0:1]
        k = joined[64:128] + BQ[1, pl.ds(mine, BLK), 0:1]
        v = joined[128:192] + BQ[2, pl.ds(mine, BLK), 0:1]
        q = turn(q, cosine, sine)
        k = turn(k, cosine, sine)
        rows = pl.ds(pl.multiple_of(n * CHUNK, CHUNK), CHUNK)
        QT[m, :, lanes(n)] = (q.astype(BF16).astype(F32) * 0.125).astype(BF16)
        KT[m, :, lanes(n)] = k.astype(BF16)
        VT[m, :, lanes(n)] = v.astype(BF16)
        KN[m, rows, :] = k.T.astype(BF16)
        VN[m, rows, :] = v.T.astype(BF16)

    @pl.loop(0, 8)
    def _(it):
        @pl.when(it == 0)
        def _():
            z_gather(0, 1)
            z_gather(1, 1)

        @pl.when(it == 4)
        def _():
            z_gather(2, 1)
            z_gather(3, 1)

        @pl.when(it == 3)
        def _():
            pair(1, WO.at[:, core, 1 - f], WO.at[:, core, 1 - f]).wait_recv()
            remote(WO.at[:, core], WO.at[:, core], wos_s, wos_r, "ctx", sib).start()

        m = lax.div(it, 4)
        n = lax.rem(it, 4)
        s = nn(KN[m], QT[m, :, lanes(n)])
        e = jnp.exp(s - jnp.max(s, axis=0, keepdims=True))
        p = (e * (1.0 / jnp.sum(e, axis=0, keepdims=True))).astype(BF16)
        PT[m, :, lanes(n)] = p
        ATD[m, :, lanes(n)] = nn(VT[m], p)

    for j in range(8):
        a0 = ATD[0, :, 128 * j : 128 * j + 128]
        a1 = ATD[1, :, 128 * j : 128 * j + 128]
        ATS[2 * j] = jnp.where(low_half, a0, pltpu.roll(a1, 64, 1)).astype(BF16)
        ATS[2 * j + 1] = jnp.where(low_half, pltpu.roll(a0, 64, 1), a1).astype(BF16)
    AT[c] = ATS[c]
    send_all(2, lambda to: ATS.at[to], AT.at[c])

    z_gather(0, 2)
    z_gather(1, 2)
    remote(WO.at[:, 1 - core], WO.at[:, 1 - core], wos_s, wos_r, "ctx", sib).wait_recv()
    recv_all(2, AT.at[0:15])

    z_gather(2, 2)
    z_gather(3, 2)
    att_rows = AT[...].reshape(D, 128).T
    resid = x_ref[...].reshape(128, D).astype(F32) + nn(att_rows, WO[...].reshape(D, D)) + VF[2:3, :]
    center = resid - row_mean(resid)
    root = lax.rsqrt(row_mean(center * center) + 1e-05)
    z = center * root
    hidden = z * VF[4:5, :] + VF[5:6, :]
    Z1[...] = z
    R1[...] = jnp.broadcast_to(root, (128, 128))
    H1[...] = hidden
    hidden_low = hidden.astype(BF16)
    for m in range(2):
        HF[grp, m, pl.ds(mine, BLK)] = hidden_low[m * BLK : (m + 1) * BLK]

    def plane(buf, make, early, ready, after_one, after_two, finish):
        far = ((yy * 2 + 1 - f), ((1 - yy) * 2 + f))
        groups = tuple((grp, far[m], far[1 - m], (1 - yy) * 2 + 1 - f) for m in range(2))

        def to(axis, src, dst, ss, rs):
            if axis == 0:
                return remote(src, dst, ss, rs, "fsdp", 1 - f)
            return remote(src, dst, ss, rs, "ctx", c + 2 - 4 * yy)

        def at(m, i, row0):
            return buf.at[groups[m][i], m, pl.ds(row0, BLK)]

        def hand_over(m, i):
            remote(at(m, i, mine), at(m, i, mine), pb_s, pb_r.at[m, i], "ctx", sib).start()

        def arrive(m, i, n):
            to(m, at(m, i, mine), at(m, i, mine), pa_s, pa_r.at[m, n]).wait_recv()

        def work(places):
            part = make(groups[0][places[0]])
            for m in range(2):
                PB[m, places[m]] = part[128 * m : 128 * (m + 1)]
            for m in range(2):
                i = places[m]
                SS[m, i] = PB[m, i, pl.ds(other, BLK)].astype(BF16)
                remote(SS.at[m, i], SR.at[m, i], ps_s, ps_r.at[m, i], "ctx", sib).start()

        def both(m, i):
            remote(at(m, i, other), at(m, i, other), pb_s, pb_r.at[m, i], "ctx", sib).wait_recv()

        def share(m, i):
            remote(SR.at[m, i], SR.at[m, i], ps_s, ps_r.at[m, i], "ctx", sib).wait_recv()
            return PB[m, i, pl.ds(mine, BLK)] + SR[m, i].astype(F32)

        def push(m, n, value, axis):
            RSD[m, n, 0:BLK] = value.astype(BF16)
            to(axis, RSD.at[m, n, pl.ds(0, BLK)], RR.at[m, n, pl.ds(0, BLK)], pr_s, pr_r.at[m, n]).start()

        def pulled(m, n):
            got = RR.at[m, n, pl.ds(0, BLK)]
            to(m, got, got, pr_s, pr_r.at[m, n]).wait_recv()
            return RR[m, n, 0:BLK].astype(F32)

        for m in range(2):
            to(m, at(m, 0, mine), at(m, 0, mine), pa_s, pa_r.at[m, 0]).start()
        for m in range(2):
            hand_over(m, 0)
            to(1 - m, at(m, 0, mine), at(m, 0, mine), pa_s, pa_r.at[m, 1]).start()
        for m in range(2):
            both(m, 0)
        if early is not None:
            work((0, 0))
        for m in range(2):
            arrive(m, 1, 0)
            to(1 - m, at(m, 1, mine), at(m, 1, mine), pa_s, pa_r.at[m, 2]).start()
            hand_over(m, 1)
        for m in range(2):
            arrive(m, 2, 1)
            hand_over(m, 2)
        for i in (1, 2):
            for m in range(2):
                both(m, i)
        if early is not None:
            work((1, 2))
        for m in range(2):
            arrive(m, 3, 2)
            hand_over(m, 3)
        if early is not None:
            work((2, 1))
        for m in range(2):
            both(m, 3)
        if ready is not None:
            ready()
        work((3, 3))
        if early is not None:
            early()
        else:
            work((1, 2))
        for m in range(2):
            push(m, 1, share(m, 3), 1 - m)
        if early is None:
            work((2, 1))
        for m in range(2):
            push(m, 0, share(m, 2), 1 - m)
        if early is None:
            work((0, 0))
        after_one()
        for m in range(2):
            push(m, 2, share(m, 1) + pulled(m, 1), m)
        after_two()
        for m in range(2):
            finish(m, share(m, 0) + pulled(m, 0) + pulled(m, 2))
        remote(XF.at[0, 0:3], XF.at[0, 0:3], pa_s, sbx_r, "ctx", sib).wait_send()
        remote(XF.at[0, 0:4], XF.at[0, 0:4], pb_s, sbx_r, "ctx", sib).wait_send()
        remote(XF.at[0, 0:4], XF.at[0, 0:4], ps_s, sbx_r, "ctx", sib).wait_send()
        remote(XF.at[0, 0:3], XF.at[0, 0:3], pr_s, sbx_r, "ctx", sib).wait_send()

    def ring(make, extra, finish):
        def first(k):
            slot = 2 - lax.div(k + 7, 8) * (2 - lax.rem(k, 2))
            for d in range(2):
                ch = chip_of(d, k)
                PB[d, slot] = make(d, ch)
                SS[d, k] = PB[d, slot, pl.ds(other, BLK)].astype(BF16)
                remote(SS.at[d, k], SR.at[d, k], ss_s, ss_r.at[d, k], "ctx", sib).start()

        def sums(d, k):
            at = SR.at[d, k]
            remote(at, at, ss_s, ss_r.at[d, k], "ctx", sib).wait_recv()

        def arrived(d, q, k):
            got = RR.at[d, k, rows_of(q)]
            remote(got, got, rs_s, rs_r.at[d, k * RQS + q], "ctx", sib).wait_recv()

        def rows_of(q):
            return pl.ds(q * ROWS, ROWS if q < RQS - 1 else ROWS + 16)

        def second(k):
            slot = lax.rem(k, 2)
            pl.when(k == 1)(lambda: pair(5, XRO, XRO).wait_recv())
            for d in range(2):
                sums(d, k)
            for q in range(RQS):
                for d in range(2):
                    part = pl.ds(q * ROWS, ROWS)
                    total = PB[d, slot, pl.ds(pl.multiple_of(core * BLK + q * ROWS, ROWS), ROWS)] + SR[d, k, part].astype(F32)
                    rider = q == RQS - 1
                    if rider:
                        ride = riders(d, chip_of(d, k))

                    @pl.when(k > 1)
                    def _():
                        arrived(d, q, k - 1)
                        RSD[d, k, part] = (total + RR[d, k - 1, part].astype(F32)).astype(BF16)
                        if rider:
                            RSD[d, k, BLK : BLK + 16] = (ride + RR[d, k - 1, BLK : BLK + 16].astype(F32)).astype(BF16)

                    @pl.when(k == 1)
                    def _():
                        RSD[d, k, part] = total.astype(BF16)
                        if rider:
                            RSD[d, k, BLK : BLK + 16] = ride.astype(BF16)

                    remote(
                        RSD.at[d, k, rows_of(q)], RR.at[d, k, rows_of(q)], rs_s, rs_r.at[d, k * RQS + q],
                        "ctx", target(d),
                    ).start()

        @pl.loop(0, 9)
        def _(it):
            @pl.when(it < 8)
            def _():
                first(it)

            @pl.when(it > 1)
            def _():
                second(it - 1)

            extra(it)

        for d in range(2):
            sums(d, 0)
            for q in range(RQS):
                arrived(d, q, 7)
            finish(d, PB[d, 2, pl.ds(mine, BLK)] + SR[d, 0].astype(F32) + RR[d, 7, 0:BLK].astype(F32))

        remote(SS, SS, ss_s, sbx_r, "ctx", sib).wait_send()
        remote(RSD.at[:, 0:7], RSD.at[:, 0:7], rs_s, sbx_r, "ctx", sib).wait_send()

    def nothing():
        pass

    def up_w():
        return WU[...].reshape(D, FF_UNITS)

    def down_w():
        return WD[...].reshape(FF_UNITS, D)

    def make_up(g):
        u = nn(HF[g].reshape(256, D), up_w()) + UB[0:1, :]
        phi = 0.5 * (1.0 + lax.erf(u * 0.7071067811865476))
        a = (u * phi).astype(BF16)
        DG[g] = (phi + u * (jnp.exp(-0.5 * u * u) * 0.3989422804014327)).reshape(2, 128, FF_UNITS)
        ACT[g] = a.reshape(2, 128, FF_UNITS)
        return nn(a, down_w())

    def finish_up(d, total):
        rows = slice(d * BLK, (d + 1) * BLK)
        SEC[rows, :] = H1[rows, :] + total + VF[3:4, :]

    def weights_in():
        for kd in range(4):
            z_gather(kd, 3)

    plane(HF, make_up, None, weights_in, nothing, nothing, finish_up)

    resid = SEC[...]
    center = resid - row_mean(resid)
    root = lax.rsqrt(row_mean(center * center) + 1e-05)
    z = center * root
    out_ref[...] = (z * VF[6:7, :] + VF[7:8, :]).astype(BF16).reshape(2, BLK, D)
    cot = ct_ref[...].reshape(128, D).astype(F32)
    SG[...] = jnp.zeros((8, D), F32)
    SG[4:5, :] = col_sum(cot * z)
    SG[5:6, :] = col_sum(cot)
    u = cot * VF[6:7, :]
    grad = (u - row_mean(u) - z * row_mean(u * z)) * root
    G2[...] = grad
    grad_low = grad.astype(BF16)
    SG[1:2, :] = col_sum(grad_low.astype(F32))
    for m in range(2):
        BG[grp, m, pl.ds(mine, BLK)] = grad_low[m * BLK : (m + 1) * BLK]

    def make_down(g):
        pg = (nt(BG[g].reshape(256, D), down_w()) * DG[g].reshape(256, FF_UNITS)).astype(BF16)
        PG[g] = pg.reshape(2, 128, FF_UNITS)
        return nt(pg, up_w())

    def finish_down(d, total):
        rows = slice(d * BLK, (d + 1) * BLK)
        SEC[rows, :] = G2[rows, :] + total

    def down_grads():
        TT[...] = ACT[...].reshape(1024, FF_UNITS).T
        for i in range(4):
            DWD[i] = nn(TT[128 * i : 128 * (i + 1), :], BG[...].reshape(1024, D)).astype(BF16)
        z_start(1)

    def up_grads():
        TT[...] = PG[...].reshape(1024, FF_UNITS).T
        for i in range(4):
            g = nn(TT[...], HF[:, :, :, CHUNK * i : CHUNK * (i + 1)].reshape(1024, CHUNK))
            DWU[i] = g.T.astype(BF16).reshape(8, 32, FF_UNITS)
        sums = nn(jnp.ones((8, 1024), BF16), PG[...].reshape(1024, FF_UNITS))[0:1, :]
        for i in range(8):
            SG[6:7, 128 * i : 128 * (i + 1)] = sums[:, 128 * (i // 2) : 128 * (i // 2) + 128]

    plane(BG, make_down, nothing, down_grads, nothing, up_grads, finish_down)

    hid = SEC[...]
    z = Z1[...]
    SG[2:3, :] = col_sum(hid * z)
    SG[3:4, :] = col_sum(hid)
    u = hid * VF[4:5, :]
    grad = (u - row_mean(u) - z * row_mean(u * z)) * R1[:, 0:1]
    H1[...] = grad
    proj = grad.astype(BF16)
    SG[0:1, :] = col_sum(proj.astype(F32))
    sent_all(2, ATS.at[0:15])
    ATS[...] = nt(WO[...].reshape(D, D), proj).astype(BF16).reshape(NCTX, HEAD, 128)
    AGT[c] = ATS[c]
    send_all(3, lambda to: ATS.at[to], AGT.at[c])
    z_start(0)

    for j in range(NCHIP):
        SSO[j] = nn(AT[2 * j + 1 - core], proj).astype(BF16)
    remote(SSO, SRO, po_s, po_r, "ctx", sib).start()
    pair(4, SG, SGR).start()
    for j in range(NCHIP):
        GO[j] = nn(AT[2 * j + core], proj)
    remote(SRO, SRO, po_s, po_r, "ctx", sib).wait_recv()
    for j in range(NCHIP):
        GO[j] = GO[j] + SRO[j].astype(F32)
        XSO[j] = GO[j, pl.ds(pl.multiple_of((1 - f) * 32, 32), 32)].astype(BF16)
    pair(5, XSO, XRO).start()
    recv_all(3, AGT.at[0:15])
    sent_all(3, ATS.at[0:15])

    for j in range(8):
        t0 = AGT[2 * j].astype(F32)
        t1 = AGT[2 * j + 1].astype(F32)
        AGQ[0, :, 128 * j : 128 * j + 128] = jnp.where(low_half, t0, pltpu.roll(t1, 64, 1)).astype(BF16)
        AGQ[1, :, 128 * j : 128 * j + 128] = jnp.where(low_half, pltpu.roll(t0, 64, 1), t1).astype(BF16)

    DK[...] = jnp.zeros((2, HEAD, D), F32)
    DV[...] = jnp.zeros((2, HEAD, D), F32)

    def small_push():
        pair(4, SGR, SGR).wait_recv()
        SGT[...] = SG[...] + SGR[...]
        SGT[6:7, :] = SG[6:7, :]
        SGC[c] = SGT[:, pl.ds(pl.multiple_of(chip * 128, 128), 128)]
        send_all(4, lambda to: SGT.at[:, pl.ds(pl.multiple_of(lax.div(to, 2) * 128, 128), 128)], SGC.at[c])

    def up_push():
        def put(total):
            PUS[...] = total.astype(BF16)

        z_total(0, put)
        RU[pp] = PUS[pp]
        send_plane(1, lambda to: PUS.at[to], RU.at[pp])

    @pl.loop(0, 8)
    def _(it):
        pl.when(it == 2)(small_push)
        pl.when(it == 0)(lambda: z_relay(1))
        pl.when(it == 7)(lambda: z_relay(0))
        m = lax.div(it, 4)
        n = lax.rem(it, 4)
        q = QT[m, :, lanes(n)]
        g = AGQ[m, :, lanes(n)]
        delta = jnp.sum(g.astype(F32) * ATD[m, :, lanes(n)], axis=0, keepdims=True)
        p = PT[m, :, lanes(n)]
        ds = (p.astype(F32) * (nn(VN[m], g) - delta)).astype(BF16)
        DK[m] = DK[m] + nt(q, ds)
        DV[m] = DV[m] + nt(g, p)
        dq = nn(KT[m], ds) * 0.125
        JG[m, 0:64, lanes(n)] = unturn(dq, rope_ref[0, :, lanes(n)], rope_ref[1, :, lanes(n)]).astype(BF16)

    for m in range(2):
        JG[m, 64:128, :] = unturn(DK[m], rope_ref[0], rope_ref[1]).astype(BF16)
        JG[m, 128:192, :] = DV[m].astype(BF16)

    def make_token(m, ch):
        jg = JG[m, :, pl.ds(pl.multiple_of(ch * 128, 128), 128)]
        return tn(jg, WHT[0:192, :])

    def finish_token(d, total):
        tg_ref[d] = H1[d * BLK : (d + 1) * BLK, :] + total
        go_ref[16 * d : 16 * d + 16, :] = riders(d, chip) + RR[d, 7, BLK : BLK + 16].astype(F32)

    def qkv_bias_rows():
        b = nt(jnp.ones((8, D), BF16), JG[0]) + nt(jnp.ones((8, D), BF16), JG[1])
        b = jnp.concatenate([b, jnp.zeros((8, 64), F32)], axis=1)
        QBP[...] = jnp.zeros((32, UNITS), F32)
        QBP[0:1, 128:256] = jnp.where(low_half, 0.0, pltpu.roll(b[0:1, 0:128], 64, 1))
        QBP[1:2, 128:256] = jnp.where(low_half, 0.0, b[0:1, 0:128])
        QBP[2:3, 128:256] = jnp.where(low_half, 0.0, pltpu.roll(b[0:1, 128:256], 64, 1))

    def qkv_grad(n):
        cols = slice(CHUNK * n, CHUNK * (n + 1))
        g = nn(JG[0], XF[0, :, :, cols].reshape(D, CHUNK)) + nn(JG[1], XF[1, :, :, cols].reshape(D, CHUNK))
        g = jnp.concatenate([g, jnp.zeros((64, CHUNK), F32)], axis=0)
        GU[4 * n : 4 * n + 4] = g.T.reshape(4, 2, 32, UNITS) + QBP[...]

    def qkv_pair():
        XSQ[...] = GU[:, 1 - f].astype(BF16)
        pair(8, XSQ, XRQ).start()

    def qkv_push():
        pair(8, XRQ, XRQ).wait_recv()
        AQ[...] = (GU[:, f] + XRQ[...].astype(F32)).astype(BF16)
        RQ[c] = AQ[c]
        send_all(6, lambda to: AQ.at[to], RQ.at[c])

    def riders(d, ch):
        return GO[ch, pl.ds(pl.multiple_of(f * 32 + 16 * d, 16), 16)] + XRO[ch, 16 * d : 16 * d + 16].astype(F32)

    def small_rest():
        recv_all(4, SGC.at[0:15])
        total = SGC[0]
        for w in range(1, NCTX):
            total = total + SGC[w]
        gs_ref[...] = total
        here = lax.rem(c, 4)
        gs_ref[6:7, :] = SGC[here, 6:7, :] + SGC[4 + here, 6:7, :] + SGC[8 + here, 6:7, :] + SGC[12 + here, 6:7, :]

    def down_rest():
        def put(total):
            gd_ref[...] = total

        z_total(1, put)

    def on_the_way(it):
        pl.when(it == 0)(qkv_bias_rows)
        for n in range(4):
            pl.when(it == n)(partial(qkv_grad, n))
        pl.when(it == 3)(qkv_pair)
        pl.when(it == 4)(small_rest)
        pl.when(it == 5)(qkv_push)
        pl.when(it == 6)(down_rest)
        pl.when(it == 8)(up_push)

    ring(make_token, on_the_way, finish_token)
    recv_plane(1, RU.at[0:7])
    recv_all(6, RQ.at[0:15])

    remote(XF.at[0, 0:7], XF.at[0, 0:7], agx_s, sbx_r, "ctx", sib).wait_send()
    remote(XF.at[0], XF.at[0], sbx_s, sbx_r, "ctx", sib).wait_send()
    remote(WO.at[0:7, 0, 0], WO.at[0:7, 0, 0], wo_s, sbx_r, "ctx", sib).wait_send()
    remote(WO.at[:, 0], WO.at[:, 0], wos_s, sbx_r, "ctx", sib).wait_send()
    sent_all(0, WP.at[0:15])
    sent_all(1, VB.at[0:15])
    sent_all(4, SGC.at[0:15])
    sent_all(6, AQ.at[0:15])
    remote(SSO, SSO, po_s, po_r, "ctx", sib).wait_send()
    sent_plane(0, WUS.at[0:7])
    sent_plane(1, PUS.at[0:7])
    for kd in range(2):
        for s in range(3):
            z_gather(kd, s, True)
            z_gather(kd + 2, s, True)
        z_start(kd, True)
        z_relay(kd, True)
    for i, at in ((0, VEC), (1, WO.at[:, core, f]), (3, WB.at[:, f]), (4, SG), (5, XSO), (8, XSQ)):
        pair(i, at, at).wait_send()


def rope_tables():
    freqs = (np.float32(10000.0) ** (-np.arange(0, HEAD, 2, dtype=np.float32) / np.float32(HEAD))).astype(np.float32)
    angles = freqs[:, None] * np.arange(1024, dtype=np.float32)[None, :]
    return np.stack([np.cos(angles), np.sin(angles)]).astype(np.float32)


def fused_body(
    tokens, cotangent, qkv_weight, out_weight, up_weight, down_weight, qkv_bias, out_bias, up_bias, down_bias,
    first_gain, first_shift, second_gain, second_shift,
):
    scratch = [
        ((8, 128), F32),
        ((2, 8, 128, D), BF16), ((4, 2, 128, D), BF16), ((4, 2, 128, D), BF16),
        ((16, 32, 256), BF16), ((16, 2, 32, 256), BF16), ((8, 32, FF_UNITS), BF16), ((4, 8, 32, FF_UNITS), BF16),
        ((8, 2, 2, 32, D), BF16), ((4, 128, D), BF16),
        ((16, 2, 8, 128), F32), ((8, D), F32), ((8, FF_UNITS), F32), ((24, 128), F32), ((3, 128, 128), F32),
        ((256, D), BF16),
        ((2, 64, D), BF16), ((2, 64, D), BF16), ((2, 64, D), BF16), ((2, D, 64), BF16), ((2, D, 64), BF16),
        ((2, D, D), BF16), ((2, 64, D), F32),
        ((16, 64, 128), BF16), ((16, 64, 128), BF16), ((16, 64, 128), BF16),
        ((128, D), F32), ((128, D), F32), ((128, 128), F32), ((128, D), F32), ((128, D), F32),
        ((4, 2, 128, FF_UNITS), F32), ((4, 2, 128, FF_UNITS), BF16), ((4, 2, 128, FF_UNITS), BF16),
        ((2, 4, 128, D), F32),
        ((2, 8, BLK, D), BF16), ((2, 8, BLK, D), BF16), ((2, 8, 80, D), BF16), ((2, 8, 80, D), BF16),
        ((FF_UNITS, 1024), BF16),
        ((16, 2, 32, UNITS), F32), ((8, 32, FF_UNITS), BF16),
        ((4, 8, 32, FF_UNITS), BF16), ((4, 128, D), BF16), ((4, 8, 32, FF_UNITS), BF16), ((4, 128, D), BF16),
        ((8, BLK, D), F32), ((8, 32, D), BF16), ((8, 32, D), BF16), ((8, BLK, D), BF16), ((8, BLK, D), BF16),
        ((8, D), F32), ((8, D), F32), ((8, D), F32), ((16, 8, 128), F32), ((2, 64, D), BF16),
        ((2, 64, D), F32), ((2, 64, D), F32), ((2, 192, D), BF16),
        ((16, 32, UNITS), BF16), ((16, 32, UNITS), BF16), ((16, 32, UNITS), BF16), ((32, UNITS), F32),
    ]
    sems = [(14,), (2, 8 * AQS), (2, 8), (2, 8 * RQS), (2, 8), (9,), (9,), (11,), (11,), (2,), (2,)]
    sems += [(2, 3), (2, 4), (2, 4), (2, 3), (4, 6), (4, 4), (2, 4), (2, 4)]
    vmem = pl.BlockSpec(memory_space=pltpu.VMEM)
    shapes = [((2, BLK, D), BF16), ((2, BLK, D), F32), ((16, 32, UNITS), BF16), ((32, D), F32), ((8, 32, FF_UNITS), BF16), ((128, D), F32), ((8, 128), F32)]
    final = shapes[:2] + [((32, 3 * D), F32), shapes[3], ((32, 4 * D), F32), shapes[5]]
    bias = (up_bias, qkv_bias, out_bias, down_bias, first_gain, first_shift, second_gain, second_shift)
    made = pl.pallas_call(
        layer_kernel,
        out_shape=[jax.ShapeDtypeStruct(s, t) for s, t in shapes],
        in_specs=[vmem] * 15,
        out_specs=[vmem] * 7,
        scratch_shapes=[pltpu.VMEM(s, t) for s, t in scratch] + [pltpu.SemaphoreType.DMA(s) for s in sems],
        compiler_params=pltpu.CompilerParams(collective_id=0, has_side_effects=True, vmem_limit_bytes=VMEM_LIMIT),
        name="layer",
    )(
        tokens[:, 0], cotangent[:, 0], qkv_weight, out_weight, up_weight, down_weight, jnp.asarray(rope_tables()),
        *(v[None] for v in bias),
    )
    anywhere = pl.BlockSpec(memory_space=pl.ANY)
    widths = (96, 32, 128, 32, 32, 32, 32, 32)
    last = pl.pallas_call(
        finish_kernel,
        out_shape=[jax.ShapeDtypeStruct(s, t) for s, t in final] + [jax.ShapeDtypeStruct((1, w), F32) for w in widths],
        in_specs=[anywhere, anywhere, vmem, anywhere, vmem, anywhere, vmem],
        out_specs=[vmem] * 14,
        scratch_shapes=[pltpu.VMEM((24, 128), F32), pltpu.SemaphoreType.DMA((4,))],
        name="finish",
    )(*made)
    return (last[0][:, None], last[1][:, None], *last[2:6], *(v[0] for v in last[6:]))


def finish_kernel(*refs):
    (out, tg, rq, go, ru, gd, gs), done, small, (gb, sems) = refs[:7], refs[7:13], refs[13:21], refs[21:]
    pairs = ((out, done[0]), (tg, done[1]), (go, done[3]), (gd, done[5]))
    copies = [pltpu.make_async_copy(a, b, sems.at[i]) for i, (a, b) in enumerate(pairs)]
    for copy in copies:
        copy.start()
    gq, gu = done[2], done[4]
    low_half = lax.broadcasted_iota(jnp.int32, (1, 128), 1) < 64
    for j in range(8):
        a = rq[2 * j].astype(F32)
        b = rq[2 * j + 1].astype(F32)
        a0, a1, b0, b1 = a[:, 0:128], a[:, 128:256], b[:, 0:128], b[:, 128:256]
        v = pltpu.roll(b1, 64, 1)
        gq[:, 128 * j : 128 * (j + 1)] = jnp.where(low_half, a0, pltpu.roll(b0, 64, 1))
        gq[:, D + 128 * j : D + 128 * (j + 1)] = jnp.where(low_half, pltpu.roll(a0, 64, 1), b0)
        gq[:, 2 * D + 128 * j : 2 * D + 128 * (j + 1)] = jnp.where(low_half, a1, v)
        bias = jnp.where(low_half, pltpu.roll(a1, 64, 1), b1)
        for i in range(3):
            gb[8 * i + j : 8 * i + j + 1, :] = bias[i : i + 1, :]
    for w in range(8):
        for i in range(4):
            gu[:, 128 * (8 * i + w) : 128 * (8 * i + w + 1)] = ru[w, :, 128 * i : 128 * (i + 1)].astype(F32)
    index = lax.axis_index("ctx") * 2 + lax.axis_index("fsdp")
    place = lax.rem(index, 4)
    turned = pltpu.roll(gs[...], lax.rem(128 - 32 * place, 128), 1)
    for ref, row in zip(small[1:], (0, 6, 1, 2, 3, 4, 5)):
        ref[...] = gs[6:7, :] if row == 6 else turned[row : row + 1, 0:32]
    offset = lax.rem(96 * index, 128)
    row = lax.div(96 * index, 128)
    lane = lax.broadcasted_iota(jnp.int32, (1, 128), 1)
    back = lax.rem(128 - offset, 128)
    one = pltpu.roll(gb[pl.ds(row, 1), :], back, 1)
    two = pltpu.roll(gb[pl.ds(lax.rem(row + 1, 24), 1), :], back, 1)
    small[0][...] = jnp.where(lane < 128 - offset, one, two)[:, 0:96]
    for copy in copies:
        copy.wait()


VMEM_LIMIT = 63 * 1024 * 1024


def layernorm(resid, gain, shift):
    center = resid - jnp.mean(resid, axis=-1, keepdims=True)
    spread = jnp.mean(center * center, axis=-1, keepdims=True)
    return center * lax.rsqrt(spread + 1e-05) * gain + shift


def tables(position):
    freqs = 10000.0 ** (-jnp.arange(0, HEAD, 2, dtype=jnp.float32) / HEAD)
    angles = position[:, None] * freqs[None, :]
    return (jnp.cos(angles)[:, None, :], jnp.sin(angles)[:, None, :])


def rotate(heads_in, cosine, sine):
    middle = heads_in.shape[-1] // 2
    first = heads_in[..., :middle]
    second = heads_in[..., middle:]
    return jnp.concatenate(
        [first * cosine - second * sine, second * cosine + first * sine], axis=-1
    )


def unrotate(heads_in, cosine, sine):
    middle = heads_in.shape[-1] // 2
    first = heads_in[..., :middle]
    second = heads_in[..., middle:]
    return jnp.concatenate(
        [first * cosine + second * sine, second * cosine - first * sine], axis=-1
    )


def split_heads(flat_rows):
    return flat_rows.reshape(flat_rows.shape[0], HEADS, HEAD)


def over_blocks(update, carried, count, limit):
    size = math.gcd(count, limit)

    def advance(block_idx, state):
        return update(state, block_idx * size, size)

    return lax.fori_loop(0, count // size, advance, carried)


def column_sum(matrix):
    return jnp.sum(matrix.astype(jnp.float32), axis=0)


def forward_local(sequence, weights_now, cosine, sine, group):
    (
        qkv_full,
        out_full,
        up_full,
        down_full,
        qkv_vector,
        out_vector,
        up_vector,
        down_vector,
        gain_first,
        shift_first,
        gain_second,
        shift_second,
    ) = weights_now
    rows = sequence.shape[0]
    width = sequence.shape[1]
    joined = jnp.dot(sequence, qkv_full, preferred_element_type=jnp.float32) + qkv_vector.astype(
        jnp.float32
    )
    query_flat = (
        rotate(split_heads(joined[:, :width]), cosine, sine)
        .astype(jnp.bfloat16)
        .reshape(rows, width)
    )
    keys_flat = (
        rotate(split_heads(joined[:, width : 2 * width]), cosine, sine)
        .astype(jnp.bfloat16)
        .reshape(rows, width)
    )
    values_flat = joined[:, 2 * width :].astype(jnp.bfloat16)
    query_heads = split_heads(query_flat)
    start_state = (
        jnp.full((HEADS, rows), -1e30, jnp.float32),
        jnp.zeros((HEADS, rows), jnp.float32),
        jnp.zeros((rows, HEADS, HEAD), jnp.float32),
    )
    keys_piece = lax.all_gather(keys_flat, "ctx", axis=0, tiled=True)
    values_piece = lax.all_gather(values_flat, "ctx", axis=0, tiled=True)

    def absorb_block(state, offset, size):
        running, total, accum = state
        key_block = split_heads(lax.dynamic_slice_in_dim(keys_piece, offset, size, 0))
        value_block = split_heads(lax.dynamic_slice_in_dim(values_piece, offset, size, 0))
        scores = (
            jnp.einsum("qhd,khd->hqk", query_heads, key_block, preferred_element_type=jnp.float32)
            * 0.125
        )
        highest_new = jnp.maximum(running, jnp.max(scores, axis=-1))
        factor = jnp.exp(running - highest_new)
        expo = jnp.exp(scores - highest_new[:, :, None])
        total = total * factor + jnp.sum(expo, axis=-1)
        accum = accum * factor.T[:, :, None] + jnp.einsum(
            "hqk,khd->qhd",
            expo.astype(jnp.bfloat16),
            value_block,
            preferred_element_type=jnp.float32,
        )
        return (highest_new, total, accum)

    running, total, accum = over_blocks(absorb_block, start_state, keys_piece.shape[0], group)
    attended = accum / total.T[:, :, None]
    logsum = running + jnp.log(total)
    att_low = attended.reshape(rows, width).astype(jnp.bfloat16)
    projected = jnp.dot(att_low, out_full, preferred_element_type=jnp.float32) + out_vector.astype(
        jnp.float32
    )
    resid_first = sequence.astype(jnp.float32) + projected
    hidden = layernorm(resid_first, gain_first.astype(jnp.float32), shift_first.astype(jnp.float32))
    hidden_low = hidden.astype(jnp.bfloat16)
    preact = jnp.dot(hidden_low, up_full, preferred_element_type=jnp.float32) + up_vector.astype(
        jnp.float32
    )
    activ_low = jax.nn.gelu(preact, approximate=False).astype(jnp.bfloat16)
    branch = jnp.dot(activ_low, down_full, preferred_element_type=jnp.float32) + down_vector.astype(
        jnp.float32
    )
    resid_second = hidden + branch
    output = layernorm(
        resid_second, gain_second.astype(jnp.float32), shift_second.astype(jnp.float32)
    )
    saved = (
        query_flat,
        keys_flat,
        values_flat,
        attended,
        logsum,
        att_low,
        resid_first,
        hidden_low,
        preact,
        activ_low,
        resid_second,
    )
    return (output.astype(jnp.bfloat16), saved)


def body(
    tokens,
    cotangent,
    qkv_weight,
    out_weight,
    up_weight,
    down_weight,
    qkv_bias,
    out_bias,
    up_bias,
    down_bias,
    first_gain,
    first_shift,
    second_gain,
    second_shift,
):
    gathered = (
        lax.all_gather(qkv_weight, ("ctx", "fsdp"), axis=0, tiled=True),
        lax.all_gather(out_weight, ("ctx", "fsdp"), axis=0, tiled=True),
        lax.all_gather(up_weight, ("ctx", "fsdp"), axis=0, tiled=True),
        lax.all_gather(down_weight, ("ctx", "fsdp"), axis=0, tiled=True),
        lax.all_gather(qkv_bias, ("ctx", "fsdp"), axis=0, tiled=True),
        lax.all_gather(out_bias, ("ctx", "fsdp"), axis=0, tiled=True),
        lax.all_gather(up_bias, ("ctx", "fsdp"), axis=0, tiled=True),
        lax.all_gather(down_bias, ("ctx", "fsdp"), axis=0, tiled=True),
        lax.all_gather(first_gain, ("ctx", "fsdp"), axis=0, tiled=True),
        lax.all_gather(first_shift, ("ctx", "fsdp"), axis=0, tiled=True),
        lax.all_gather(second_gain, ("ctx", "fsdp"), axis=0, tiled=True),
        lax.all_gather(second_shift, ("ctx", "fsdp"), axis=0, tiled=True),
    )
    rows = tokens.shape[2]
    width = tokens.shape[3]
    cycle_size = lax.axis_size("ctx")
    group = rows * math.gcd(cycle_size, 8)
    length = rows * cycle_size
    position = (lax.axis_index("ctx") * rows + jnp.arange(rows)).astype(jnp.float32)
    cosine, sine = tables(position)
    outputs = []
    savings = []
    for micro_idx in range(MICRO):
        output, saved = forward_local(tokens[micro_idx, 0], gathered, cosine, sine, group)
        outputs.append(output)
        savings.append(saved)
    weights_back = (
        lax.all_gather(qkv_weight, ("ctx", "fsdp"), axis=0, tiled=True),
        lax.all_gather(out_weight, ("ctx", "fsdp"), axis=0, tiled=True),
        lax.all_gather(up_weight, ("ctx", "fsdp"), axis=0, tiled=True),
        lax.all_gather(down_weight, ("ctx", "fsdp"), axis=0, tiled=True),
        lax.all_gather(qkv_bias, ("ctx", "fsdp"), axis=0, tiled=True),
        lax.all_gather(out_bias, ("ctx", "fsdp"), axis=0, tiled=True),
        lax.all_gather(up_bias, ("ctx", "fsdp"), axis=0, tiled=True),
        lax.all_gather(down_bias, ("ctx", "fsdp"), axis=0, tiled=True),
        lax.all_gather(first_gain, ("ctx", "fsdp"), axis=0, tiled=True),
        lax.all_gather(first_shift, ("ctx", "fsdp"), axis=0, tiled=True),
        lax.all_gather(second_gain, ("ctx", "fsdp"), axis=0, tiled=True),
        lax.all_gather(second_shift, ("ctx", "fsdp"), axis=0, tiled=True),
    )
    (
        qkv_full,
        out_full,
        up_full,
        down_full,
        qkv_vector,
        out_vector,
        up_vector,
        down_vector,
        gain_first,
        shift_first,
        gain_second,
        shift_second,
    ) = weights_back
    token_grads = []
    totals = []
    for micro_idx in range(MICRO):
        (
            query_flat,
            keys_flat,
            values_flat,
            attended,
            logsum,
            att_low,
            resid_first,
            hidden_low,
            preact,
            activ_low,
            resid_second,
        ) = savings[micro_idx]
        sequence = tokens[micro_idx, 0]
        grad_out = cotangent[micro_idx, 0].astype(jnp.float32)
        unused_two, second_back = jax.vjp(
            layernorm,
            resid_second,
            gain_second.astype(jnp.float32),
            shift_second.astype(jnp.float32),
        )
        grad_second, second_gain_grad, second_shift_grad = second_back(grad_out)
        branch_grad = grad_second.astype(jnp.bfloat16)
        down_bias_grad = column_sum(branch_grad)
        down_weight_grad = jnp.einsum(
            "tf,td->fd", activ_low, branch_grad, preferred_element_type=jnp.float32
        )
        activ_grad = jnp.einsum(
            "td,fd->tf", branch_grad, down_full, preferred_element_type=jnp.float32
        )
        unused_gelu, gelu_back = jax.vjp(partial(jax.nn.gelu, approximate=False), preact)
        preact_grad = gelu_back(activ_grad)[0].astype(jnp.bfloat16)
        up_bias_grad = column_sum(preact_grad)
        up_weight_grad = jnp.einsum(
            "td,tf->df", hidden_low, preact_grad, preferred_element_type=jnp.float32
        )
        hidden_grad = grad_second + jnp.einsum(
            "tf,df->td", preact_grad, up_full, preferred_element_type=jnp.float32
        )
        unused_one, first_back = jax.vjp(
            layernorm, resid_first, gain_first.astype(jnp.float32), shift_first.astype(jnp.float32)
        )
        grad_first, first_gain_grad, first_shift_grad = first_back(hidden_grad)
        proj_grad = grad_first.astype(jnp.bfloat16)
        out_bias_grad = column_sum(proj_grad)
        out_weight_grad = jnp.einsum(
            "tc,te->ce", att_low, proj_grad, preferred_element_type=jnp.float32
        )
        att_grad = jnp.einsum(
            "te,ce->tc", proj_grad, out_full, preferred_element_type=jnp.float32
        ).astype(jnp.bfloat16)
        att_heads = split_heads(att_grad)
        query_heads = split_heads(query_flat)
        delta = jnp.sum(att_heads.astype(jnp.float32) * attended, axis=-1).T
        key_all, value_all = (
            lax.all_gather(keys_flat, "ctx", axis=0, tiled=True),
            lax.all_gather(values_flat, "ctx", axis=0, tiled=True),
        )

        def query_update(state, offset, size):
            key_block = split_heads(lax.dynamic_slice_in_dim(key_all, offset, size, 0))
            value_block = split_heads(lax.dynamic_slice_in_dim(value_all, offset, size, 0))
            scores = (
                jnp.einsum(
                    "qhd,khd->hqk", query_heads, key_block, preferred_element_type=jnp.float32
                )
                * 0.125
            )
            chance = jnp.exp(scores - logsum[:, :, None])
            dprob = jnp.einsum(
                "qhd,khd->hqk", att_heads, value_block, preferred_element_type=jnp.float32
            )
            score_grad = (chance * (dprob - delta[:, :, None])).astype(jnp.bfloat16)
            return state + jnp.einsum(
                "hqk,khd->qhd", score_grad, key_block, preferred_element_type=jnp.float32
            )

        query_grad = (
            over_blocks(query_update, jnp.zeros((rows, HEADS, HEAD), jnp.float32), length, group)
            * 0.125
        )

        def fill(state, offset, size):
            key_block = split_heads(lax.dynamic_slice_in_dim(key_all, offset, size, 0))
            value_block = split_heads(lax.dynamic_slice_in_dim(value_all, offset, size, 0))
            scores = (
                jnp.einsum(
                    "qhd,khd->hqk", query_heads, key_block, preferred_element_type=jnp.float32
                )
                * 0.125
            )
            chance = jnp.exp(scores - logsum[:, :, None])
            value_part = jnp.einsum(
                "hqk,qhd->khd",
                chance.astype(jnp.bfloat16),
                att_heads,
                preferred_element_type=jnp.float32,
            )
            dprob = jnp.einsum(
                "qhd,khd->hqk", att_heads, value_block, preferred_element_type=jnp.float32
            )
            score_grad = (chance * (dprob - delta[:, :, None])).astype(jnp.bfloat16)
            key_part = (
                jnp.einsum(
                    "hqk,qhd->khd", score_grad, query_heads, preferred_element_type=jnp.float32
                )
                * 0.125
            )
            piece = jnp.concatenate(
                [key_part.reshape(size, width), value_part.reshape(size, width)], axis=1
            )
            return lax.dynamic_update_slice_in_dim(state, piece, offset, 0)

        combined = lax.psum_scatter(
            over_blocks(
                fill,
                jnp.zeros((lax.axis_size("ctx") * rows, 2 * width), jnp.float32),
                lax.axis_size("ctx") * rows,
                group,
            ),
            "ctx",
            scatter_dimension=0,
            tiled=True,
        )
        key_grad = split_heads(combined[:, :width])
        value_grad = combined[:, width:]
        joined_grad = jnp.concatenate(
            [
                unrotate(query_grad, cosine, sine).reshape(rows, width),
                unrotate(key_grad, cosine, sine).reshape(rows, width),
                value_grad,
            ],
            axis=1,
        ).astype(jnp.bfloat16)
        qkv_bias_grad = column_sum(joined_grad)
        qkv_weight_grad = jnp.einsum(
            "tc,te->ce", sequence, joined_grad, preferred_element_type=jnp.float32
        )
        token_grads.append(
            grad_first
            + jnp.einsum("te,ce->tc", joined_grad, qkv_full, preferred_element_type=jnp.float32)
        )
        fresh = [
            qkv_weight_grad,
            out_weight_grad,
            up_weight_grad,
            down_weight_grad,
            qkv_bias_grad,
            out_bias_grad,
            up_bias_grad,
            down_bias_grad,
            first_gain_grad,
            first_shift_grad,
            second_gain_grad,
            second_shift_grad,
        ]
        if micro_idx == 0:
            totals = fresh
        else:
            totals = [older + newer for older, newer in zip(totals, fresh)]
    summed = (
        lax.psum_scatter(totals[0], ("ctx", "fsdp"), scatter_dimension=0, tiled=True),
        lax.psum_scatter(totals[1], ("ctx", "fsdp"), scatter_dimension=0, tiled=True),
        lax.psum_scatter(totals[2], ("ctx", "fsdp"), scatter_dimension=0, tiled=True),
        lax.psum_scatter(totals[3], ("ctx", "fsdp"), scatter_dimension=0, tiled=True),
        lax.psum_scatter(totals[4], ("ctx", "fsdp"), scatter_dimension=0, tiled=True),
        lax.psum_scatter(totals[5], ("ctx", "fsdp"), scatter_dimension=0, tiled=True),
        lax.psum_scatter(totals[6], ("ctx", "fsdp"), scatter_dimension=0, tiled=True),
        lax.psum_scatter(totals[7], ("ctx", "fsdp"), scatter_dimension=0, tiled=True),
        lax.psum_scatter(totals[8], ("ctx", "fsdp"), scatter_dimension=0, tiled=True),
        lax.psum_scatter(totals[9], ("ctx", "fsdp"), scatter_dimension=0, tiled=True),
        lax.psum_scatter(totals[10], ("ctx", "fsdp"), scatter_dimension=0, tiled=True),
        lax.psum_scatter(totals[11], ("ctx", "fsdp"), scatter_dimension=0, tiled=True),
    )
    output_all = jnp.stack(outputs)[:, None]
    token_all = jnp.stack(token_grads)[:, None]
    return (
        output_all,
        token_all,
        summed[0],
        summed[1],
        summed[2],
        summed[3],
        summed[4],
        summed[5],
        summed[6],
        summed[7],
        summed[8],
        summed[9],
        summed[10],
        summed[11],
    )


def solution(mesh):
    in_specs = (
        P(None, "fsdp", "ctx", None),
        P(None, "fsdp", "ctx", None),
        P(("ctx", "fsdp"), None),
        P(("ctx", "fsdp"), None),
        P(("ctx", "fsdp"), None),
        P(("ctx", "fsdp"), None),
        P(("ctx", "fsdp")),
        P(("ctx", "fsdp")),
        P(("ctx", "fsdp")),
        P(("ctx", "fsdp")),
        P(("ctx", "fsdp")),
        P(("ctx", "fsdp")),
        P(("ctx", "fsdp")),
        P(("ctx", "fsdp")),
    )
    out_specs = (
        P(None, "fsdp", "ctx", None),
        P(None, "fsdp", "ctx", None),
        P(("ctx", "fsdp"), None),
        P(("ctx", "fsdp"), None),
        P(("ctx", "fsdp"), None),
        P(("ctx", "fsdp"), None),
        P(("ctx", "fsdp")),
        P(("ctx", "fsdp")),
        P(("ctx", "fsdp")),
        P(("ctx", "fsdp")),
        P(("ctx", "fsdp")),
        P(("ctx", "fsdp")),
        P(("ctx", "fsdp")),
        P(("ctx", "fsdp")),
    )
    fused = mesh.shape["ctx"] == NCTX and mesh.shape["fsdp"] == 2
    return jax.shard_map(fused_body if fused else body, mesh=mesh, in_specs=in_specs, out_specs=out_specs, check_vma=False)
```

```python
from functools import partial
import math

import jax
import jax.numpy as jnp
from jax import lax
from jax.experimental import pallas as pl
from jax.experimental.pallas import tpu as pltpu
from jax.sharding import PartitionSpec as P
import numpy as np

HEADS = 16
HEAD = 64
MICRO = 2
MESH = pl.DeviceIdType.MESH
F32 = jnp.float32
BF16 = jnp.bfloat16


NCTX = 16
NCHIP = 8
BLK = 64
D = 1024
UNITS = 256
FF_UNITS = 512
CHUNK = 256
AQS = 4
RQS = 4
ROWS = BLK // RQS


def chip_at(place):
    row = lax.div(place, 4)
    return ((1 - row) * place + row * (7 - place)) * 2 + row


def nn(a, b):
    return jnp.dot(a, b, preferred_element_type=F32)


def nt(a, b):
    return lax.dot_general(a, b, (((1,), (1,)), ((), ())), preferred_element_type=F32)


def tn(a, b):
    return lax.dot_general(a, b, (((0,), (0,)), ((), ())), preferred_element_type=F32)


def row_mean(v):
    return jnp.sum(v, axis=1, keepdims=True) * (1.0 / D)


def col_sum(v):
    return jnp.sum(v, axis=0, keepdims=True)


def layer_kernel(
    x_ref, ct_ref, wq_ref, wo_ref, wu_ref, wd_ref, rope_ref, v0, v1, v2, v3, v4, v5, v6, v7,
    out_ref, tg_ref, RQ, go_ref, RU, gd_ref, gs_ref,
    VEC, XF, HF, BG, WP, WB, WUS, WU, WO, WD, VB, VF, UB, QBR, BQ, WHT, QT, KT, VT, KN, VN, PT, ATD, ATS, AT, AGT,
    H1, Z1, R1, SEC, G2, DG, ACT, PG, PB, SS, SR, RSD, RR, TT,
    GU, PUS, DWU, DWD, ZRU, ZRD, GO, XSO, XRO, SSO, SRO, SG, SGR, SGT, SGC, AGQ,
    DK, DV, JG, XSQ, XRQ, AQ, QBP,
    one, ag_r, ss_r, rs_r, wo_r, all_s, all_r, pair_s, pair_r, plane_s, plane_r,
    pa_r, pb_r, ps_r, pr_r, z_s, z_r, q_s, q_r,
):
    c = lax.axis_index("ctx")
    f = lax.axis_index("fsdp")
    core = lax.rem(c, 2)
    chip = lax.div(c, 2)
    yy = lax.rem(chip, 2)
    zz = lax.div(chip, 2)
    r = (1 - yy) * zz + yy * (7 - zz)
    nxt = chip_at(lax.rem(r + 1, 8)) * 2 + core
    prv = chip_at(lax.rem(r + 7, 8)) * 2 + core
    sib = c + 1 - 2 * core
    mine = pl.multiple_of(core * BLK, BLK)
    other = pl.multiple_of((1 - core) * BLK, BLK)
    lane = lax.broadcasted_iota(jnp.int32, (1, 128), 1)
    low_half = lane < 64

    def remote(src, dst, ss, rs, axis, to):
        return pltpu.make_async_remote_copy(
            src_ref=src, dst_ref=dst, send_sem=ss, recv_sem=rs, device_id={axis: to}, device_id_type=MESH
        )

    def target(d):
        return nxt if d == 0 else prv

    def chip_of(d, k):
        return chip_at(lax.rem(r - k + 8, 8) if d == 0 else lax.rem(r + k, 8))

    def send_all(e, src_at, dst):
        @pl.loop(1, NCTX)
        def _(o):
            to = lax.rem(c + o, NCTX)
            remote(src_at(to), dst, all_s.at[e], all_r.at[e], "ctx", to).start()

    def recv_all(e, slab):
        remote(slab, slab, all_s.at[e], all_r.at[e], "ctx", sib).wait_recv()

    def sent_all(e, slab):
        remote(slab, slab, all_s.at[e], all_r.at[e], "ctx", sib).wait_send()

    pp = lax.rem(c, 4) * 2 + f
    grp = yy * 2 + f

    def send_plane(e, src_at, dst):
        @pl.loop(1, 8)
        def _(o):
            to = lax.rem(pp + o, 8)
            pltpu.make_async_remote_copy(
                src_ref=src_at(to), dst_ref=dst, send_sem=plane_s.at[e], recv_sem=plane_r.at[e],
                device_id={"ctx": zz * 4 + lax.div(to, 2), "fsdp": lax.rem(to, 2)}, device_id_type=MESH,
            ).start()

    def recv_plane(e, slab):
        remote(slab, slab, plane_s.at[e], plane_r.at[e], "ctx", sib).wait_recv()

    def sent_plane(e, slab):
        remote(slab, slab, plane_s.at[e], plane_r.at[e], "ctx", sib).wait_send()

    def at_plane(body):
        for place in range(4):

            @pl.when(zz == place)
            def _():
                body(place)

    def z_block(kd, b, dr, s, place):
        at = WU.at[b, pl.ds(4 * kd, 4)] if kd < 2 else WD.at[b, pl.ds(64 * kd - 128, 64)]
        return remote(at, at, z_s.at[kd, dr * 3 + s], z_r.at[kd, b], "ctx", c + (4 if dr == 0 else -4))

    def z_gather(kd, s, sent=False):
        def body(place):
            for dr in range(2):
                b = place - s if dr == 0 else place + s
                more = place < 3 if dr == 0 else place > 0
                if not 0 <= b < 4:
                    continue
                if s > 0 and not sent:
                    z_block(kd, b, dr, s - 1, place).wait_recv()
                if s < 3 and more:
                    copy = z_block(kd, b, dr, s, place)
                    copy.wait_send() if sent else copy.start()

        at_plane(body)

    def z_slot(source, t):
        return (source - t) % 4 - 1

    def z_term(kd, t, there, slot, place):
        src, got = ((DWU, ZRU), (DWD, ZRD))[kd]
        return remote(src.at[t], got.at[slot], q_s.at[kd, t], q_r.at[kd, slot], "ctx", c + 4 * (there - place))

    def z_start(kd, sent=False):
        def body(place):
            for t in (3, 2, 1, 0) if place < 2 else (0, 1, 2, 3):
                if t == place or (place, t) in ((1, 3), (2, 0)):
                    continue
                far = (place, t) in ((0, 3), (3, 0))
                there = (1 if place == 0 else 2) if far else t
                copy = z_term(kd, t, there, 3 if far else z_slot(place, t), place)
                copy.wait_send() if sent else copy.start()

        at_plane(body)

    def z_relay(kd, sent=False):
        def body(place):
            if place in (1, 2):
                t = 3 if place == 1 else 0
                src, got = ((DWU, ZRU), (DWD, ZRD))[kd]
                copy = z_term(kd, t, t, z_slot(place, t), place)
                if sent:
                    copy.wait_send()
                else:
                    z_term(kd, t, t, 3, place).wait_recv()
                    src[t] = (src[t].astype(F32) + got[3].astype(F32)).astype(BF16)
                    copy.start()

        at_plane(body)

    def z_total(kd, put):
        def body(place):
            src, got = ((DWU, ZRU), (DWD, ZRD))[kd]
            total = src[place].astype(F32)
            for source in range(4):
                if source != place and (source, place) not in ((0, 3), (3, 0)):
                    slot = z_slot(source, place)
                    z_term(kd, place, place, slot, place).wait_recv()
                    total = total + got[slot].astype(F32)
            put(total)

        at_plane(body)

    def pair(i, src, dst):
        return remote(src, dst, pair_s.at[i], pair_r.at[i], "fsdp", 1 - f)

    agx_s, sbx_s, sbx_r, ss_s, rs_s, wo_s, wos_s, wos_r, po_s, po_r, pa_s, pb_s, ps_s, pr_s = (one.at[i] for i in range(14))
    barrier = pltpu.get_barrier_semaphore()

    @pl.loop(1, NCTX)
    def _(o):
        pl.semaphore_signal(barrier, inc=1, device_id={"ctx": lax.rem(c + o, NCTX)}, device_id_type=MESH)

    @pl.loop(0, 4)
    def _(o):
        there = lax.div(c, 4) * 4 + lax.rem(c + o, 4)
        pl.semaphore_signal(barrier, inc=1, device_id={"ctx": there, "fsdp": 1 - f}, device_id_type=MESH)

    pl.semaphore_wait(barrier, NCTX + 3)

    def block(buf, m, ch, row0):
        return buf.at[m, ch, pl.ds(row0, BLK)]

    def sub(m, ch, q):
        return XF.at[m, ch, pl.ds(pl.multiple_of(core * BLK + (BLK // AQS) * q, BLK // AQS), BLK // AQS)]

    for m in range(2):
        XF[m, chip, pl.ds(mine, BLK)] = x_ref[m]
    WO[chip, core, f] = wo_ref[...]
    WD[zz] = wd_ref[...]
    VEC[...] = jnp.zeros((8, 128), F32)
    for i, v in enumerate((v0, v1, v2, v3, v4, v5, v6, v7)):
        VEC[i : i + 1, 0 : v.shape[1]] = v[...].astype(F32)
    VB[c, f] = VEC[...]

    def gather_x(k):
        for d in range(2):
            ch = chip_of(d, k)
            for q in range(AQS):
                at = sub(d, ch, q)

                @pl.when(k > 0)
                def _():
                    remote(at, at, agx_s, ag_r.at[d, (k - 1) * AQS + q], "ctx", target(d)).wait_recv()

                @pl.when(k < 7)
                def _():
                    remote(at, at, agx_s, ag_r.at[d, k * AQS + q], "ctx", target(d)).start()

            whole = block(XF, d, ch, mine)
            remote(whole, whole, sbx_s, sbx_r, "ctx", sib).start()

    def gather_wo(k):
        for d in range(2):
            at = WO.at[chip_of(d, k), core, f, pl.ds(16 * d, 16)]

            @pl.when(k > 0)
            def _():
                remote(at, at, wo_s, wo_r.at[d, k - 1], "ctx", target(d)).wait_recv()

            @pl.when(k < 7)
            def _():
                remote(at, at, wo_s, wo_r.at[d, k], "ctx", target(d)).start()

            pair(1, at, at).start()

    pl.loop(0, 1)(gather_x)
    pair(0, VEC, VB.at[c, f]).start()

    for j in range(8):
        qt = wq_ref[:, 128 * j : 128 * j + 128].astype(F32)
        kt = wq_ref[:, D + 128 * j : D + 128 * j + 128].astype(F32)
        vt = wq_ref[:, 2 * D + 128 * j : 2 * D + 128 * j + 128].astype(F32)
        for e in range(2):
            w = 2 * j + e
            qk = jnp.where(low_half, qt, pltpu.roll(kt, 64, 1)) if e == 0 else jnp.where(low_half, pltpu.roll(qt, 64, 1), kt)
            WP[w, :, 0:128] = qk.astype(BF16)
            WP[w, :, 128:256] = (vt if e == 0 else pltpu.roll(vt, 64, 1)).astype(BF16)
    WB[c, f] = WP[c]
    send_all(0, lambda to: WP.at[to], WB.at[c, f])
    for w in range(8):
        for i in range(4):
            WUS[w, :, 128 * i : 128 * (i + 1)] = wu_ref[:, 128 * (8 * i + w) : 128 * (8 * i + w + 1)]
    WU[zz, pp] = WUS[pp]
    send_plane(0, lambda to: WUS.at[to], WU.at[zz, pp])

    @pl.loop(1, 4)
    def _(k):
        gather_x(k)
        gather_wo(k - 1)

    pair(0, VB.at[c, 1 - f], VB.at[c, 1 - f]).wait_recv()
    send_all(1, lambda to: VB.at[c], VB.at[c])
    recv_all(0, WB.at[0:15, 0])
    pair(3, WB.at[:, f], WB.at[:, f]).start()
    recv_plane(0, WU.at[zz, 0:7])

    def head_weights():
        pair(3, WB.at[:, 1 - f], WB.at[:, 1 - f]).wait_recv()
        WHT[...] = WB[...].reshape(D, 256).T

    def vectors():
        recv_all(1, VB.at[0:15])
        for j in range(8):
            tiles = [VB[2 * j + q // 2, q % 2] for q in range(4)]
            total = tiles[0]
            for q in range(1, 4):
                total = total + pltpu.roll(tiles[q], 32 * q, 1)
            VF[:, 128 * j : 128 * j + 128] = total
            v1 = pltpu.roll(tiles[1], 96, 1)
            v2 = pltpu.roll(tiles[2], 64, 1)
            v3 = pltpu.roll(tiles[3], 32, 1)
            rows = (
                tiles[0] + jnp.where(lane >= 96, v1, 0.0),
                jnp.where(lane < 64, v1, 0.0) + jnp.where(lane >= 64, v2, 0.0),
                jnp.where(lane < 32, v2, 0.0) + v3,
            )
            for i in range(3):
                QBR[3 * j + i : 3 * j + i + 1, :] = rows[i][1:2, :]
        for i in range(4):
            UB[0:1, 128 * i : 128 * (i + 1)] = VB[4 * i + lax.rem(c, 4), f, 0:1, :]
        for i in range(3):
            row = QBR[pl.ds(8 * i + chip, 1), :]
            BQ[i] = jnp.broadcast_to(row, (128, 128)).T

    @pl.loop(4, 8)
    def _(k):
        gather_x(k)
        gather_wo(k - 1)
        pl.when(k == 6)(vectors)
        pl.when(k == 7)(head_weights)

        @pl.when(k == 6)
        def _():
            z_gather(0, 0)
            z_gather(1, 0)


    gather_wo(jnp.int32(7))
    z_gather(2, 0)
    z_gather(3, 0)
    remote(XF.at[0], XF.at[0], sbx_s, sbx_r, "ctx", sib).wait_recv()


    def lanes(n):
        return pl.ds(pl.multiple_of(n * CHUNK, CHUNK), CHUNK)

    def turn(u, cosine, sine):
        a, b = u[0:32], u[32:64]
        return jnp.concatenate([a * cosine - b * sine, b * cosine + a * sine], axis=0)

    def unturn(u, cosine, sine):
        a, b = u[0:32], u[32:64]
        return jnp.concatenate([a * cosine + b * sine, b * cosine - a * sine], axis=0)

    @pl.loop(0, 8)
    def _(it):
        m = lax.div(it, 4)
        n = lax.rem(it, 4)
        xs = XF[m, pl.ds(2 * n, 2)].reshape(CHUNK, D)
        joined = nt(WHT[0:192, :], xs)
        cosine = rope_ref[0, :, lanes(n)]
        sine = rope_ref[1, :, lanes(n)]
        q = joined[0:64] + BQ[0, pl.ds(mine, BLK), 0:1]
        k = joined[64:128] + BQ[1, pl.ds(mine, BLK), 0:1]
        v = joined[128:192] + BQ[2, pl.ds(mine, BLK), 0:1]
        q = turn(q, cosine, sine)
        k = turn(k, cosine, sine)
        rows = pl.ds(pl.multiple_of(n * CHUNK, CHUNK), CHUNK)
        QT[m, :, lanes(n)] = (q.astype(BF16).astype(F32) * 0.125).astype(BF16)
        KT[m, :, lanes(n)] = k.astype(BF16)
        VT[m, :, lanes(n)] = v.astype(BF16)
        KN[m, rows, :] = k.T.astype(BF16)
        VN[m, rows, :] = v.T.astype(BF16)

    @pl.loop(0, 8)
    def _(it):
        @pl.when(it == 0)
        def _():
            z_gather(0, 1)
            z_gather(1, 1)

        @pl.when(it == 4)
        def _():
            z_gather(2, 1)
            z_gather(3, 1)

        @pl.when(it == 3)
        def _():
            pair(1, WO.at[:, core, 1 - f], WO.at[:, core, 1 - f]).wait_recv()
            remote(WO.at[:, core], WO.at[:, core], wos_s, wos_r, "ctx", sib).start()

        m = lax.div(it, 4)
        n = lax.rem(it, 4)
        s = nn(KN[m], QT[m, :, lanes(n)])
        e = jnp.exp(s - jnp.max(s, axis=0, keepdims=True))
        p = (e * (1.0 / jnp.sum(e, axis=0, keepdims=True))).astype(BF16)
        PT[m, :, lanes(n)] = p
        ATD[m, :, lanes(n)] = nn(VT[m], p)

    for j in range(8):
        a0 = ATD[0, :, 128 * j : 128 * j + 128]
        a1 = ATD[1, :, 128 * j : 128 * j + 128]
        ATS[2 * j] = jnp.where(low_half, a0, pltpu.roll(a1, 64, 1)).astype(BF16)
        ATS[2 * j + 1] = jnp.where(low_half, pltpu.roll(a0, 64, 1), a1).astype(BF16)
    AT[c] = ATS[c]
    send_all(2, lambda to: ATS.at[to], AT.at[c])

    z_gather(0, 2)
    z_gather(1, 2)
    remote(WO.at[:, 1 - core], WO.at[:, 1 - core], wos_s, wos_r, "ctx", sib).wait_recv()
    recv_all(2, AT.at[0:15])

    z_gather(2, 2)
    z_gather(3, 2)
    att_rows = AT[...].reshape(D, 128).T
    resid = x_ref[...].reshape(128, D).astype(F32) + nn(att_rows, WO[...].reshape(D, D)) + VF[2:3, :]
    center = resid - row_mean(resid)
    root = lax.rsqrt(row_mean(center * center) + 1e-05)
    z = center * root
    hidden = z * VF[4:5, :] + VF[5:6, :]
    Z1[...] = z
    R1[...] = jnp.broadcast_to(root, (128, 128))
    H1[...] = hidden
    hidden_low = hidden.astype(BF16)
    for m in range(2):
        HF[grp, m, pl.ds(mine, BLK)] = hidden_low[m * BLK : (m + 1) * BLK]

    def plane(buf, make, early, ready, after_one, after_two, finish):
        far = ((yy * 2 + 1 - f), ((1 - yy) * 2 + f))
        groups = tuple((grp, far[m], far[1 - m], (1 - yy) * 2 + 1 - f) for m in range(2))

        def to(axis, src, dst, ss, rs):
            if axis == 0:
                return remote(src, dst, ss, rs, "fsdp", 1 - f)
            return remote(src, dst, ss, rs, "ctx", c + 2 - 4 * yy)

        def at(m, i, row0):
            return buf.at[groups[m][i], m, pl.ds(row0, BLK)]

        def hand_over(m, i):
            remote(at(m, i, mine), at(m, i, mine), pb_s, pb_r.at[m, i], "ctx", sib).start()

        def arrive(m, i, n):
            to(m, at(m, i, mine), at(m, i, mine), pa_s, pa_r.at[m, n]).wait_recv()

        def half(m, i, h):
            return buf.at[groups[m][i], m, pl.ds(pl.multiple_of(core * BLK + 32 * h, 32), 32)]

        def work(places):
            part = make(groups[0][places[0]])
            for m in range(2):
                PB[m, places[m]] = part[128 * m : 128 * (m + 1)]
            for m in range(2):
                i = places[m]
                SS[m, i] = PB[m, i, pl.ds(other, BLK)].astype(BF16)
                remote(SS.at[m, i], SR.at[m, i], ps_s, ps_r.at[m, i], "ctx", sib).start()

        def both(m, i):
            remote(at(m, i, other), at(m, i, other), pb_s, pb_r.at[m, i], "ctx", sib).wait_recv()

        def share(m, i):
            remote(SR.at[m, i], SR.at[m, i], ps_s, ps_r.at[m, i], "ctx", sib).wait_recv()
            return PB[m, i, pl.ds(mine, BLK)] + SR[m, i].astype(F32)

        def push(m, n, value, axis):
            for h in range(2):
                rows = pl.ds(32 * h, 32)
                RSD[m, n, rows] = value[32 * h : 32 * (h + 1)].astype(BF16)
                to(axis, RSD.at[m, n, rows], RR.at[m, n, rows], pr_s, pr_r.at[m, 2 * n + h]).start()

        def pulled(m, n, h):
            got = RR.at[m, n, pl.ds(32 * h, 32)]
            to(m, got, got, pr_s, pr_r.at[m, 2 * n + h]).wait_recv()
            return RR[m, n, 32 * h : 32 * (h + 1)].astype(F32)

        def pulled_all(m, n):
            return jnp.concatenate([pulled(m, n, h) for h in range(2)], axis=0)

        for m in range(2):
            for h in range(2):
                to(m, half(m, 0, h), half(m, 0, h), pa_s, pa_r.at[m, 3 * h]).start()
        for m in range(2):
            hand_over(m, 0)
            to(1 - m, at(m, 0, mine), at(m, 0, mine), pa_s, pa_r.at[m, 1]).start()
        for m in range(2):
            both(m, 0)
        if early is not None:
            work((0, 0))
        for m in range(2):
            for h in range(2):
                to(m, half(m, 1, h), half(m, 1, h), pa_s, pa_r.at[m, 3 * h]).wait_recv()
                to(1 - m, half(m, 1, h), half(m, 1, h), pa_s, pa_r.at[m, 2 + 2 * h]).start()
            hand_over(m, 1)
        for m in range(2):
            arrive(m, 2, 1)
            hand_over(m, 2)
        for i in (1, 2):
            for m in range(2):
                both(m, i)
        if early is not None:
            work((1, 2))
        for m in range(2):
            for h in range(2):
                to(m, half(m, 3, h), half(m, 3, h), pa_s, pa_r.at[m, 2 + 2 * h]).wait_recv()
            hand_over(m, 3)
        if early is not None:
            work((2, 1))
        for m in range(2):
            both(m, 3)
        if ready is not None:
            ready()
        work((3, 3))
        if early is not None:
            early()
        else:
            work((1, 2))
        for m in range(2):
            push(m, 1, share(m, 3), 1 - m)
        if early is None:
            work((2, 1))
        for m in range(2):
            push(m, 0, share(m, 2), 1 - m)
        if early is None:
            work((0, 0))
        after_one()
        for m in range(2):
            value = share(m, 1)
            for h in range(2):
                rows = pl.ds(32 * h, 32)
                RSD[m, 2, rows] = (value[32 * h : 32 * (h + 1)] + pulled(m, 1, h)).astype(BF16)
                to(m, RSD.at[m, 2, rows], RR.at[m, 2, rows], pr_s, pr_r.at[m, 4 + h]).start()
        after_two()
        for m in range(2):
            finish(m, share(m, 0) + pulled_all(m, 0) + pulled_all(m, 2))
        remote(XF.at[0, 0:3], XF.at[0, 0:3], pa_s, sbx_r, "ctx", sib).wait_send()
        remote(XF.at[0, 0:4], XF.at[0, 0:4], pb_s, sbx_r, "ctx", sib).wait_send()
        remote(XF.at[0, 0:4], XF.at[0, 0:4], ps_s, sbx_r, "ctx", sib).wait_send()
        remote(XF.at[0, 0:3], XF.at[0, 0:3], pr_s, sbx_r, "ctx", sib).wait_send()

    def ring(make, extra, finish):
        def first(k):
            slot = 2 - lax.div(k + 7, 8) * (2 - lax.rem(k, 2))
            for d in range(2):
                ch = chip_of(d, k)
                PB[d, slot] = make(d, ch)
                SS[d, k] = PB[d, slot, pl.ds(other, BLK)].astype(BF16)
                remote(SS.at[d, k], SR.at[d, k], ss_s, ss_r.at[d, k], "ctx", sib).start()

        def sums(d, k):
            at = SR.at[d, k]
            remote(at, at, ss_s, ss_r.at[d, k], "ctx", sib).wait_recv()

        def arrived(d, q, k):
            got = RR.at[d, k, rows_of(q)]
            remote(got, got, rs_s, rs_r.at[d, k * RQS + q], "ctx", sib).wait_recv()

        def rows_of(q):
            return pl.ds(q * ROWS, ROWS if q < RQS - 1 else ROWS + 16)

        def second(k):
            slot = lax.rem(k, 2)
            pl.when(k == 1)(lambda: pair(5, XRO, XRO).wait_recv())
            for d in range(2):
                sums(d, k)
            for q in range(RQS):
                for d in range(2):
                    part = pl.ds(q * ROWS, ROWS)
                    total = PB[d, slot, pl.ds(pl.multiple_of(core * BLK + q * ROWS, ROWS), ROWS)] + SR[d, k, part].astype(F32)
                    rider = q == RQS - 1
                    if rider:
                        ride = riders(d, chip_of(d, k))

                    @pl.when(k > 1)
                    def _():
                        arrived(d, q, k - 1)
                        RSD[d, k, part] = (total + RR[d, k - 1, part].astype(F32)).astype(BF16)
                        if rider:
                            RSD[d, k, BLK : BLK + 16] = (ride + RR[d, k - 1, BLK : BLK + 16].astype(F32)).astype(BF16)

                    @pl.when(k == 1)
                    def _():
                        RSD[d, k, part] = total.astype(BF16)
                        if rider:
                            RSD[d, k, BLK : BLK + 16] = ride.astype(BF16)

                    remote(
                        RSD.at[d, k, rows_of(q)], RR.at[d, k, rows_of(q)], rs_s, rs_r.at[d, k * RQS + q],
                        "ctx", target(d),
                    ).start()

        @pl.loop(0, 9)
        def _(it):
            @pl.when(it < 8)
            def _():
                first(it)

            @pl.when(it > 1)
            def _():
                second(it - 1)

            extra(it)

        for d in range(2):
            sums(d, 0)
            for q in range(RQS):
                arrived(d, q, 7)
            finish(d, PB[d, 2, pl.ds(mine, BLK)] + SR[d, 0].astype(F32) + RR[d, 7, 0:BLK].astype(F32))

        remote(SS, SS, ss_s, sbx_r, "ctx", sib).wait_send()
        remote(RSD.at[:, 0:7], RSD.at[:, 0:7], rs_s, sbx_r, "ctx", sib).wait_send()

    def nothing():
        pass

    def up_w():
        return WU[...].reshape(D, FF_UNITS)

    def down_w():
        return WD[...].reshape(FF_UNITS, D)

    def make_up(g):
        u = nn(HF[g].reshape(256, D), up_w()) + UB[0:1, :]
        phi = 0.5 * (1.0 + lax.erf(u * 0.7071067811865476))
        a = (u * phi).astype(BF16)
        DG[g] = (phi + u * (jnp.exp(-0.5 * u * u) * 0.3989422804014327)).reshape(2, 128, FF_UNITS)
        ACT[g] = a.reshape(2, 128, FF_UNITS)
        return nn(a, down_w())

    def finish_up(d, total):
        rows = slice(d * BLK, (d + 1) * BLK)
        SEC[rows, :] = H1[rows, :] + total + VF[3:4, :]

    def weights_in():
        for kd in range(4):
            z_gather(kd, 3)

    plane(HF, make_up, None, weights_in, nothing, nothing, finish_up)

    resid = SEC[...]
    center = resid - row_mean(resid)
    root = lax.rsqrt(row_mean(center * center) + 1e-05)
    z = center * root
    out_ref[...] = (z * VF[6:7, :] + VF[7:8, :]).astype(BF16).reshape(2, BLK, D)
    cot = ct_ref[...].reshape(128, D).astype(F32)
    SG[...] = jnp.zeros((8, D), F32)
    SG[4:5, :] = col_sum(cot * z)
    SG[5:6, :] = col_sum(cot)
    u = cot * VF[6:7, :]
    grad = (u - row_mean(u) - z * row_mean(u * z)) * root
    G2[...] = grad
    grad_low = grad.astype(BF16)
    SG[1:2, :] = col_sum(grad_low.astype(F32))
    for m in range(2):
        BG[grp, m, pl.ds(mine, BLK)] = grad_low[m * BLK : (m + 1) * BLK]

    def make_down(g):
        pg = (nt(BG[g].reshape(256, D), down_w()) * DG[g].reshape(256, FF_UNITS)).astype(BF16)
        PG[g] = pg.reshape(2, 128, FF_UNITS)
        return nt(pg, up_w())

    def finish_down(d, total):
        rows = slice(d * BLK, (d + 1) * BLK)
        SEC[rows, :] = G2[rows, :] + total

    def down_grads():
        TT[...] = ACT[...].reshape(1024, FF_UNITS).T
        for i in range(4):
            DWD[i] = nn(TT[128 * i : 128 * (i + 1), :], BG[...].reshape(1024, D)).astype(BF16)
        z_start(1)

    def up_grads():
        TT[...] = PG[...].reshape(1024, FF_UNITS).T
        for i in range(4):
            g = nn(TT[...], HF[:, :, :, CHUNK * i : CHUNK * (i + 1)].reshape(1024, CHUNK))
            DWU[i] = g.T.astype(BF16).reshape(8, 32, FF_UNITS)
        sums = nn(jnp.ones((8, 1024), BF16), PG[...].reshape(1024, FF_UNITS))[0:1, :]
        for i in range(8):
            SG[6:7, 128 * i : 128 * (i + 1)] = sums[:, 128 * (i // 2) : 128 * (i // 2) + 128]

    plane(BG, make_down, nothing, down_grads, nothing, up_grads, finish_down)

    hid = SEC[...]
    z = Z1[...]
    SG[2:3, :] = col_sum(hid * z)
    SG[3:4, :] = col_sum(hid)
    u = hid * VF[4:5, :]
    grad = (u - row_mean(u) - z * row_mean(u * z)) * R1[:, 0:1]
    H1[...] = grad
    proj = grad.astype(BF16)
    SG[0:1, :] = col_sum(proj.astype(F32))
    sent_all(2, ATS.at[0:15])
    ATS[...] = nt(WO[...].reshape(D, D), proj).astype(BF16).reshape(NCTX, HEAD, 128)
    AGT[c] = ATS[c]
    send_all(3, lambda to: ATS.at[to], AGT.at[c])
    z_start(0)

    for j in range(NCHIP):
        SSO[j] = nn(AT[2 * j + 1 - core], proj).astype(BF16)
    remote(SSO, SRO, po_s, po_r, "ctx", sib).start()
    pair(4, SG, SGR).start()
    for j in range(NCHIP):
        GO[j] = nn(AT[2 * j + core], proj)
    remote(SRO, SRO, po_s, po_r, "ctx", sib).wait_recv()
    for j in range(NCHIP):
        GO[j] = GO[j] + SRO[j].astype(F32)
        XSO[j] = GO[j, pl.ds(pl.multiple_of((1 - f) * 32, 32), 32)].astype(BF16)
    pair(5, XSO, XRO).start()
    recv_all(3, AGT.at[0:15])
    sent_all(3, ATS.at[0:15])

    for j in range(8):
        t0 = AGT[2 * j].astype(F32)
        t1 = AGT[2 * j + 1].astype(F32)
        AGQ[0, :, 128 * j : 128 * j + 128] = jnp.where(low_half, t0, pltpu.roll(t1, 64, 1)).astype(BF16)
        AGQ[1, :, 128 * j : 128 * j + 128] = jnp.where(low_half, pltpu.roll(t0, 64, 1), t1).astype(BF16)

    DK[...] = jnp.zeros((2, HEAD, D), F32)
    DV[...] = jnp.zeros((2, HEAD, D), F32)

    def small_push():
        pair(4, SGR, SGR).wait_recv()
        SGT[...] = SG[...] + SGR[...]
        SGT[6:7, :] = SG[6:7, :]
        SGC[c] = SGT[:, pl.ds(pl.multiple_of(chip * 128, 128), 128)]
        send_all(4, lambda to: SGT.at[:, pl.ds(pl.multiple_of(lax.div(to, 2) * 128, 128), 128)], SGC.at[c])

    def up_push():
        def put(total):
            PUS[...] = total.astype(BF16)

        z_total(0, put)
        RU[pp] = PUS[pp]
        send_plane(1, lambda to: PUS.at[to], RU.at[pp])

    @pl.loop(0, 8)
    def _(it):
        pl.when(it == 2)(small_push)
        pl.when(it == 0)(lambda: z_relay(1))
        pl.when(it == 7)(lambda: z_relay(0))
        m = lax.div(it, 4)
        n = lax.rem(it, 4)
        q = QT[m, :, lanes(n)]
        g = AGQ[m, :, lanes(n)]
        delta = jnp.sum(g.astype(F32) * ATD[m, :, lanes(n)], axis=0, keepdims=True)
        p = PT[m, :, lanes(n)]
        ds = (p.astype(F32) * (nn(VN[m], g) - delta)).astype(BF16)
        DK[m] = DK[m] + nt(q, ds)
        DV[m] = DV[m] + nt(g, p)
        dq = nn(KT[m], ds) * 0.125
        JG[m, 0:64, lanes(n)] = unturn(dq, rope_ref[0, :, lanes(n)], rope_ref[1, :, lanes(n)]).astype(BF16)

    for m in range(2):
        JG[m, 64:128, :] = unturn(DK[m], rope_ref[0], rope_ref[1]).astype(BF16)
        JG[m, 128:192, :] = DV[m].astype(BF16)

    def make_token(m, ch):
        jg = JG[m, :, pl.ds(pl.multiple_of(ch * 128, 128), 128)]
        return tn(jg, WHT[0:192, :])

    def finish_token(d, total):
        tg_ref[d] = H1[d * BLK : (d + 1) * BLK, :] + total
        go_ref[16 * d : 16 * d + 16, :] = riders(d, chip) + RR[d, 7, BLK : BLK + 16].astype(F32)

    def qkv_bias_rows():
        b = nt(jnp.ones((8, D), BF16), JG[0]) + nt(jnp.ones((8, D), BF16), JG[1])
        b = jnp.concatenate([b, jnp.zeros((8, 64), F32)], axis=1)
        QBP[...] = jnp.zeros((32, UNITS), F32)
        QBP[0:1, 128:256] = jnp.where(low_half, 0.0, pltpu.roll(b[0:1, 0:128], 64, 1))
        QBP[1:2, 128:256] = jnp.where(low_half, 0.0, b[0:1, 0:128])
        QBP[2:3, 128:256] = jnp.where(low_half, 0.0, pltpu.roll(b[0:1, 128:256], 64, 1))

    def qkv_grad(n):
        cols = slice(CHUNK * n, CHUNK * (n + 1))
        g = nn(JG[0], XF[0, :, :, cols].reshape(D, CHUNK)) + nn(JG[1], XF[1, :, :, cols].reshape(D, CHUNK))
        g = jnp.concatenate([g, jnp.zeros((64, CHUNK), F32)], axis=0)
        GU[4 * n : 4 * n + 4] = g.T.reshape(4, 2, 32, UNITS) + QBP[...]

    def qkv_pair():
        XSQ[...] = GU[:, 1 - f].astype(BF16)
        pair(8, XSQ, XRQ).start()

    def qkv_push():
        pair(8, XRQ, XRQ).wait_recv()
        AQ[...] = (GU[:, f] + XRQ[...].astype(F32)).astype(BF16)
        RQ[c] = AQ[c]
        send_all(6, lambda to: AQ.at[to], RQ.at[c])

    def riders(d, ch):
        return GO[ch, pl.ds(pl.multiple_of(f * 32 + 16 * d, 16), 16)] + XRO[ch, 16 * d : 16 * d + 16].astype(F32)

    def small_rest():
        recv_all(4, SGC.at[0:15])
        total = SGC[0]
        for w in range(1, NCTX):
            total = total + SGC[w]
        gs_ref[...] = total
        here = lax.rem(c, 4)
        gs_ref[6:7, :] = SGC[here, 6:7, :] + SGC[4 + here, 6:7, :] + SGC[8 + here, 6:7, :] + SGC[12 + here, 6:7, :]

    def down_rest():
        def put(total):
            gd_ref[...] = total

        z_total(1, put)

    def on_the_way(it):
        pl.when(it == 0)(qkv_bias_rows)
        for n in range(4):
            pl.when(it == n)(partial(qkv_grad, n))
        pl.when(it == 3)(qkv_pair)
        pl.when(it == 4)(small_rest)
        pl.when(it == 5)(qkv_push)
        pl.when(it == 6)(down_rest)
        pl.when(it == 8)(up_push)

    ring(make_token, on_the_way, finish_token)
    recv_plane(1, RU.at[0:7])
    recv_all(6, RQ.at[0:15])

    remote(XF.at[0, 0:7], XF.at[0, 0:7], agx_s, sbx_r, "ctx", sib).wait_send()
    remote(XF.at[0], XF.at[0], sbx_s, sbx_r, "ctx", sib).wait_send()
    remote(WO.at[0:7, 0, 0], WO.at[0:7, 0, 0], wo_s, sbx_r, "ctx", sib).wait_send()
    remote(WO.at[:, 0], WO.at[:, 0], wos_s, sbx_r, "ctx", sib).wait_send()
    sent_all(0, WP.at[0:15])
    sent_all(1, VB.at[0:15])
    sent_all(4, SGC.at[0:15])
    sent_all(6, AQ.at[0:15])
    remote(SSO, SSO, po_s, po_r, "ctx", sib).wait_send()
    sent_plane(0, WUS.at[0:7])
    sent_plane(1, PUS.at[0:7])
    for kd in range(2):
        for s in range(3):
            z_gather(kd, s, True)
            z_gather(kd + 2, s, True)
        z_start(kd, True)
        z_relay(kd, True)
    for i, at in ((0, VEC), (1, WO.at[:, core, f]), (3, WB.at[:, f]), (4, SG), (5, XSO), (8, XSQ)):
        pair(i, at, at).wait_send()


def rope_tables():
    freqs = (np.float32(10000.0) ** (-np.arange(0, HEAD, 2, dtype=np.float32) / np.float32(HEAD))).astype(np.float32)
    angles = freqs[:, None] * np.arange(1024, dtype=np.float32)[None, :]
    return np.stack([np.cos(angles), np.sin(angles)]).astype(np.float32)


def fused_body(
    tokens, cotangent, qkv_weight, out_weight, up_weight, down_weight, qkv_bias, out_bias, up_bias, down_bias,
    first_gain, first_shift, second_gain, second_shift,
):
    scratch = [
        ((8, 128), F32),
        ((2, 8, 128, D), BF16), ((4, 2, 128, D), BF16), ((4, 2, 128, D), BF16),
        ((16, 32, 256), BF16), ((16, 2, 32, 256), BF16), ((8, 32, FF_UNITS), BF16), ((4, 8, 32, FF_UNITS), BF16),
        ((8, 2, 2, 32, D), BF16), ((4, 128, D), BF16),
        ((16, 2, 8, 128), F32), ((8, D), F32), ((8, FF_UNITS), F32), ((24, 128), F32), ((3, 128, 128), F32),
        ((256, D), BF16),
        ((2, 64, D), BF16), ((2, 64, D), BF16), ((2, 64, D), BF16), ((2, D, 64), BF16), ((2, D, 64), BF16),
        ((2, D, D), BF16), ((2, 64, D), F32),
        ((16, 64, 128), BF16), ((16, 64, 128), BF16), ((16, 64, 128), BF16),
        ((128, D), F32), ((128, D), F32), ((128, 128), F32), ((128, D), F32), ((128, D), F32),
        ((4, 2, 128, FF_UNITS), F32), ((4, 2, 128, FF_UNITS), BF16), ((4, 2, 128, FF_UNITS), BF16),
        ((2, 4, 128, D), F32),
        ((2, 8, BLK, D), BF16), ((2, 8, BLK, D), BF16), ((2, 8, 80, D), BF16), ((2, 8, 80, D), BF16),
        ((FF_UNITS, 1024), BF16),
        ((16, 2, 32, UNITS), F32), ((8, 32, FF_UNITS), BF16),
        ((4, 8, 32, FF_UNITS), BF16), ((4, 128, D), BF16), ((4, 8, 32, FF_UNITS), BF16), ((4, 128, D), BF16),
        ((8, BLK, D), F32), ((8, 32, D), BF16), ((8, 32, D), BF16), ((8, BLK, D), BF16), ((8, BLK, D), BF16),
        ((8, D), F32), ((8, D), F32), ((8, D), F32), ((16, 8, 128), F32), ((2, 64, D), BF16),
        ((2, 64, D), F32), ((2, 64, D), F32), ((2, 192, D), BF16),
        ((16, 32, UNITS), BF16), ((16, 32, UNITS), BF16), ((16, 32, UNITS), BF16), ((32, UNITS), F32),
    ]
    sems = [(14,), (2, 8 * AQS), (2, 8), (2, 8 * RQS), (2, 8), (9,), (9,), (11,), (11,), (2,), (2,)]
    sems += [(2, 5), (2, 4), (2, 4), (2, 6), (4, 6), (4, 4), (2, 4), (2, 4)]
    vmem = pl.BlockSpec(memory_space=pltpu.VMEM)
    shapes = [((2, BLK, D), BF16), ((2, BLK, D), F32), ((16, 32, UNITS), BF16), ((32, D), F32), ((8, 32, FF_UNITS), BF16), ((128, D), F32), ((8, 128), F32)]
    final = shapes[:2] + [((32, 3 * D), F32), shapes[3], ((32, 4 * D), F32), shapes[5]]
    bias = (up_bias, qkv_bias, out_bias, down_bias, first_gain, first_shift, second_gain, second_shift)
    made = pl.pallas_call(
        layer_kernel,
        out_shape=[jax.ShapeDtypeStruct(s, t) for s, t in shapes],
        in_specs=[vmem] * 15,
        out_specs=[vmem] * 7,
        scratch_shapes=[pltpu.VMEM(s, t) for s, t in scratch] + [pltpu.SemaphoreType.DMA(s) for s in sems],
        compiler_params=pltpu.CompilerParams(collective_id=0, has_side_effects=True, vmem_limit_bytes=VMEM_LIMIT),
        name="layer",
    )(
        tokens[:, 0], cotangent[:, 0], qkv_weight, out_weight, up_weight, down_weight, jnp.asarray(rope_tables()),
        *(v[None] for v in bias),
    )
    anywhere = pl.BlockSpec(memory_space=pl.ANY)
    widths = (96, 32, 128, 32, 32, 32, 32, 32)
    last = pl.pallas_call(
        finish_kernel,
        out_shape=[jax.ShapeDtypeStruct(s, t) for s, t in final] + [jax.ShapeDtypeStruct((1, w), F32) for w in widths],
        in_specs=[anywhere, anywhere, vmem, anywhere, vmem, anywhere, vmem],
        out_specs=[vmem] * 14,
        scratch_shapes=[pltpu.VMEM((24, 128), F32), pltpu.SemaphoreType.DMA((4,))],
        name="finish",
    )(*made)
    return (last[0][:, None], last[1][:, None], *last[2:6], *(v[0] for v in last[6:]))


def finish_kernel(*refs):
    (out, tg, rq, go, ru, gd, gs), done, small, (gb, sems) = refs[:7], refs[7:13], refs[13:21], refs[21:]
    pairs = ((out, done[0]), (tg, done[1]), (go, done[3]), (gd, done[5]))
    copies = [pltpu.make_async_copy(a, b, sems.at[i]) for i, (a, b) in enumerate(pairs)]
    for copy in copies:
        copy.start()
    gq, gu = done[2], done[4]
    low_half = lax.broadcasted_iota(jnp.int32, (1, 128), 1) < 64
    for j in range(8):
        a = rq[2 * j].astype(F32)
        b = rq[2 * j + 1].astype(F32)
        a0, a1, b0, b1 = a[:, 0:128], a[:, 128:256], b[:, 0:128], b[:, 128:256]
        v = pltpu.roll(b1, 64, 1)
        gq[:, 128 * j : 128 * (j + 1)] = jnp.where(low_half, a0, pltpu.roll(b0, 64, 1))
        gq[:, D + 128 * j : D + 128 * (j + 1)] = jnp.where(low_half, pltpu.roll(a0, 64, 1), b0)
        gq[:, 2 * D + 128 * j : 2 * D + 128 * (j + 1)] = jnp.where(low_half, a1, v)
        bias = jnp.where(low_half, pltpu.roll(a1, 64, 1), b1)
        for i in range(3):
            gb[8 * i + j : 8 * i + j + 1, :] = bias[i : i + 1, :]
    for w in range(8):
        for i in range(4):
            gu[:, 128 * (8 * i + w) : 128 * (8 * i + w + 1)] = ru[w, :, 128 * i : 128 * (i + 1)].astype(F32)
    index = lax.axis_index("ctx") * 2 + lax.axis_index("fsdp")
    place = lax.rem(index, 4)
    turned = pltpu.roll(gs[...], lax.rem(128 - 32 * place, 128), 1)
    for ref, row in zip(small[1:], (0, 6, 1, 2, 3, 4, 5)):
        ref[...] = gs[6:7, :] if row == 6 else turned[row : row + 1, 0:32]
    offset = lax.rem(96 * index, 128)
    row = lax.div(96 * index, 128)
    lane = lax.broadcasted_iota(jnp.int32, (1, 128), 1)
    back = lax.rem(128 - offset, 128)
    one = pltpu.roll(gb[pl.ds(row, 1), :], back, 1)
    two = pltpu.roll(gb[pl.ds(lax.rem(row + 1, 24), 1), :], back, 1)
    small[0][...] = jnp.where(lane < 128 - offset, one, two)[:, 0:96]
    for copy in copies:
        copy.wait()


VMEM_LIMIT = 63 * 1024 * 1024


def layernorm(resid, gain, shift):
    center = resid - jnp.mean(resid, axis=-1, keepdims=True)
    spread = jnp.mean(center * center, axis=-1, keepdims=True)
    return center * lax.rsqrt(spread + 1e-05) * gain + shift


def tables(position):
    freqs = 10000.0 ** (-jnp.arange(0, HEAD, 2, dtype=jnp.float32) / HEAD)
    angles = position[:, None] * freqs[None, :]
    return (jnp.cos(angles)[:, None, :], jnp.sin(angles)[:, None, :])


def rotate(heads_in, cosine, sine):
    middle = heads_in.shape[-1] // 2
    first = heads_in[..., :middle]
    second = heads_in[..., middle:]
    return jnp.concatenate(
        [first * cosine - second * sine, second * cosine + first * sine], axis=-1
    )


def unrotate(heads_in, cosine, sine):
    middle = heads_in.shape[-1] // 2
    first = heads_in[..., :middle]
    second = heads_in[..., middle:]
    return jnp.concatenate(
        [first * cosine + second * sine, second * cosine - first * sine], axis=-1
    )


def split_heads(flat_rows):
    return flat_rows.reshape(flat_rows.shape[0], HEADS, HEAD)


def over_blocks(update, carried, count, limit):
    size = math.gcd(count, limit)

    def advance(block_idx, state):
        return update(state, block_idx * size, size)

    return lax.fori_loop(0, count // size, advance, carried)


def column_sum(matrix):
    return jnp.sum(matrix.astype(jnp.float32), axis=0)


def forward_local(sequence, weights_now, cosine, sine, group):
    (
        qkv_full,
        out_full,
        up_full,
        down_full,
        qkv_vector,
        out_vector,
        up_vector,
        down_vector,
        gain_first,
        shift_first,
        gain_second,
        shift_second,
    ) = weights_now
    rows = sequence.shape[0]
    width = sequence.shape[1]
    joined = jnp.dot(sequence, qkv_full, preferred_element_type=jnp.float32) + qkv_vector.astype(
        jnp.float32
    )
    query_flat = (
        rotate(split_heads(joined[:, :width]), cosine, sine)
        .astype(jnp.bfloat16)
        .reshape(rows, width)
    )
    keys_flat = (
        rotate(split_heads(joined[:, width : 2 * width]), cosine, sine)
        .astype(jnp.bfloat16)
        .reshape(rows, width)
    )
    values_flat = joined[:, 2 * width :].astype(jnp.bfloat16)
    query_heads = split_heads(query_flat)
    start_state = (
        jnp.full((HEADS, rows), -1e30, jnp.float32),
        jnp.zeros((HEADS, rows), jnp.float32),
        jnp.zeros((rows, HEADS, HEAD), jnp.float32),
    )
    keys_piece = lax.all_gather(keys_flat, "ctx", axis=0, tiled=True)
    values_piece = lax.all_gather(values_flat, "ctx", axis=0, tiled=True)

    def absorb_block(state, offset, size):
        running, total, accum = state
        key_block = split_heads(lax.dynamic_slice_in_dim(keys_piece, offset, size, 0))
        value_block = split_heads(lax.dynamic_slice_in_dim(values_piece, offset, size, 0))
        scores = (
            jnp.einsum("qhd,khd->hqk", query_heads, key_block, preferred_element_type=jnp.float32)
            * 0.125
        )
        highest_new = jnp.maximum(running, jnp.max(scores, axis=-1))
        factor = jnp.exp(running - highest_new)
        expo = jnp.exp(scores - highest_new[:, :, None])
        total = total * factor + jnp.sum(expo, axis=-1)
        accum = accum * factor.T[:, :, None] + jnp.einsum(
            "hqk,khd->qhd",
            expo.astype(jnp.bfloat16),
            value_block,
            preferred_element_type=jnp.float32,
        )
        return (highest_new, total, accum)

    running, total, accum = over_blocks(absorb_block, start_state, keys_piece.shape[0], group)
    attended = accum / total.T[:, :, None]
    logsum = running + jnp.log(total)
    att_low = attended.reshape(rows, width).astype(jnp.bfloat16)
    projected = jnp.dot(att_low, out_full, preferred_element_type=jnp.float32) + out_vector.astype(
        jnp.float32
    )
    resid_first = sequence.astype(jnp.float32) + projected
    hidden = layernorm(resid_first, gain_first.astype(jnp.float32), shift_first.astype(jnp.float32))
    hidden_low = hidden.astype(jnp.bfloat16)
    preact = jnp.dot(hidden_low, up_full, preferred_element_type=jnp.float32) + up_vector.astype(
        jnp.float32
    )
    activ_low = jax.nn.gelu(preact, approximate=False).astype(jnp.bfloat16)
    branch = jnp.dot(activ_low, down_full, preferred_element_type=jnp.float32) + down_vector.astype(
        jnp.float32
    )
    resid_second = hidden + branch
    output = layernorm(
        resid_second, gain_second.astype(jnp.float32), shift_second.astype(jnp.float32)
    )
    saved = (
        query_flat,
        keys_flat,
        values_flat,
        attended,
        logsum,
        att_low,
        resid_first,
        hidden_low,
        preact,
        activ_low,
        resid_second,
    )
    return (output.astype(jnp.bfloat16), saved)


def body(
    tokens,
    cotangent,
    qkv_weight,
    out_weight,
    up_weight,
    down_weight,
    qkv_bias,
    out_bias,
    up_bias,
    down_bias,
    first_gain,
    first_shift,
    second_gain,
    second_shift,
):
    gathered = (
        lax.all_gather(qkv_weight, ("ctx", "fsdp"), axis=0, tiled=True),
        lax.all_gather(out_weight, ("ctx", "fsdp"), axis=0, tiled=True),
        lax.all_gather(up_weight, ("ctx", "fsdp"), axis=0, tiled=True),
        lax.all_gather(down_weight, ("ctx", "fsdp"), axis=0, tiled=True),
        lax.all_gather(qkv_bias, ("ctx", "fsdp"), axis=0, tiled=True),
        lax.all_gather(out_bias, ("ctx", "fsdp"), axis=0, tiled=True),
        lax.all_gather(up_bias, ("ctx", "fsdp"), axis=0, tiled=True),
        lax.all_gather(down_bias, ("ctx", "fsdp"), axis=0, tiled=True),
        lax.all_gather(first_gain, ("ctx", "fsdp"), axis=0, tiled=True),
        lax.all_gather(first_shift, ("ctx", "fsdp"), axis=0, tiled=True),
        lax.all_gather(second_gain, ("ctx", "fsdp"), axis=0, tiled=True),
        lax.all_gather(second_shift, ("ctx", "fsdp"), axis=0, tiled=True),
    )
    rows = tokens.shape[2]
    width = tokens.shape[3]
    cycle_size = lax.axis_size("ctx")
    group = rows * math.gcd(cycle_size, 8)
    length = rows * cycle_size
    position = (lax.axis_index("ctx") * rows + jnp.arange(rows)).astype(jnp.float32)
    cosine, sine = tables(position)
    outputs = []
    savings = []
    for micro_idx in range(MICRO):
        output, saved = forward_local(tokens[micro_idx, 0], gathered, cosine, sine, group)
        outputs.append(output)
        savings.append(saved)
    weights_back = (
        lax.all_gather(qkv_weight, ("ctx", "fsdp"), axis=0, tiled=True),
        lax.all_gather(out_weight, ("ctx", "fsdp"), axis=0, tiled=True),
        lax.all_gather(up_weight, ("ctx", "fsdp"), axis=0, tiled=True),
        lax.all_gather(down_weight, ("ctx", "fsdp"), axis=0, tiled=True),
        lax.all_gather(qkv_bias, ("ctx", "fsdp"), axis=0, tiled=True),
        lax.all_gather(out_bias, ("ctx", "fsdp"), axis=0, tiled=True),
        lax.all_gather(up_bias, ("ctx", "fsdp"), axis=0, tiled=True),
        lax.all_gather(down_bias, ("ctx", "fsdp"), axis=0, tiled=True),
        lax.all_gather(first_gain, ("ctx", "fsdp"), axis=0, tiled=True),
        lax.all_gather(first_shift, ("ctx", "fsdp"), axis=0, tiled=True),
        lax.all_gather(second_gain, ("ctx", "fsdp"), axis=0, tiled=True),
        lax.all_gather(second_shift, ("ctx", "fsdp"), axis=0, tiled=True),
    )
    (
        qkv_full,
        out_full,
        up_full,
        down_full,
        qkv_vector,
        out_vector,
        up_vector,
        down_vector,
        gain_first,
        shift_first,
        gain_second,
        shift_second,
    ) = weights_back
    token_grads = []
    totals = []
    for micro_idx in range(MICRO):
        (
            query_flat,
            keys_flat,
            values_flat,
            attended,
            logsum,
            att_low,
            resid_first,
            hidden_low,
            preact,
            activ_low,
            resid_second,
        ) = savings[micro_idx]
        sequence = tokens[micro_idx, 0]
        grad_out = cotangent[micro_idx, 0].astype(jnp.float32)
        unused_two, second_back = jax.vjp(
            layernorm,
            resid_second,
            gain_second.astype(jnp.float32),
            shift_second.astype(jnp.float32),
        )
        grad_second, second_gain_grad, second_shift_grad = second_back(grad_out)
        branch_grad = grad_second.astype(jnp.bfloat16)
        down_bias_grad = column_sum(branch_grad)
        down_weight_grad = jnp.einsum(
            "tf,td->fd", activ_low, branch_grad, preferred_element_type=jnp.float32
        )
        activ_grad = jnp.einsum(
            "td,fd->tf", branch_grad, down_full, preferred_element_type=jnp.float32
        )
        unused_gelu, gelu_back = jax.vjp(partial(jax.nn.gelu, approximate=False), preact)
        preact_grad = gelu_back(activ_grad)[0].astype(jnp.bfloat16)
        up_bias_grad = column_sum(preact_grad)
        up_weight_grad = jnp.einsum(
            "td,tf->df", hidden_low, preact_grad, preferred_element_type=jnp.float32
        )
        hidden_grad = grad_second + jnp.einsum(
            "tf,df->td", preact_grad, up_full, preferred_element_type=jnp.float32
        )
        unused_one, first_back = jax.vjp(
            layernorm, resid_first, gain_first.astype(jnp.float32), shift_first.astype(jnp.float32)
        )
        grad_first, first_gain_grad, first_shift_grad = first_back(hidden_grad)
        proj_grad = grad_first.astype(jnp.bfloat16)
        out_bias_grad = column_sum(proj_grad)
        out_weight_grad = jnp.einsum(
            "tc,te->ce", att_low, proj_grad, preferred_element_type=jnp.float32
        )
        att_grad = jnp.einsum(
            "te,ce->tc", proj_grad, out_full, preferred_element_type=jnp.float32
        ).astype(jnp.bfloat16)
        att_heads = split_heads(att_grad)
        query_heads = split_heads(query_flat)
        delta = jnp.sum(att_heads.astype(jnp.float32) * attended, axis=-1).T
        key_all, value_all = (
            lax.all_gather(keys_flat, "ctx", axis=0, tiled=True),
            lax.all_gather(values_flat, "ctx", axis=0, tiled=True),
        )

        def query_update(state, offset, size):
            key_block = split_heads(lax.dynamic_slice_in_dim(key_all, offset, size, 0))
            value_block = split_heads(lax.dynamic_slice_in_dim(value_all, offset, size, 0))
            scores = (
                jnp.einsum(
                    "qhd,khd->hqk", query_heads, key_block, preferred_element_type=jnp.float32
                )
                * 0.125
            )
            chance = jnp.exp(scores - logsum[:, :, None])
            dprob = jnp.einsum(
                "qhd,khd->hqk", att_heads, value_block, preferred_element_type=jnp.float32
            )
            score_grad = (chance * (dprob - delta[:, :, None])).astype(jnp.bfloat16)
            return state + jnp.einsum(
                "hqk,khd->qhd", score_grad, key_block, preferred_element_type=jnp.float32
            )

        query_grad = (
            over_blocks(query_update, jnp.zeros((rows, HEADS, HEAD), jnp.float32), length, group)
            * 0.125
        )

        def fill(state, offset, size):
            key_block = split_heads(lax.dynamic_slice_in_dim(key_all, offset, size, 0))
            value_block = split_heads(lax.dynamic_slice_in_dim(value_all, offset, size, 0))
            scores = (
                jnp.einsum(
                    "qhd,khd->hqk", query_heads, key_block, preferred_element_type=jnp.float32
                )
                * 0.125
            )
            chance = jnp.exp(scores - logsum[:, :, None])
            value_part = jnp.einsum(
                "hqk,qhd->khd",
                chance.astype(jnp.bfloat16),
                att_heads,
                preferred_element_type=jnp.float32,
            )
            dprob = jnp.einsum(
                "qhd,khd->hqk", att_heads, value_block, preferred_element_type=jnp.float32
            )
            score_grad = (chance * (dprob - delta[:, :, None])).astype(jnp.bfloat16)
            key_part = (
                jnp.einsum(
                    "hqk,qhd->khd", score_grad, query_heads, preferred_element_type=jnp.float32
                )
                * 0.125
            )
            piece = jnp.concatenate(
                [key_part.reshape(size, width), value_part.reshape(size, width)], axis=1
            )
            return lax.dynamic_update_slice_in_dim(state, piece, offset, 0)

        combined = lax.psum_scatter(
            over_blocks(
                fill,
                jnp.zeros((lax.axis_size("ctx") * rows, 2 * width), jnp.float32),
                lax.axis_size("ctx") * rows,
                group,
            ),
            "ctx",
            scatter_dimension=0,
            tiled=True,
        )
        key_grad = split_heads(combined[:, :width])
        value_grad = combined[:, width:]
        joined_grad = jnp.concatenate(
            [
                unrotate(query_grad, cosine, sine).reshape(rows, width),
                unrotate(key_grad, cosine, sine).reshape(rows, width),
                value_grad,
            ],
            axis=1,
        ).astype(jnp.bfloat16)
        qkv_bias_grad = column_sum(joined_grad)
        qkv_weight_grad = jnp.einsum(
            "tc,te->ce", sequence, joined_grad, preferred_element_type=jnp.float32
        )
        token_grads.append(
            grad_first
            + jnp.einsum("te,ce->tc", joined_grad, qkv_full, preferred_element_type=jnp.float32)
        )
        fresh = [
            qkv_weight_grad,
            out_weight_grad,
            up_weight_grad,
            down_weight_grad,
            qkv_bias_grad,
            out_bias_grad,
            up_bias_grad,
            down_bias_grad,
            first_gain_grad,
            first_shift_grad,
            second_gain_grad,
            second_shift_grad,
        ]
        if micro_idx == 0:
            totals = fresh
        else:
            totals = [older + newer for older, newer in zip(totals, fresh)]
    summed = (
        lax.psum_scatter(totals[0], ("ctx", "fsdp"), scatter_dimension=0, tiled=True),
        lax.psum_scatter(totals[1], ("ctx", "fsdp"), scatter_dimension=0, tiled=True),
        lax.psum_scatter(totals[2], ("ctx", "fsdp"), scatter_dimension=0, tiled=True),
        lax.psum_scatter(totals[3], ("ctx", "fsdp"), scatter_dimension=0, tiled=True),
        lax.psum_scatter(totals[4], ("ctx", "fsdp"), scatter_dimension=0, tiled=True),
        lax.psum_scatter(totals[5], ("ctx", "fsdp"), scatter_dimension=0, tiled=True),
        lax.psum_scatter(totals[6], ("ctx", "fsdp"), scatter_dimension=0, tiled=True),
        lax.psum_scatter(totals[7], ("ctx", "fsdp"), scatter_dimension=0, tiled=True),
        lax.psum_scatter(totals[8], ("ctx", "fsdp"), scatter_dimension=0, tiled=True),
        lax.psum_scatter(totals[9], ("ctx", "fsdp"), scatter_dimension=0, tiled=True),
        lax.psum_scatter(totals[10], ("ctx", "fsdp"), scatter_dimension=0, tiled=True),
        lax.psum_scatter(totals[11], ("ctx", "fsdp"), scatter_dimension=0, tiled=True),
    )
    output_all = jnp.stack(outputs)[:, None]
    token_all = jnp.stack(token_grads)[:, None]
    return (
        output_all,
        token_all,
        summed[0],
        summed[1],
        summed[2],
        summed[3],
        summed[4],
        summed[5],
        summed[6],
        summed[7],
        summed[8],
        summed[9],
        summed[10],
        summed[11],
    )


def solution(mesh):
    in_specs = (
        P(None, "fsdp", "ctx", None),
        P(None, "fsdp", "ctx", None),
        P(("ctx", "fsdp"), None),
        P(("ctx", "fsdp"), None),
        P(("ctx", "fsdp"), None),
        P(("ctx", "fsdp"), None),
        P(("ctx", "fsdp")),
        P(("ctx", "fsdp")),
        P(("ctx", "fsdp")),
        P(("ctx", "fsdp")),
        P(("ctx", "fsdp")),
        P(("ctx", "fsdp")),
        P(("ctx", "fsdp")),
        P(("ctx", "fsdp")),
    )
    out_specs = (
        P(None, "fsdp", "ctx", None),
        P(None, "fsdp", "ctx", None),
        P(("ctx", "fsdp"), None),
        P(("ctx", "fsdp"), None),
        P(("ctx", "fsdp"), None),
        P(("ctx", "fsdp"), None),
        P(("ctx", "fsdp")),
        P(("ctx", "fsdp")),
        P(("ctx", "fsdp")),
        P(("ctx", "fsdp")),
        P(("ctx", "fsdp")),
        P(("ctx", "fsdp")),
        P(("ctx", "fsdp")),
        P(("ctx", "fsdp")),
    )
    fused = mesh.shape["ctx"] == NCTX and mesh.shape["fsdp"] == 2
    return jax.shard_map(fused_body if fused else body, mesh=mesh, in_specs=in_specs, out_specs=out_specs, check_vma=False)
```
